32 devices in a mesh: tiles: 8 (over y, x, core), heads: 4 (over z).
Axes of the slice: x: 2, y: 2, z: 4, core: 2. Of those that a mesh axis runs over, the one named last changes fastest.
Arguments:
- vit_tokens: bfloat16 [2, 1152, 1024], P(None, 'tiles'), may hold values from -6 to 6
- hires_maps: bfloat16 [2, 4608, 1536], P(None, 'tiles', 'heads'), may hold values from -6 to 6
- map_sizes: int32 [2, 2], replicated, may hold values from 24 to 48, as said below
- out_grad: bfloat16 [2, 1152, 1024], P(None, 'tiles'), may hold values from -6 to 6
- ln_gain: float32 [2, 1024], replicated, may hold values from 0.5 to 1.5
- ln_bias: float32 [2, 1024], replicated, may hold values from -2 to 2
- dw_params: float32 [10, 1024], P(None, 'heads'), may hold values from -2 to 2
- conv_w: bfloat16 [1536, 1024], P('heads', 'tiles'), may hold values from -0.15625 to 0.15625
- gate_w: bfloat16 [1024, 1024], P('tiles', 'heads'), may hold values from -0.1875 to 0.1875
- join_w: bfloat16 [1024, 1024], P('heads', 'tiles'), may hold values from -0.1875 to 0.1875
- attn_in_w: bfloat16 [3, 1024, 1024], P(None, 'tiles', 'heads'), may hold values from -0.1875 to 0.1875
- out_w: bfloat16 [1024, 1024], P('heads', 'tiles'), may hold values from -4 to 4
- up_w: bfloat16 [1024, 4096], P('tiles', 'heads'), may hold values from -0.1875 to 0.1875
- down_w: bfloat16 [4096, 1024], P('heads', 'tiles'), may hold values from -0.09375 to 0.09375
Outputs:
- block_out: bfloat16 [2, 1152, 1024], P(None, 'tiles')
- tokens_grad: float32 [2, 1152, 1024], P(None, 'tiles')
- hires_grad: float32 [2, 4608, 1536], P(None, 'tiles', 'heads')
- ln1_grad: float32 [2, 1024], replicated
- ln2_grad: float32 [2, 1024], replicated
- dw_params_grad: float32 [10, 1024], P(None, 'heads')
- conv_w_grad: float32 [1536, 1024], P('heads', 'tiles')
- gate_w_grad: float32 [1024, 1024], P('tiles', 'heads')
- join_w_grad: float32 [1024, 1024], P('heads', 'tiles')
- attn_in_w_grad: float32 [3, 1024, 1024], P(None, 'tiles', 'heads')
- out_w_grad: float32 [1024, 1024], P('heads', 'tiles')
- up_w_grad: float32 [1024, 4096], P('tiles', 'heads')
- down_w_grad: float32 [4096, 1024], P('heads', 'tiles')
The draws below stay inside these ranges and needn't reach their ends.
Inputs may be any that keep to these rules, and one draw needn't show every extreme that they name: `map_sizes`: each entry is 24, 32 or 48; in every micro-batch some image has 48.
All inputs are finite; a program needn't handle non-finite values.
Results may differ from the reference program's by a relative error of at most 0.025.
Values may be sent and summed in bfloat16 or wider, within the bound.
No kernel may reach another device: no remote copies, remote signals or barrier semaphores. Data moves between devices by JAX's collectives and lax.ppermute only.
A program may use at most 128 MiB of HBM per device.

```python
import jax
import jax.numpy as jnp
from jax import lax

D = 1024
HEADS = 16
HEAD_DIM = 64
FF = 4096
CH = 1536
GRID = 24
HR_MAX = 48
MB = 2
TILE = 12
HR_TILE = 24
HR_ROWS = 576
IMAGES = 2
TOKENS = 1152
N_TILES = 8


def draw_map_sizes(key, part):
    pick_key = jax.random.fold_in(key, 11)
    place_key = jax.random.fold_in(key, 12)
    side_table = jnp.array([HR_MAX // 2, 2 * HR_MAX // 3, HR_MAX], dtype=jnp.int32)
    picked = jax.random.randint(pick_key, (MB, IMAGES), 0, 3)
    drawn_sides = jnp.take(side_table, picked)
    largest = jax.random.randint(place_key, (MB, 1), 0, IMAGES)
    columns = jnp.arange(IMAGES, dtype=jnp.int32)[None, :]
    return jnp.where(columns == largest, HR_MAX, drawn_sides).astype(jnp.int32)


def level_of(own_key, dims, shards, least, high):
    level = 1.0
    for axis_at, parts in shards:
        steps = jax.random.uniform(jax.random.fold_in(jax.random.fold_in(own_key, 6), axis_at), (parts,), jnp.float32, least / len(shards), high / len(shards))
        level = level * jnp.repeat(jnp.exp(steps), dims[axis_at] // parts).reshape((-1,) + (1,) * (len(dims) - 1 - axis_at))
    return level


def scatter_about(rng, dims, scale, limit, pieces=(), kind=jnp.bfloat16):
    values = scale * jax.random.normal(rng, dims, jnp.float32)
    if pieces:
        values = values * level_of(rng, dims, pieces, -0.22, 0.18)
    return jnp.clip(values, -limit, limit).astype(kind)


def setup_inputs(seed: int = 0) -> dict:
    seeds = jax.random.split(jax.random.key(seed), 15)
    return {
        "vit_tokens": scatter_about(seeds[0], (MB, TOKENS, D), 1.0, 6.0, ((1, 8),)),
        "hires_maps": scatter_about(seeds[1], (MB, N_TILES * HR_ROWS, CH), 1.0, 6.0, ((1, 8), (2, 4))),
        "map_sizes": draw_map_sizes(jax.random.fold_in(seeds[14], 71), 0),
        "out_grad": scatter_about(seeds[3], (MB, TOKENS, D), 1.0, 6.0, ((1, 8),)),
        "ln_gain": jnp.clip(1.0 + 0.1 * jax.random.normal(seeds[4], (2, D), jnp.float32), 0.5, 1.5),
        "ln_bias": scatter_about(seeds[5], (2, D), 0.3, 2.0, (), jnp.float32),
        "dw_params": scatter_about(seeds[6], (10, D), 9 ** -0.5, 2.0, ((1, 4),), jnp.float32),
        "conv_w": scatter_about(seeds[7], (CH, D), CH ** -0.5, 0.15625, ((0, 4), (1, 8))),
        "gate_w": scatter_about(seeds[8], (D, D), D ** -0.5, 0.1875, ((0, 8), (1, 4))),
        "join_w": scatter_about(seeds[9], (D, D), D ** -0.5, 0.1875, ((0, 4), (1, 8))),
        "attn_in_w": scatter_about(seeds[10], (3, D, D), D ** -0.5, 0.1875, ((1, 8), (2, 4))),
        "out_w": scatter_about(seeds[11], (D, D), (max(1, D // 384)) ** -0.5, 4.0, ((0, 4), (1, 8))),
        "up_w": scatter_about(seeds[12], (D, FF), D ** -0.5, 0.1875, ((0, 8), (1, 4))),
        "down_w": scatter_about(seeds[13], (FF, D), FF ** -0.5, 0.09375, ((0, 4), (1, 8))),
    }


norm_eps = 1e-05
inv_root_two = 0.7071067811865476

@jax.custom_vjp
def low(v):
    return lax.optimization_barrier(v.astype(jnp.bfloat16)).astype(jnp.float32)

@jax.custom_vjp
def low_back(v):
    return v

def low_keep(v):
    return (low(v), None)

def low_pass(kept, grad):
    return (grad,)

def back_keep(v):
    return (v, None)

def back_low(kept, grad):
    return (low(grad),)
low.defvjp(low_keep, low_pass)
low_back.defvjp(back_keep, back_low)

def pool_matrix(map_side):
    cell_ids = jnp.arange(TILE, dtype=jnp.int32)
    pixel_ids = jnp.arange(HR_TILE, dtype=jnp.int32)
    bin_start = cell_ids * map_side // GRID
    bin_stop = ((cell_ids + 1) * map_side + GRID - 1) // GRID
    inside = (pixel_ids[None, :] >= bin_start[:, None]) & (pixel_ids[None, :] < bin_stop[:, None])
    weights = inside.astype(jnp.float32) / (bin_stop - bin_start).astype(jnp.float32)[:, None]
    return (weights[:, None, :, None] * weights[None, :, None, :]).reshape(TILE * TILE, HR_TILE * HR_TILE)

def gelu_value(inputs):
    return 0.5 * inputs * (1.0 + lax.erf(inputs * inv_root_two))

def layer_norm(values, gain, offset):
    centre = lax.optimization_barrier(jnp.mean(values, axis=-1, keepdims=True))
    centred = values - centre
    spread = lax.optimization_barrier(jnp.mean(centred * centred, axis=-1, keepdims=True))
    return centred * lax.rsqrt(spread + norm_eps) * gain + offset

def to_grid(values):
    chans = values.shape[-1]
    shaped = values.reshape(IMAGES, 2, 2, TILE, TILE, chans)
    return shaped.transpose(0, 1, 3, 2, 4, 5).reshape(IMAGES, GRID, GRID, chans)

def from_grid(values):
    chans = values.shape[-1]
    shaped = values.reshape(IMAGES, 2, TILE, 2, TILE, chans)
    return shaped.transpose(0, 1, 3, 2, 4, 5).reshape(TOKENS, chans)

def one_image(inputs):
    queries, keys, values = inputs
    highest = lax.Precision.HIGHEST
    scores = jnp.einsum('qhd,khd->hqk', queries, keys, precision=highest) * HEAD_DIM ** (-0.5)
    scores = low_back(scores)
    probs = jax.nn.softmax(scores, axis=-1)
    return jnp.einsum('hqk,khd->qhd', low(probs), values, precision=highest)

def attention(qkv):
    shaped = qkv.reshape(3, IMAGES, GRID * GRID, HEADS, HEAD_DIM)
    mixed = lax.map(jax.checkpoint(one_image), (shaped[0], shaped[1], shaped[2]))
    return mixed.reshape(TOKENS, D)

def forward(tokens, pixels, ln_gain, ln_bias, dw_params, conv_w, gate_w, join_w, attn_in_w, out_w, up_w, down_w, pools):
    highest = lax.Precision.HIGHEST
    tiled = pixels.reshape(N_TILES, HR_TILE * HR_TILE, CH)
    pooled = jnp.einsum('tpr,trc->tpc', pools, tiled, precision=highest).reshape(TOKENS, CH)
    pooled = low_back(low(pooled))
    mapped = low_back(low(jnp.dot(pooled, conv_w, precision=highest)))
    padded = jnp.pad(to_grid(mapped), ((0, 0), (1, 1), (1, 1), (0, 0)))
    spread = dw_params[9]
    for tap_row in range(3):
        for tap_col in range(3):
            spread = spread + dw_params[3 * tap_row + tap_col] * padded[:, tap_row:tap_row + GRID, tap_col:tap_col + GRID]
    spread = from_grid(spread)
    gate = jnp.tanh(low_back(jnp.dot(tokens, gate_w, precision=highest)))
    joined = low(gate * spread)
    first = tokens + low_back(jnp.dot(joined, join_w, precision=highest))
    normed1 = low(layer_norm(first, ln_gain[0], ln_bias[0]))
    qkv = low_back(low(jnp.einsum('td,sdc->stc', normed1, attn_in_w, precision=highest)))
    mixed = low_back(low(attention(qkv)))
    second = first + low_back(jnp.dot(mixed, out_w, precision=highest))
    normed2 = low(layer_norm(second, ln_gain[1], ln_bias[1]))
    hidden_in = low_back(jnp.dot(normed2, up_w, precision=highest))
    hidden = low(gelu_value(hidden_in))
    return second + low_back(jnp.dot(hidden, down_w, precision=highest))

def reference(vit_tokens, hires_maps, map_sizes, out_grad, ln_gain, ln_bias, dw_params, conv_w, gate_w, join_w, attn_in_w, out_w, up_w, down_w):
    params = tuple((weight.astype(jnp.float32) for weight in (ln_gain, ln_bias, dw_params, conv_w, gate_w, join_w, attn_in_w, out_w, up_w, down_w)))

    def one_batch(totals, batch):
        tokens, pixels, sizes_row, upstream = batch
        tile_sides = jnp.repeat(sizes_row, 4)
        pools = jax.vmap(pool_matrix)(tile_sides)

        def run(tokens_in, pixels_in, *weights):
            return forward(tokens_in, pixels_in, *weights, pools)
        result, pull = jax.vjp(run, tokens.astype(jnp.float32), pixels.astype(jnp.float32), *params)
        grads = pull(upstream.astype(jnp.float32))
        totals = tuple((acc + extra for acc, extra in zip(totals, grads[2:])))
        return (totals, (result.astype(jnp.bfloat16), grads[0], grads[1]))
    zeros = tuple((jnp.zeros(weight.shape, jnp.float32) for weight in params))
    totals, stacked = lax.scan(one_batch, zeros, (vit_tokens, hires_maps, map_sizes, out_grad))
    block_out, tokens_grad, hires_grad = stacked
    ln1_grad = jnp.stack([totals[0][0], totals[1][0]])
    ln2_grad = jnp.stack([totals[0][1], totals[1][1]])
    return (block_out, tokens_grad, hires_grad, ln1_grad, ln2_grad, totals[2], totals[3], totals[4], totals[5], totals[6], totals[7], totals[8], totals[9])
```

```python
import jax
import jax.numpy as jnp
from jax import lax
from jax.sharding import PartitionSpec as P

HEAD_DIM = 64
GRID = 24
TILE = 12
HR_TILE = 24

norm_eps = 1e-05
inv_root_two = 0.7071067811865476
inv_root_two_pi = 0.3989422804014327

low = jnp.bfloat16
wide = jnp.float32


def swap_with(value, axis, mask):
    pairs = [(source, source ^ mask) for source in range(lax.axis_size(axis))]
    return lax.ppermute(value, axis, pairs)


def over_core(value):
    return swap_with(value, "tiles", 1)


def over_x(value):
    return swap_with(value, "tiles", 2)


def over_y(value):
    return swap_with(value, "tiles", 4)


def dot(left, right, contract=(1, 0)):
    return lax.dot_general(
        left, right, (((contract[0],), (contract[1],)), ((), ())), preferred_element_type=wide
    )


def blocks_of(value, axis, count):
    size = value.shape[axis] // count
    return [lax.slice_in_dim(value, i * size, (i + 1) * size, axis=axis) for i in range(count)]


def reorder(value, axis, order):
    pieces = blocks_of(value, axis, len(order))
    return jnp.concatenate([pieces[i] for i in order], axis=axis)


def xor_blocks(value, axis, count, amount):
    bit = 1
    while bit < count:
        swapped = reorder(value, axis, [i ^ bit for i in range(count)])
        value = jnp.where((amount & bit) != 0, swapped, value)
        bit *= 2
    return value


def place_mask(place, count):
    half = count // 2
    return ((place % half) * 2) | (place // half)


def mask_place(mask, count):
    return (mask // 2) | ((mask % 2) * (count // 2))


def to_relative(value, axis):
    count = lax.axis_size("tiles")
    value = reorder(value, axis, [place_mask(p, count) for p in range(count)])
    return xor_blocks(value, axis, count, mask_place(lax.axis_index("tiles"), count))


def from_relative(value, axis):
    count = lax.axis_size("tiles")
    value = xor_blocks(value, axis, count, mask_place(lax.axis_index("tiles"), count))
    return reorder(value, axis, [mask_place(b, count) for b in range(count)])


def gather_tiles(block):
    count = lax.axis_size("tiles")
    if count != 8:
        every = lax.all_gather(block, "tiles")
        order = lax.axis_index("tiles") ^ jnp.array(
            [place_mask(p, count) for p in range(count)], jnp.int32
        )
        return jnp.take(every, order, axis=0).reshape(-1, block.shape[1])
    half = block.shape[0] // 2
    from_x = over_x(block)
    from_y = over_y(block)
    corner_a = over_y(from_x[:half])
    corner_b = over_x(from_y[half:])
    mine = jnp.concatenate([block, from_x, from_y, corner_a, corner_b], axis=0)
    return jnp.concatenate([mine, over_core(mine)], axis=0)


def scatter_tiles(parts):
    count = lax.axis_size("tiles")
    if count != 8:
        joint = jnp.concatenate([part.astype(low) for part in parts], axis=1)
        stacked = joint.reshape(count, -1, joint.shape[1])
        order = jnp.array([mask_place(b, count) for b in range(count)], jnp.int32)
        shift = mask_place(lax.axis_index("tiles"), count)
        whole = jnp.take(stacked, order ^ shift, axis=0)
        return lax.psum_scatter(whole, "tiles", scatter_dimension=0, tiled=False).astype(wide)
    sums = []
    for part in parts:
        half = part.shape[0] // 2
        part = part.astype(low)
        got = over_core(part[half:])
        sums.append((part[:half].astype(wide) + got.astype(wide)).astype(low))
    joint = jnp.concatenate(sums, axis=1)
    rows = joint.shape[0] // 4
    half = rows // 2
    own, to_x, to_y = joint[:rows], joint[rows : 2 * rows], joint[2 * rows : 3 * rows]
    got_a = over_x(joint[3 * rows : 3 * rows + half])
    got_b = over_y(joint[3 * rows + half :])
    to_y = jnp.concatenate([(to_y[:half].astype(wide) + got_a).astype(low), to_y[half:]], axis=0)
    to_x = jnp.concatenate([to_x[:half], (to_x[half:].astype(wide) + got_b).astype(low)], axis=0)
    got_x = over_x(to_x)
    got_y = over_y(to_y)
    return own.astype(wide) + got_x.astype(wide) + got_y.astype(wide)


def scatter_heads(part, axis=0):
    count = lax.axis_size("heads")
    pieces = blocks_of(part.astype(low), axis, count)
    total = pieces[0].astype(wide)
    for step in range(1, count):
        total = total + swap_with(pieces[step], "heads", step).astype(wide)
    return total


def gather_heads(own, axis=0):
    count = lax.axis_size("heads")
    return jnp.concatenate(
        [own] + [swap_with(own, "heads", step) for step in range(1, count)], axis=axis
    )


def pool_matrix(map_side):
    cell_ids = jnp.arange(TILE, dtype=jnp.int32)
    pixel_ids = jnp.arange(HR_TILE, dtype=jnp.int32)
    bin_start = cell_ids * map_side // GRID
    bin_stop = ((cell_ids + 1) * map_side + GRID - 1) // GRID
    inside = (pixel_ids[None, :] >= bin_start[:, None]) & (pixel_ids[None, :] < bin_stop[:, None])
    weights = inside.astype(wide) / (bin_stop - bin_start).astype(wide)[:, None]
    return (weights[:, None, :, None] * weights[None, :, None, :]).reshape(
        TILE * TILE, HR_TILE * HR_TILE
    )


def gelu_value(inputs):
    return 0.5 * inputs * (1.0 + lax.erf(inputs * inv_root_two))


def gelu_slope(inputs):
    return 0.5 * (1.0 + lax.erf(inputs * inv_root_two)) + inputs * inv_root_two_pi * jnp.exp(
        -0.5 * inputs * inputs
    )


def norm_forward(values, gain, offset):
    centre = jnp.mean(values, axis=-1, keepdims=True)
    centred = values - centre
    inv_std = lax.rsqrt(jnp.mean(centred * centred, axis=-1, keepdims=True) + norm_eps)
    scaled = centred * inv_std
    return (scaled * gain + offset, scaled, inv_std)


def norm_backward(upstream, scaled, inv_std, gain):
    weighted = upstream * gain
    inner = (
        weighted
        - jnp.mean(weighted, axis=-1, keepdims=True)
        - scaled * jnp.mean(weighted * scaled, axis=-1, keepdims=True)
    )
    sums = jnp.stack([jnp.sum(upstream * scaled, axis=0), jnp.sum(upstream, axis=0)])
    return (inv_std * inner, sums)


def halo(grid_values, right_edge, lower_edge):
    send_col = jnp.where(right_edge, grid_values[:, :, -1], grid_values[:, :, 0]).astype(low)
    got_col = over_core(send_col).astype(wide)
    zero_col = jnp.zeros_like(got_col)
    left_col = jnp.where(right_edge, zero_col, got_col)
    right_col = jnp.where(right_edge, got_col, zero_col)
    widened = jnp.concatenate(
        [left_col[:, :, None], grid_values, right_col[:, :, None]], axis=2
    )
    send_row = jnp.where(lower_edge, widened[:, -1], widened[:, 0]).astype(low)
    got_row = over_x(send_row).astype(wide)
    zero_row = jnp.zeros_like(got_row)
    top_row = jnp.where(lower_edge, zero_row, got_row)
    bottom_row = jnp.where(lower_edge, got_row, zero_row)
    return jnp.concatenate([top_row[:, None], widened, bottom_row[:, None]], axis=1)


def attend(queries, keys, values):
    scores = jnp.einsum(
        "bqhd,bkhd->bhqk", queries, keys, preferred_element_type=wide
    ) * HEAD_DIM ** (-0.5)
    peak = jnp.max(scores, axis=-1, keepdims=True)
    expo = jnp.exp(scores - peak)
    totals = jnp.sum(expo, axis=-1, keepdims=True)
    probs_low = (expo / totals).astype(low)
    mixed = jnp.einsum("bhqk,bkhd->bqhd", probs_low, values, preferred_element_type=wide)
    return (mixed.astype(low), peak + jnp.log(totals))


def attend_back(queries, keys, values, log_sums, d_mixed):
    scale = HEAD_DIM ** (-0.5)
    scores = jnp.einsum("bqhd,bkhd->bhqk", queries, keys, preferred_element_type=wide) * scale
    probs = jnp.exp(scores - log_sums)
    probs_low = probs.astype(low)
    d_probs = jnp.einsum("bqhd,bkhd->bhqk", d_mixed, values, preferred_element_type=wide)
    d_scores = (probs * (d_probs - jnp.sum(probs * d_probs, axis=-1, keepdims=True))).astype(low)
    d_query = jnp.einsum("bhqk,bkhd->bqhd", d_scores, keys, preferred_element_type=wide) * scale
    d_keys = jnp.einsum("bhqk,bqhd->bkhd", d_scores, queries, preferred_element_type=wide) * scale
    d_values = jnp.einsum("bhqk,bqhd->bkhd", probs_low, d_mixed, preferred_element_type=wide)
    return d_query, d_keys, d_values


def local(
    vit_tokens,
    hires_maps,
    map_sizes,
    out_grad,
    ln_gain,
    ln_bias,
    dw_params,
    conv_w,
    gate_w,
    join_w,
    attn_in_w,
    out_w,
    up_w,
    down_w,
):
    tile = lax.axis_index("tiles")
    head = lax.axis_index("heads")
    tiles = lax.axis_size("tiles")
    heads = lax.axis_size("heads")
    image_slot = tile // 4
    right_edge = tile % 2 == 0
    lower_edge = tile // 2 % 2 == 0
    batches, rows, width = vit_tokens.shape
    total_rows = batches * rows
    shard = total_rows // heads
    chans = dw_params.shape[1]
    inner = tiles // heads
    inner_place = tile % inner
    outer_place = tile // inner

    conv_t = gather_tiles(conv_w.T)
    gate_join = gather_tiles(jnp.concatenate([gate_w, join_w.T], axis=1))
    gate_full, join_t = gate_join[:, :chans], gate_join[:, chans:]
    attn_proj = gather_tiles(
        jnp.concatenate([attn_in_w[0], attn_in_w[1], attn_in_w[2], out_w.T], axis=1)
    )
    attn_full, proj_t = attn_proj[:, : 3 * chans], attn_proj[:, 3 * chans :]
    up_down = gather_tiles(jnp.concatenate([up_w, down_w.T], axis=1))
    hidden_width = up_w.shape[1]
    up_full, down_t = up_down[:, :hidden_width], up_down[:, hidden_width:]

    def rows_relative(value):
        return xor_blocks(value, 0, heads, head)

    tokens = rows_relative(to_relative(vit_tokens.reshape(total_rows, width), 1))
    upstream = rows_relative(to_relative(out_grad.reshape(total_rows, width), 1))
    tokens_own = tokens[:shard].astype(wide)
    upstream_own = upstream[:shard].astype(wide)
    gains = to_relative(ln_gain, 1)
    biases = to_relative(ln_bias, 1)

    pools = []
    pooled = []
    for batch in range(batches):
        map_side = lax.dynamic_index_in_dim(map_sizes[batch], image_slot, keepdims=False)
        pools.append(pool_matrix(map_side).astype(low))
        pooled.append(dot(pools[batch], hires_maps[batch]).astype(low))
    pooled = jnp.concatenate(pooled, axis=0)
    half = tiles // 2
    by_chunk = [
        place_mask_order
        for chunk in range(heads)
        for place_mask_order in [
            mask_place(chunk * inner + part, tiles) for part in range(inner)
        ]
    ]
    back_order = [by_chunk.index(p) for p in range(tiles)]
    conv_part = reorder(dot(pooled, conv_t, (1, 1)).astype(low), 1, by_chunk)
    conv_part = xor_blocks(conv_part, 1, heads, head ^ outer_place)
    mapped = xor_blocks(scatter_heads(conv_part, 1).astype(low), 1, inner, inner_place)

    padded = halo(
        mapped.astype(wide).reshape(batches, TILE, TILE, chans), right_edge, lower_edge
    )
    spread = dw_params[9]
    for tap in range(9):
        row, col = divmod(tap, 3)
        spread = spread + dw_params[tap] * padded[:, row : row + TILE, col : col + TILE]
    spread = rows_relative(spread.reshape(total_rows, chans))
    gate = jnp.tanh(dot(tokens, gate_full))
    joined = (gate * spread).astype(low)
    first = tokens_own + scatter_heads(dot(joined, join_t, (1, 1)))

    normed1_own, scaled1, inv_std1 = norm_forward(first, gains[0], biases[0])
    normed1 = gather_heads(normed1_own.astype(low))
    qkv = dot(normed1, attn_full).astype(low)
    kv_own = qkv[:, chans:]
    kv_x = over_x(kv_own)
    kv_all = [kv_own, kv_x, over_core(kv_own), over_core(kv_x)]
    heads_here = chans // HEAD_DIM
    whole = jnp.concatenate([part.reshape(batches, rows, 2 * chans) for part in kv_all], axis=1)
    keys = whole[:, :, :chans].reshape(batches, 4 * rows, heads_here, HEAD_DIM)
    values = whole[:, :, chans:].reshape(batches, 4 * rows, heads_here, HEAD_DIM)
    queries = qkv[:, :chans].reshape(batches, rows, heads_here, HEAD_DIM)
    mixed, log_sums = attend(queries, keys, values)
    mixed = mixed.reshape(total_rows, chans)
    second = first + scatter_heads(dot(mixed, proj_t, (1, 1)))

    normed2_own, scaled2, inv_std2 = norm_forward(second, gains[1], biases[1])
    normed2 = gather_heads(normed2_own.astype(low))
    hidden_in = dot(normed2, up_full)
    hidden = gelu_value(hidden_in).astype(low)
    d_hidden = dot(upstream, down_t)
    d_hidden_in = (d_hidden * gelu_slope(hidden_in)).astype(low)
    d_normed2 = scatter_heads(dot(d_hidden_in, up_full, (1, 1)))
    d_norm2, ln2_sums = norm_backward(d_normed2, scaled2, inv_std2, gains[1])
    d_second = upstream_own + d_norm2
    d_attn = gather_heads(d_second.astype(low))

    result = second + scatter_heads(dot(hidden, down_t, (1, 1)))
    block_out = rows_relative(gather_heads(from_relative(result.astype(low), 1)))
    up_down_sum = scatter_tiles(
        [dot(normed2, d_hidden_in, (0, 0)), dot(upstream, hidden, (0, 0))]
    )

    d_mixed = dot(d_attn, proj_t).astype(low).reshape(batches, rows, heads_here, HEAD_DIM)
    d_query, d_keys, d_values = attend_back(queries, keys, values, log_sums, d_mixed)
    d_whole = jnp.concatenate(
        [
            d_keys.reshape(batches, 4 * rows, chans),
            d_values.reshape(batches, 4 * rows, chans),
        ],
        axis=2,
    )
    d_pair = d_whole[:, : 2 * rows] + over_core(d_whole[:, 2 * rows :].astype(low))
    d_own = d_pair[:, :rows] + over_x(d_pair[:, rows:].astype(low))
    d_qkv = jnp.concatenate(
        [
            d_query.reshape(total_rows, chans).astype(low),
            d_own.reshape(total_rows, 2 * chans).astype(low),
        ],
        axis=1,
    )
    d_normed1 = scatter_heads(dot(d_qkv, attn_full, (1, 1)))
    d_norm1, ln1_sums = norm_backward(d_normed1, scaled1, inv_std1, gains[0])
    d_first = d_second + d_norm1
    d_join_low = gather_heads(d_first.astype(low))
    attn_proj_sum = scatter_tiles([dot(normed1, d_qkv, (0, 0)), dot(d_attn, mixed, (0, 0))])

    d_joined = dot(d_join_low, join_t)
    d_spread = d_joined * gate
    d_gate_in = (d_joined * spread * (1.0 - gate * gate)).astype(low)
    d_grid = rows_relative(d_spread).reshape(batches, TILE, TILE, chans)
    d_padded = halo(d_grid, right_edge, lower_edge)
    d_mapped = jnp.zeros(d_grid.shape, wide)
    tap_sums = []
    for tap in range(9):
        row, col = divmod(tap, 3)
        d_mapped = (
            d_mapped
            + dw_params[tap] * d_padded[:, 2 - row : 2 - row + TILE, 2 - col : 2 - col + TILE]
        )
        tap_sums.append(
            jnp.sum(d_grid * padded[:, row : row + TILE, col : col + TILE], axis=(0, 1, 2))
        )
    tap_sums.append(jnp.sum(d_grid, axis=(0, 1, 2)))
    d_mapped = d_mapped.reshape(total_rows, chans).astype(low)
    d_mapped_all = gather_heads(xor_blocks(d_mapped, 1, inner, inner_place), 1)
    d_mapped_all = reorder(
        xor_blocks(d_mapped_all, 1, heads, head ^ outer_place), 1, back_order
    )
    d_pooled = dot(d_mapped_all, conv_t).astype(low)
    hires_grad = jnp.stack(
        [
            dot(pools[batch], d_pooled[batch * rows : (batch + 1) * rows], (0, 0))
            for batch in range(batches)
        ]
    )
    conv_sum = scatter_tiles([dot(d_mapped_all, pooled, (0, 0))])
    gate_join_sum = scatter_tiles([dot(tokens, d_gate_in, (0, 0)), dot(d_join_low, joined, (0, 0))])
    d_tokens = d_first + scatter_heads(dot(d_gate_in, gate_full, (1, 1)))
    tokens_grad = rows_relative(gather_heads(from_relative(d_tokens.astype(low), 1)))

    ln_sums = from_relative(jnp.concatenate([ln1_sums, ln2_sums], axis=0), 1)
    taps_sum = jnp.stack(tap_sums)
    bit = 1
    while bit < tiles:
        ln_sums = ln_sums + swap_with(ln_sums, "tiles", bit)
        taps_sum = taps_sum + swap_with(taps_sum, "tiles", bit)
        bit *= 2
    bit = 1
    while bit < heads:
        ln_sums = ln_sums + swap_with(ln_sums, "heads", bit)
        bit *= 2

    return (
        block_out.reshape(batches, rows, width),
        tokens_grad.astype(wide).reshape(batches, rows, width),
        hires_grad,
        ln_sums[:2],
        ln_sums[2:],
        taps_sum,
        conv_sum.T,
        gate_join_sum[:, :chans],
        gate_join_sum[:, chans:].T,
        jnp.stack([attn_proj_sum[:, s * chans : (s + 1) * chans] for s in range(3)]),
        attn_proj_sum[:, 3 * chans :].T,
        up_down_sum[:, :hidden_width],
        up_down_sum[:, hidden_width:].T,
    )


def solution(mesh):
    placed = (
        P(None, "tiles", None),
        P(None, "tiles", "heads"),
        P(),
        P(None, "tiles", None),
        P(),
        P(),
        P(None, "heads"),
        P("heads", "tiles"),
        P("tiles", "heads"),
        P("heads", "tiles"),
        P(None, "tiles", "heads"),
        P("heads", "tiles"),
        P("tiles", "heads"),
        P("heads", "tiles"),
    )
    return jax.shard_map(
        local,
        mesh=mesh,
        in_specs=placed,
        out_specs=(
            P(None, "tiles", None),
            P(None, "tiles", None),
            P(None, "tiles", "heads"),
            P(),
            P(),
            P(None, "heads"),
            P("heads", "tiles"),
            P("tiles", "heads"),
            P("heads", "tiles"),
            P(None, "tiles", "heads"),
            P("heads", "tiles"),
            P("tiles", "heads"),
            P("heads", "tiles"),
        ),
        check_vma=False,
    )
```

```python
import jax
import jax.numpy as jnp
from jax import lax
from jax.experimental import pallas as pl
from jax.experimental.pallas import tpu as pltpu
from jax.sharding import PartitionSpec as P

HEAD_DIM = 64
GRID = 24
TILE = 12
HR_TILE = 24
PAD = 16
LANES = 128

norm_eps = 1e-05
inv_root_two = 0.7071067811865476
inv_root_two_pi = 0.3989422804014327

low = jnp.bfloat16
wide = jnp.float32
VMEM_LIMIT = 24 * 1024 * 1024


def shape(dims, kind=low):
    return jax.ShapeDtypeStruct(tuple(dims), kind)


def run_kernel(body, outs, *args, scratch=(), flops=0):
    whole = pl.BlockSpec(memory_space=pltpu.VMEM)
    traffic = sum(a.size * a.dtype.itemsize for a in args)
    traffic += sum(o.size * o.dtype.itemsize for o in outs)
    return pl.pallas_call(
        body,
        out_shape=tuple(outs),
        in_specs=[whole] * len(args),
        out_specs=tuple([whole] * len(outs)),
        scratch_shapes=[pltpu.VMEM(dims, kind) for dims, kind in scratch],
        cost_estimate=pl.CostEstimate(flops=flops, bytes_accessed=traffic, transcendentals=0),
        compiler_params=pltpu.CompilerParams(vmem_limit_bytes=VMEM_LIMIT),
    )(*args)


def dot(left, right, contract=(1, 0)):
    return lax.dot_general(
        left, right, (((contract[0],), (contract[1],)), ((), ())), preferred_element_type=wide
    )


def cat(parts, axis):
    return parts[0] if len(parts) == 1 else jnp.concatenate(parts, axis=axis)


def stack_rows(refs, lanes=slice(None)):
    return cat([ref[:, lanes].astype(wide) for ref in refs], 0).astype(low)


def swap_with(value, axis, mask):
    pairs = [(source, source ^ mask) for source in range(lax.axis_size(axis))]
    return lax.ppermute(value, axis, pairs)


def over_core(value):
    return swap_with(value, "tiles", 1)


def over_x(value):
    return swap_with(value, "tiles", 2)


def over_y(value):
    return swap_with(value, "tiles", 4)


def fast_tiles():
    return lax.axis_size("tiles") == 8


BLOCKS = 8


def place_mask(place):
    half = BLOCKS // 2
    return ((place % half) * 2) | (place // half)


def block_at(place):
    if fast_tiles():
        return lax.axis_index("tiles") ^ place_mask(place)
    return place


def gather_blocks(block):
    found = [block, over_x(block), over_y(block), swap_with(block, "tiles", 6)]
    return found + [over_core(part) for part in found]


def pieces_of(packed, full):
    if fast_tiles():
        return gather_blocks(packed)
    return full


def scatter_heads(parts):
    return [parts[0]] + [swap_with(parts[j], "heads", j) for j in range(1, len(parts))]


def gather_heads(own):
    return [own] + [swap_with(own, "heads", j) for j in range(1, lax.axis_size("heads"))]


def add_rows_body(keep_ref, got_ref, *out_refs):
    for i, out_ref in enumerate(out_refs):
        total = keep_ref[i].astype(wide) + got_ref[i].astype(wide)
        out_ref[...] = total.astype(out_ref.dtype)


def scatter_blocks(keep, send):
    rows = keep.shape[1]
    if not fast_tiles():
        whole = jnp.concatenate([keep, send], axis=0)
        return whole
    got = over_core(send)
    sums = run_kernel(add_rows_body, [shape((rows, LANES))] * 4, keep, got)
    return [sums[0], over_x(sums[1]), over_y(sums[2]), swap_with(sums[3], "tiles", 6)]


def gelu_parts(inputs):
    bell = 0.5 * (1.0 + lax.erf(inputs * inv_root_two))
    return inputs * bell, bell + inputs * inv_root_two_pi * jnp.exp(-0.5 * inputs * inputs)


def normed(values):
    centred = values - jnp.mean(values, axis=-1, keepdims=True)
    inv_std = lax.rsqrt(jnp.mean(centred * centred, axis=-1, keepdims=True) + norm_eps)
    return centred * inv_std, inv_std


def total_of(refs, at=Ellipsis):
    total = refs[0][at].astype(wide)
    for ref in refs[1:]:
        total = total + ref[at].astype(wide)
    return total


def pool_matrices(map_sides):
    cell_ids = jnp.arange(TILE, dtype=jnp.int32)
    pixel_ids = jnp.arange(HR_TILE, dtype=jnp.int32)
    sides = map_sides[:, None]
    bin_start = cell_ids * sides // GRID
    bin_stop = ((cell_ids + 1) * sides + GRID - 1) // GRID
    inside = (pixel_ids >= bin_start[:, :, None]) & (pixel_ids < bin_stop[:, :, None])
    weights = inside.astype(wide) / (bin_stop - bin_start).astype(wide)[:, :, None]
    return (
        (weights[:, :, None, :, None] * weights[:, None, :, None, :])
        .reshape(-1, TILE * TILE, HR_TILE * HR_TILE)
        .astype(low)
    )


def pack_body(gate_ref, join_ref, attn_ref, out_ref, up_ref, down_ref, gj_ref, ap_ref, ud_ref):
    def spread_lanes(value, target, start):
        for m in range(value.shape[1] // LANES):
            rows = value.shape[0]
            target[start + m * rows : start + (m + 1) * rows] = value[
                :, m * LANES : (m + 1) * LANES
            ]

    gate_rows = gate_ref.shape[0] * (gate_ref.shape[1] // LANES)
    spread_lanes(gate_ref[...], gj_ref, 0)
    gj_ref[gate_rows:] = join_ref[...]
    for s in range(3):
        spread_lanes(attn_ref[s], ap_ref, s * gate_rows)
    ap_ref[3 * gate_rows :] = out_ref[...]
    up_rows = up_ref.shape[0] * (up_ref.shape[1] // LANES)
    spread_lanes(up_ref[...], ud_ref, 0)
    ud_ref[up_rows:] = down_ref[...]


def wide_rows(refs, start, count):
    return cat(
        [
            cat([ref[start + m * LANES : start + (m + 1) * LANES] for m in range(count)], 1)
            for ref in refs
        ],
        0,
    )


def wide_cols(refs, start, rows):
    return cat([ref[start : start + rows] for ref in refs], 1)


def relative_body(tok_ref, up_ref, gain_ref, bias_ref, tok_out, up_out, gain_out, bias_out, hold):
    head = lax.axis_index("heads")
    heads = lax.axis_size("heads")
    shard = tok_ref.shape[0] // heads
    for source, target in ((tok_ref, tok_out), (up_ref, up_out)):
        for place in range(BLOCKS):
            lanes = pl.ds(pl.multiple_of(LANES * block_at(place), LANES), LANES)
            hold[...] = source[:, lanes].astype(wide)
            rows = [
                hold[pl.ds(pl.multiple_of(shard * (head ^ j), 8), shard)] for j in range(heads)
            ]
            target[:, place * LANES : (place + 1) * LANES] = cat(rows, 0).astype(low)
    for source, target in ((gain_ref, gain_out), (bias_ref, bias_out)):
        for place in range(BLOCKS):
            lanes = pl.ds(pl.multiple_of(LANES * block_at(place), LANES), LANES)
            target[:, place * LANES : (place + 1) * LANES] = source[:, lanes]


def conv_body(pooled_ref, *refs):
    piece_refs, (whole_ref, *out_refs) = refs[:BLOCKS], refs[BLOCKS:]
    head = lax.axis_index("heads")
    for place, ref in enumerate(piece_refs):
        whole_ref[block_at(place)] = ref[...]
    per_chunk = BLOCKS // len(out_refs)
    for j, out_ref in enumerate(out_refs):
        first = per_chunk * (head ^ j)
        chunk = cat([whole_ref[first + i] for i in range(per_chunk)], 1)
        out_ref[...] = dot(pooled_ref[...], chunk).astype(low)


def edge_flags():
    tile = lax.axis_index("tiles")
    return (tile & 1) == 0, (tile & 2) == 0


def send_edges(grid, hold_ref, col_ref, row_ref, corner_ref):
    right, lower = edge_flags()
    cells = TILE * TILE
    batches = grid.shape[0] // cells
    count = batches * TILE
    for at in range(count):
        begin = at * TILE
        end = begin + TILE - 1
        hold_ref[at : at + 1] = jnp.where(right, grid[end : end + 1], grid[begin : begin + 1])
    col_ref[...] = hold_ref[0:count].astype(low)
    hold_ref[...] = jnp.zeros(hold_ref.shape, wide)
    for batch in range(batches):
        base = batch * cells
        bottom = grid[base + cells - TILE : base + cells]
        top = grid[base : base + TILE]
        edge = jnp.where(lower, bottom, top)
        hold_ref[batch * PAD : batch * PAD + TILE] = edge
    row_ref[...] = hold_ref[...].astype(low)
    hold_ref[...] = jnp.zeros(hold_ref.shape, wide)
    for batch in range(batches):
        base = batch * cells
        ends = [
            jnp.where(right, grid[at + TILE - 1 : at + TILE], grid[at : at + 1])
            for at in (base + cells - TILE, base)
        ]
        hold_ref[batch : batch + 1] = jnp.where(lower, ends[0], ends[1])
    corner_ref[...] = hold_ref[0:PAD].astype(low)


def fill_padded(grid, col_ref, row_ref, corner_ref, pad_ref, hold_ref):
    right, lower = edge_flags()
    cells = TILE * TILE
    batches = grid.shape[0] // cells
    per_batch = (TILE + 2) * PAD
    pad_ref[...] = jnp.zeros(pad_ref.shape, wide)
    hold_ref[0 : batches * TILE] = col_ref[...].astype(wide)
    for batch in range(batches):
        for a in range(TILE):
            at = batch * per_batch + (a + 1) * PAD
            source = batch * cells + a * TILE
            pad_ref[at + 1 : at + 1 + TILE] = grid[source : source + TILE]
            got = hold_ref[batch * TILE + a : batch * TILE + a + 1]
            zero = jnp.zeros_like(got)
            pad_ref[at : at + 1] = jnp.where(right, zero, got)
            pad_ref[at + TILE + 1 : at + TILE + 2] = jnp.where(right, got, zero)
    rows = row_ref[...].astype(wide)
    corners = corner_ref[...].astype(wide)
    for batch in range(batches):
        got = rows[batch * PAD : batch * PAD + TILE]
        corner = corners[batch : batch + 1]
        zero = jnp.zeros_like(got)
        nil = jnp.zeros_like(corner)
        for at, used in (
            (batch * per_batch, jnp.logical_not(lower)),
            (batch * per_batch + (TILE + 1) * PAD, lower),
        ):
            pad_ref[at + 1 : at + 1 + TILE] = jnp.where(used, got, zero)
            left = jnp.logical_and(used, jnp.logical_not(right))
            pad_ref[at : at + 1] = jnp.where(left, corner, nil)
            pad_ref[at + TILE + 1 : at + TILE + 2] = jnp.where(
                jnp.logical_and(used, right), corner, nil
            )


def map_body(*refs):
    heads = lax.axis_size("heads")
    part_refs, (map_ref, col_ref, row_ref, corner_ref, grid, hold) = refs[:heads], refs[heads:]
    mapped = total_of(part_refs).astype(low)
    map_ref[...] = mapped
    grid[...] = mapped.astype(wide)
    send_edges(grid, hold, col_ref, row_ref, corner_ref)


def gate_body(tok_ref, *refs):
    piece_refs, (gate_ref,) = refs[:BLOCKS], refs[BLOCKS:]
    count = gate_ref.shape[1] // LANES
    gate_ref[...] = jnp.tanh(dot(tok_ref[...], wide_rows(piece_refs, 0, count)))


def write_chunks(result, out_refs, lanes=slice(None)):
    rows = result.shape[0] // len(out_refs)
    for j, out_ref in enumerate(out_refs):
        out_ref[:, lanes] = result[j * rows : (j + 1) * rows].astype(low)


def depthwise_body(map_ref, col_ref, row_ref, corner_ref, dw_ref, gate_ref, *refs):
    piece_refs = refs[:BLOCKS]
    heads = lax.axis_size("heads")
    head = lax.axis_index("heads")
    pad_ref, spread_ref, joined_ref = refs[BLOCKS : BLOCKS + 3]
    out_refs = refs[BLOCKS + 3 : BLOCKS + 3 + heads]
    grid, hold, flat = refs[BLOCKS + 3 + heads :]
    grid[...] = map_ref[...].astype(wide)
    fill_padded(grid, col_ref, row_ref, corner_ref, pad_ref, hold)
    cells = TILE * TILE
    batches = grid.shape[0] // cells
    per_batch = (TILE + 2) * PAD
    for batch in range(batches):
        for a in range(TILE):
            running = jnp.broadcast_to(dw_ref[9:10], (TILE, grid.shape[1]))
            for tap in range(9):
                row, col = divmod(tap, 3)
                at = batch * per_batch + (a + row) * PAD + col
                running = running + dw_ref[tap : tap + 1] * pad_ref[at : at + TILE]
            to = batch * cells + a * TILE
            flat[to : to + TILE] = running
    shard = grid.shape[0] // heads
    for j in range(heads):
        spread = flat[pl.ds(pl.multiple_of(shard * (head ^ j), 8), shard)]
        spread_ref[j * shard : (j + 1) * shard] = spread
    joined = (gate_ref[...] * spread_ref[...]).astype(low)
    joined_ref[...] = joined
    gate_rows = grid.shape[1]
    write_chunks(dot(joined, wide_cols(piece_refs, gate_rows, grid.shape[1])), out_refs)


def norm_body(base_ref, gain_ref, bias_ref, *refs):
    part_refs, (sum_ref, low_ref) = refs[:-2], refs[-2:]
    rows = sum_ref.shape[0]
    total = base_ref[0:rows].astype(wide) + total_of(part_refs)
    sum_ref[...] = total
    low_ref[...] = (normed(total)[0] * gain_ref[...] + bias_ref[...]).astype(low)


def qkv_body(*refs):
    heads = lax.axis_size("heads")
    part_refs, piece_refs = refs[:heads], refs[heads : heads + BLOCKS]
    all_ref, query_ref, kv_ref = refs[heads + BLOCKS :]
    chans = query_ref.shape[1]
    rows = stack_rows(part_refs)
    all_ref[...] = rows
    count = chans // LANES
    for s in range(3):
        result = dot(rows, wide_rows(piece_refs, s * chans, count)).astype(low)
        if s == 0:
            query_ref[...] = result
        else:
            kv_ref[:, (s - 1) * chans : s * chans] = result


def head_masks(rows):
    lane = lax.broadcasted_iota(jnp.int32, (rows, LANES), 1)
    return [lane < HEAD_DIM, lane >= HEAD_DIM]


def softmax_parts(query, keys):
    scores = dot(query, keys, (1, 1)) * HEAD_DIM ** (-0.5)
    expo = jnp.exp(scores - jnp.max(scores, axis=-1, keepdims=True))
    return expo / jnp.sum(expo, axis=-1, keepdims=True)


def attend_body(query_ref, *refs):
    kv_refs, piece_refs = refs[:4], refs[4 : 4 + BLOCKS]
    mixed_ref, *out_refs = refs[4 + BLOCKS :]
    chans = query_ref.shape[1]
    cells = TILE * TILE
    masks = head_masks(cells)
    for batch in range(query_ref.shape[0] // cells):
        at = slice(batch * cells, (batch + 1) * cells)
        for pair in range(chans // LANES):
            lanes = slice(pair * LANES, (pair + 1) * LANES)
            value_lanes = slice(chans + pair * LANES, chans + (pair + 1) * LANES)
            keys = cat([ref[at, lanes] for ref in kv_refs], 0)
            values = cat([ref[at, value_lanes] for ref in kv_refs], 0)
            query = query_ref[at, lanes]
            found = []
            for mask in masks:
                probs = softmax_parts(jnp.where(mask, query, jnp.zeros_like(query)), keys)
                found.append(dot(probs.astype(low), values))
            mixed_ref[at, lanes] = jnp.where(masks[0], found[0], found[1]).astype(low)
    write_chunks(dot(mixed_ref[...], wide_cols(piece_refs, 3 * chans, chans)), out_refs)


HIDDEN_STEP = 256


def ffn_body(upstream_ref, *refs):
    heads = lax.axis_size("heads")
    part_refs, piece_refs = refs[:heads], refs[heads : heads + BLOCKS]
    all_ref, hidden_ref, d_hidden_ref = refs[heads + BLOCKS : heads + BLOCKS + 3]
    out_refs = refs[heads + BLOCKS + 3 : heads + BLOCKS + 3 + heads]
    total_ref = refs[-1]
    hidden_width = hidden_ref.shape[1]
    all_ref[...] = stack_rows(part_refs)
    total_ref[...] = jnp.zeros(total_ref.shape, wide)
    per_step = HIDDEN_STEP // LANES

    def step(m, carry):
        at = pl.multiple_of(m * HIDDEN_STEP, HIDDEN_STEP)
        up = cat(
            [
                cat([ref[pl.ds(at + i * LANES, LANES)] for i in range(per_step)], 1)
                for ref in piece_refs
            ],
            0,
        )
        down = cat([ref[pl.ds(hidden_width + at, HIDDEN_STEP)] for ref in piece_refs], 1)
        value, slope = gelu_parts(dot(all_ref[...], up))
        hidden_ref[:, pl.ds(at, HIDDEN_STEP)] = value.astype(low)
        d_hidden = (dot(upstream_ref[...], down, (1, 1)) * slope).astype(low)
        d_hidden_ref[:, pl.ds(at, HIDDEN_STEP)] = d_hidden
        total_ref[...] += dot(d_hidden, up, (1, 1))
        return carry

    lax.fori_loop(0, hidden_width // HIDDEN_STEP, step, 0)
    write_chunks(total_ref[...], out_refs)


def down_body(hidden_ref, *refs):
    piece_refs, out_refs = refs[:BLOCKS], refs[BLOCKS:]
    width = hidden_ref.shape[1]
    for pair in range(BLOCKS // 2):
        weights = wide_cols(piece_refs[2 * pair : 2 * pair + 2], width, width)
        lanes = slice(2 * pair * LANES, 2 * (pair + 1) * LANES)
        write_chunks(dot(hidden_ref[...], weights), out_refs, lanes)


def whole_cols_body(base_ref, *refs):
    part_refs, out_ref = refs[:-1], refs[-1]
    for place in range(BLOCKS):
        lanes = slice(place * LANES, (place + 1) * LANES)
        total = base_ref[:, lanes] + total_of(part_refs, (slice(None), lanes))
        to = pl.ds(pl.multiple_of(LANES * block_at(place), LANES), LANES)
        out_ref[:, to] = total.astype(low)


def whole_rows_body(*refs):
    part_refs, out_ref, hold = refs[:-2], refs[-2], refs[-1]
    head = lax.axis_index("heads")
    shard = part_refs[0].shape[0]
    for j, ref in enumerate(part_refs):
        to = pl.ds(pl.multiple_of(shard * (head ^ j), 8), shard)
        if out_ref.dtype == wide:
            out_ref[to] = ref[...].astype(wide)
        else:
            hold[to] = ref[...].astype(wide)
    if out_ref.dtype != wide:
        out_ref[...] = hold[...].astype(out_ref.dtype)


def norm_back_body(values_ref, base_ref, gain_ref, *refs):
    part_refs, (sum_ref, low_ref, sums_ref) = refs[:-3], refs[-3:]
    rows = sum_ref.shape[0]
    scaled, inv_std = normed(values_ref[...])
    upstream = total_of(part_refs)
    weighted = upstream * gain_ref[...]
    inner = (
        weighted
        - jnp.mean(weighted, axis=-1, keepdims=True)
        - scaled * jnp.mean(weighted * scaled, axis=-1, keepdims=True)
    )
    total = base_ref[0:rows].astype(wide) + inv_std * inner
    sum_ref[...] = total
    low_ref[...] = total.astype(low)
    sums = [
        jnp.sum(upstream * scaled, axis=0, keepdims=True),
        jnp.sum(upstream, axis=0, keepdims=True),
    ]
    for place in range(BLOCKS):
        lanes = slice(place * LANES, (place + 1) * LANES)
        to = pl.ds(pl.multiple_of(LANES * block_at(place), LANES), LANES)
        for i in range(2):
            sums_ref[i : i + 1, to] = sums[i][:, lanes]


def attend_back_body(query_ref, *refs):
    heads = lax.axis_size("heads")
    kv_refs, part_refs = refs[:4], refs[4 : 4 + heads]
    piece_refs = refs[4 + heads : 4 + heads + BLOCKS]
    all_ref, d_query_ref, keep_ref, send_ref, d_mixed_ref = refs[4 + heads + BLOCKS :]
    chans = query_ref.shape[1]
    cells = TILE * TILE
    scale = HEAD_DIM ** (-0.5)
    all_ref[...] = stack_rows(part_refs)
    weights = wide_cols(piece_refs, 3 * chans, chans)
    d_mixed_ref[...] = dot(all_ref[...], weights, (1, 1)).astype(low)
    masks = head_masks(cells)
    for batch in range(query_ref.shape[0] // cells):
        at = slice(batch * cells, (batch + 1) * cells)
        for pair in range(chans // LANES):
            lanes = slice(pair * LANES, (pair + 1) * LANES)
            value_lanes = slice(chans + pair * LANES, chans + (pair + 1) * LANES)
            keys = cat([ref[at, lanes] for ref in kv_refs], 0)
            values = cat([ref[at, value_lanes] for ref in kv_refs], 0)
            query = query_ref[at, lanes]
            d_mixed = d_mixed_ref[at, lanes]
            d_queries = []
            d_keys = 0.0
            d_values = 0.0
            for mask in masks:
                own_query = jnp.where(mask, query, jnp.zeros_like(query))
                own_mixed = jnp.where(mask, d_mixed, jnp.zeros_like(d_mixed))
                probs = softmax_parts(own_query, keys)
                d_probs = dot(own_mixed, values, (1, 1))
                inner = jnp.sum(probs * d_probs, axis=-1, keepdims=True)
                d_scores = (probs * (d_probs - inner)).astype(low)
                d_queries.append(dot(d_scores, keys))
                d_keys = d_keys + dot(d_scores, own_query, (0, 0))
                d_values = d_values + dot(probs.astype(low), own_mixed, (0, 0))
            d_query = jnp.where(masks[0], d_queries[0], d_queries[1]) * scale
            d_query_ref[at, lanes] = d_query.astype(low)
            d_keys = d_keys * scale
            for i in range(4):
                target = (keep_ref, send_ref)[i // 2]
                own = slice(i * cells, (i + 1) * cells)
                target[i % 2, at, lanes] = d_keys[own].astype(target.dtype)
                target[i % 2, at, value_lanes] = d_values[own].astype(target.dtype)


def add_pair_body(keep_ref, got_ref, own_ref, send_ref):
    own_ref[...] = keep_ref[0] + got_ref[0].astype(wide)
    send_ref[...] = (keep_ref[1] + got_ref[1].astype(wide)).astype(low)


def d_qkv_body(d_query_ref, own_ref, got_ref, *refs):
    piece_refs, (d_qkv_ref, *out_refs) = refs[:BLOCKS], refs[BLOCKS:]
    chans = d_query_ref.shape[1]
    d_qkv_ref[:, :chans] = d_query_ref[...]
    d_qkv_ref[:, chans:] = (own_ref[...] + got_ref[...].astype(wide)).astype(low)
    d_qkv = d_qkv_ref[...]
    count = 3 * chans // LANES
    for pair in range(BLOCKS // 2):
        weights = wide_rows(piece_refs[2 * pair : 2 * pair + 2], 0, count)
        lanes = slice(2 * pair * LANES, 2 * (pair + 1) * LANES)
        write_chunks(dot(d_qkv, weights, (1, 1)), out_refs, lanes)


def gate_back_body(gate_ref, spread_ref, *refs):
    heads = lax.axis_size("heads")
    head = lax.axis_index("heads")
    part_refs, piece_refs = refs[:heads], refs[heads : heads + BLOCKS]
    all_ref, d_gate_ref, grid_ref, col_ref, row_ref, corner_ref, hold = refs[heads + BLOCKS :]
    all_ref[...] = stack_rows(part_refs)
    chans = gate_ref.shape[1]
    d_joined = dot(all_ref[...], wide_cols(piece_refs, chans, chans), (1, 1))
    gate = gate_ref[...]
    d_gate_ref[...] = (d_joined * spread_ref[...] * (1.0 - gate * gate)).astype(low)
    d_spread = d_joined * gate
    shard = gate.shape[0] // heads
    for j in range(heads):
        to = pl.ds(pl.multiple_of(shard * (head ^ j), 8), shard)
        grid_ref[to] = d_spread[j * shard : (j + 1) * shard]
    send_edges(grid_ref, hold, col_ref, row_ref, corner_ref)


def d_tokens_body(d_gate_ref, *refs):
    piece_refs, out_refs = refs[:BLOCKS], refs[BLOCKS:]
    count = d_gate_ref.shape[1] // LANES
    weights = wide_rows(piece_refs, 0, count)
    write_chunks(dot(d_gate_ref[...], weights, (1, 1)), out_refs)


def depthwise_back_body(grid_ref, col_ref, row_ref, corner_ref, dw_ref, pad_ref, *refs):
    out_ref, taps_ref, d_pad, hold, flat = refs
    fill_padded(grid_ref, col_ref, row_ref, corner_ref, d_pad, hold)
    cells = TILE * TILE
    batches = grid_ref.shape[0] // cells
    per_batch = (TILE + 2) * PAD
    chans = grid_ref.shape[1]
    sums = [jnp.zeros((TILE, chans), wide) for _ in range(10)]
    for batch in range(batches):
        for a in range(TILE):
            own = grid_ref[batch * cells + a * TILE : batch * cells + (a + 1) * TILE]
            running = jnp.zeros((TILE, chans), wide)
            for tap in range(9):
                row, col = divmod(tap, 3)
                at = batch * per_batch + (a + 2 - row) * PAD + 2 - col
                running = running + dw_ref[tap : tap + 1] * d_pad[at : at + TILE]
                at = batch * per_batch + (a + row) * PAD + col
                sums[tap] = sums[tap] + own * pad_ref[at : at + TILE]
            sums[9] = sums[9] + own
            flat[batch * cells + a * TILE : batch * cells + (a + 1) * TILE] = running
    out_ref[...] = flat[...].astype(low)
    for tap in range(10):
        taps_ref[tap : tap + 1] = jnp.sum(sums[tap], axis=0, keepdims=True)


def conv_back_body(pool_ref, whole_ref, *refs):
    heads = lax.axis_size("heads")
    head = lax.axis_index("heads")
    part_refs, (hires_ref,) = refs[:heads], refs[heads:]
    per_chunk = BLOCKS // heads
    d_pooled = 0.0
    for j, ref in enumerate(part_refs):
        first = per_chunk * (head ^ j)
        chunk = cat([whole_ref[first + i] for i in range(per_chunk)], 1)
        d_pooled = d_pooled + dot(ref[...], chunk, (1, 1))
    d_pooled = d_pooled.astype(low)
    batches = pool_ref.shape[0]
    rows = pool_ref.shape[1]
    for batch in range(batches):
        own = d_pooled[batch * rows : (batch + 1) * rows]
        hires_ref[batch] = dot(pool_ref[batch], own, (0, 0))


def conv_grad_body(pooled_ref, *refs):
    heads = lax.axis_size("heads")
    head = lax.axis_index("heads")
    part_refs, (keep_ref, send_ref, hold) = refs[:heads], refs[heads:]
    per_chunk = BLOCKS // heads
    for j, ref in enumerate(part_refs):
        grad = dot(pooled_ref[...], ref[...], (0, 0)).astype(low)
        for i in range(per_chunk):
            hold[per_chunk * (head ^ j) + i] = grad[:, i * LANES : (i + 1) * LANES]
    for place in range(BLOCKS):
        target = (keep_ref, send_ref)[place // 4]
        target[place % 4] = hold[block_at(place)]


def place_refs(keep_ref, send_ref, place):
    return ((keep_ref, send_ref)[place // 4]).at[place % 4]


def row_grad(left_ref, right, keep_ref, send_ref, start):
    count = right.shape[1] // LANES
    for place in range(BLOCKS):
        lanes = slice(place * LANES, (place + 1) * LANES)
        grad = dot(left_ref[:, lanes], right, (0, 0)).astype(low)
        target = place_refs(keep_ref, send_ref, place)
        for m in range(count):
            target[start + m * LANES : start + (m + 1) * LANES] = grad[
                :, m * LANES : (m + 1) * LANES
            ]


def col_grad(left_ref, right_ref, keep_ref, send_ref, start):
    width = left_ref.shape[1]
    for m in range(width // LANES):
        grad = dot(left_ref[:, m * LANES : (m + 1) * LANES], right_ref[...], (0, 0)).astype(low)
        for place in range(BLOCKS):
            target = place_refs(keep_ref, send_ref, place)
            target[start + m * LANES : start + (m + 1) * LANES] = grad[
                :, place * LANES : (place + 1) * LANES
            ]


def pair_grad_body(row_left, row_right, col_left, col_right, keep_ref, send_ref):
    width = row_right.shape[1]
    row_grad(row_left, row_right[...], keep_ref, send_ref, 0)
    col_grad(col_left, col_right, keep_ref, send_ref, width)


def final_rows(refs, start, count):
    return cat(
        [total_of(refs, slice(start + m * LANES, start + (m + 1) * LANES)) for m in range(count)],
        1,
    )


def conv_final_body(*refs):
    refs[-1][...] = total_of(refs[:-1])


def gate_join_final_body(*refs):
    part_refs, (gate_ref, join_ref) = refs[:-2], refs[-2:]
    chans = gate_ref.shape[1]
    gate_ref[...] = final_rows(part_refs, 0, chans // LANES)
    join_ref[...] = total_of(part_refs, slice(chans, chans + join_ref.shape[0]))


def attn_proj_final_body(*refs):
    part_refs, (attn_ref, out_ref) = refs[:-2], refs[-2:]
    chans = attn_ref.shape[2]
    for s in range(3):
        attn_ref[s] = final_rows(part_refs, s * chans, chans // LANES)
    out_ref[...] = total_of(part_refs, slice(3 * chans, 3 * chans + out_ref.shape[0]))


def unpack_rows(packed, count):
    places = packed.shape[0]
    return (
        packed.reshape(places, count, LANES, LANES)
        .transpose(0, 2, 1, 3)
        .reshape(places * LANES, count * LANES)
    )


def unpack_cols(packed):
    return packed.transpose(1, 0, 2).reshape(packed.shape[1], -1)


def pack_rows(weights):
    count = weights.shape[1] // LANES
    return (
        weights.reshape(BLOCKS, LANES, count, LANES)
        .transpose(0, 2, 1, 3)
        .reshape(BLOCKS, count * LANES, LANES)
    )


def pack_cols(weights):
    return weights.reshape(weights.shape[0], BLOCKS, LANES).transpose(1, 0, 2)


def scatter_dim(grad, axis):
    return lax.psum_scatter(grad, "tiles", scatter_dimension=axis, tiled=True).astype(wide)


def local(
    vit_tokens,
    hires_maps,
    map_sizes,
    out_grad,
    ln_gain,
    ln_bias,
    dw_params,
    conv_w,
    gate_w,
    join_w,
    attn_in_w,
    out_w,
    up_w,
    down_w,
):
    tile = lax.axis_index("tiles")
    tiles = lax.axis_size("tiles")
    heads = lax.axis_size("heads")
    fast = fast_tiles()
    batches, rows, width = vit_tokens.shape
    total = batches * rows
    shard = total // heads
    chans = dw_params.shape[1]
    hidden_width = down_w.shape[0]
    pixels, hires_chans = hires_maps.shape[1:]

    if fast:
        gj_own, ap_own, ud_own = run_kernel(
            pack_body,
            [
                shape((2 * chans, LANES)),
                shape((4 * chans, LANES)),
                shape((2 * hidden_width, LANES)),
            ],
            gate_w,
            join_w,
            attn_in_w,
            out_w,
            up_w,
            down_w,
        )
        conv_pieces = gather_blocks(conv_w)
        gj_pieces = gather_blocks(gj_own)
        ap_pieces = gather_blocks(ap_own)
        ud_pieces = gather_blocks(ud_own)
    else:

        def whole_of(weights, axis):
            return lax.all_gather(weights, "tiles", axis=axis, tiled=True)

        def listed(*packed):
            joint = jnp.concatenate(packed, axis=1)
            return [joint[p] for p in range(BLOCKS)]

        conv_pieces = listed(pack_cols(whole_of(conv_w, 1)))
        gj_pieces = listed(pack_rows(whole_of(gate_w, 0)), pack_cols(whole_of(join_w, 1)))
        attn_whole = whole_of(attn_in_w, 1)
        ap_pieces = listed(
            *[pack_rows(attn_whole[s]) for s in range(3)], pack_cols(whole_of(out_w, 1))
        )
        ud_pieces = listed(pack_rows(whole_of(up_w, 0)), pack_cols(whole_of(down_w, 1)))

    tokens, upstream, gains, biases = run_kernel(
        relative_body,
        [
            shape((total, width)),
            shape((total, width)),
            shape(ln_gain.shape, wide),
            shape(ln_bias.shape, wide),
        ],
        vit_tokens.reshape(total, width),
        out_grad.reshape(total, width),
        ln_gain,
        ln_bias,
        scratch=[((total, LANES), wide)],
    )

    sides = lax.dynamic_index_in_dim(map_sizes, tile // 4, axis=1, keepdims=False)
    pools = pool_matrices(sides)
    pooled = jnp.concatenate(
        [dot(pools[batch], hires_maps[batch]).astype(low) for batch in range(batches)], axis=0
    )
    conv_whole, *conv_parts = run_kernel(
        conv_body,
        [shape((BLOCKS, hires_chans, LANES))] + [shape((total, chans))] * heads,
        pooled,
        *conv_pieces,
        flops=2 * total * hires_chans * width,
    )
    edge_shapes = [
        shape((batches * TILE, chans)),
        shape((batches * PAD, chans)),
        shape((PAD, chans)),
    ]
    edge_scratch = ((batches * PAD, chans), wide)
    grid_scratch = ((total, chans), wide)
    pad_dims = (batches * (TILE + 2) * PAD, chans)
    mapped, *edges = run_kernel(
        map_body,
        [shape((total, chans))] + edge_shapes,
        *scatter_heads(conv_parts),
        scratch=[grid_scratch, edge_scratch],
    )

    def swap_edges(col, row, corner):
        return over_core(col), over_x(row), swap_with(corner, "tiles", 3)

    edges = swap_edges(*edges)

    (gate,) = run_kernel(
        gate_body, [shape((total, chans), wide)], tokens, *gj_pieces, flops=2 * total * chans * width
    )
    chunk_shapes = [shape((shard, width))] * heads
    padded, spread, joined, *join_parts = run_kernel(
        depthwise_body,
        [shape(pad_dims, wide), shape((total, chans), wide), shape((total, chans))] + chunk_shapes,
        mapped,
        *edges,
        dw_params,
        gate,
        *gj_pieces,
        scratch=[grid_scratch, edge_scratch, grid_scratch],
        flops=2 * total * chans * width,
    )
    row_shapes = [shape((shard, width), wide), shape((shard, width))]
    first, normed1_own = run_kernel(
        norm_body, row_shapes, tokens, gains[0:1], biases[0:1], *scatter_heads(join_parts)
    )

    normed1, query, kv_own = run_kernel(
        qkv_body,
        [shape((total, width)), shape((total, chans)), shape((total, 2 * chans))],
        *gather_heads(normed1_own),
        *ap_pieces,
        flops=6 * total * chans * width,
    )
    kv_x = over_x(kv_own)
    kv_all = [kv_own, kv_x, over_core(kv_own), over_core(kv_x)]
    mixed, *proj_parts = run_kernel(
        attend_body,
        [shape((total, chans))] + chunk_shapes,
        query,
        *kv_all,
        *ap_pieces,
        flops=2 * total * chans * width + 8 * total * 4 * rows * chans,
    )
    second, normed2_own = run_kernel(
        norm_body, row_shapes, first, gains[1:2], biases[1:2], *scatter_heads(proj_parts)
    )

    wide_shape = shape((total, hidden_width))
    normed2, hidden, d_hidden, *ffn_parts = run_kernel(
        ffn_body,
        [shape((total, width)), wide_shape, wide_shape] + chunk_shapes,
        upstream,
        *gather_heads(normed2_own),
        *ud_pieces,
        scratch=[((total, width), wide)],
        flops=6 * total * hidden_width * width,
    )
    back_shapes = row_shapes + [shape((2, width), wide)]
    d_second, d_attn_own, ln2_sums = run_kernel(
        norm_back_body, back_shapes, second, upstream, gains[1:2], *scatter_heads(ffn_parts)
    )
    d_attn_parts = gather_heads(d_attn_own)
    down_parts = run_kernel(
        down_body, chunk_shapes, hidden, *ud_pieces, flops=2 * total * hidden_width * width
    )
    (result_own,) = run_kernel(
        whole_cols_body, [shape((shard, width))], second, *scatter_heads(down_parts)
    )
    (block_out,) = run_kernel(
        whole_rows_body,
        [shape((total, width))],
        *gather_heads(result_own),
        scratch=[((total, width), wide)],
    )
    ud_keep, ud_send = run_kernel(
        pair_grad_body,
        [shape((4, 2 * hidden_width, LANES))] * 2,
        normed2,
        d_hidden,
        hidden,
        upstream,
        flops=4 * total * hidden_width * width,
    )
    ud_sums = scatter_blocks(ud_keep, ud_send)

    d_attn, d_query, kv_keep, kv_send = run_kernel(
        attend_back_body,
        [
            shape((total, width)),
            shape((total, chans)),
            shape((2, total, 2 * chans), wide),
            shape((2, total, 2 * chans)),
        ],
        query,
        *kv_all,
        *d_attn_parts,
        *ap_pieces,
        scratch=[((total, chans), low)],
        flops=2 * total * chans * width + 20 * total * 4 * rows * chans,
    )
    kv_mine, kv_over = run_kernel(
        add_pair_body,
        [shape((total, 2 * chans), wide), shape((total, 2 * chans))],
        kv_keep,
        over_core(kv_send),
    )
    d_qkv, *qkv_parts = run_kernel(
        d_qkv_body,
        [shape((total, 3 * chans))] + chunk_shapes,
        d_query,
        kv_mine,
        over_x(kv_over),
        *ap_pieces,
        flops=6 * total * chans * width,
    )
    d_first, d_join_own, ln1_sums = run_kernel(
        norm_back_body, back_shapes, first, d_second, gains[0:1], *scatter_heads(qkv_parts)
    )
    ap_keep, ap_send = run_kernel(
        pair_grad_body,
        [shape((4, 4 * chans, LANES))] * 2,
        normed1,
        d_qkv,
        mixed,
        d_attn,
        flops=8 * total * chans * width,
    )
    ap_sums = scatter_blocks(ap_keep, ap_send)

    d_join, d_gate_in, d_grid, *edges = run_kernel(
        gate_back_body,
        [shape((total, width)), shape((total, chans)), shape((total, chans), wide)] + edge_shapes,
        gate,
        spread,
        *gather_heads(d_join_own),
        *gj_pieces,
        scratch=[edge_scratch],
        flops=2 * total * chans * width,
    )
    edges = swap_edges(*edges)
    d_mapped, taps_sum = run_kernel(
        depthwise_back_body,
        [shape((total, chans)), shape(dw_params.shape, wide)],
        d_grid,
        *edges,
        dw_params,
        padded,
        scratch=[(pad_dims, wide), edge_scratch, grid_scratch],
    )
    d_mapped_parts = gather_heads(d_mapped)
    token_parts = run_kernel(
        d_tokens_body, chunk_shapes, d_gate_in, *gj_pieces, flops=2 * total * chans * width
    )
    (d_tokens_own,) = run_kernel(
        whole_cols_body, [shape((shard, width))], d_first, *scatter_heads(token_parts)
    )
    gj_keep, gj_send = run_kernel(
        pair_grad_body,
        [shape((4, 2 * chans, LANES))] * 2,
        tokens,
        d_gate_in,
        joined,
        d_join,
        flops=4 * total * chans * width,
    )
    gj_sums = scatter_blocks(gj_keep, gj_send)
    conv_keep, conv_send = run_kernel(
        conv_grad_body,
        [shape((4, hires_chans, LANES))] * 2,
        pooled,
        *d_mapped_parts,
        scratch=[((BLOCKS, hires_chans, LANES), low)],
        flops=2 * total * hires_chans * width,
    )
    conv_sums = scatter_blocks(conv_keep, conv_send)
    (hires_grad,) = run_kernel(
        conv_back_body,
        [shape((batches, pixels, hires_chans), wide)],
        pools,
        conv_whole,
        *d_mapped_parts,
        flops=2 * total * hires_chans * width + 2 * total * pixels * hires_chans,
    )
    (tokens_grad,) = run_kernel(
        whole_rows_body,
        [shape((total, width), wide)],
        *gather_heads(d_tokens_own),
        scratch=[((8, LANES), wide)],
    )

    ln_sums = jnp.concatenate([ln1_sums, ln2_sums], axis=0)
    bit = 1
    while bit < heads:
        ln_sums = ln_sums + swap_with(ln_sums, "heads", bit)
        bit *= 2
    bit = 1
    while bit < tiles:
        ln_sums = ln_sums + swap_with(ln_sums, "tiles", bit)
        taps_sum = taps_sum + swap_with(taps_sum, "tiles", bit)
        bit *= 2

    if fast:
        (conv_grad,) = run_kernel(conv_final_body, [shape(conv_w.shape, wide)], *conv_sums)
        gate_grad, join_grad = run_kernel(
            gate_join_final_body, [shape(gate_w.shape, wide), shape(join_w.shape, wide)], *gj_sums
        )
        attn_grad, out_w_grad = run_kernel(
            attn_proj_final_body,
            [shape(attn_in_w.shape, wide), shape(out_w.shape, wide)],
            *ap_sums,
        )
        up_grad, down_grad = run_kernel(
            gate_join_final_body, [shape(up_w.shape, wide), shape(down_w.shape, wide)], *ud_sums
        )
    else:
        count = chans // LANES
        conv_grad = scatter_dim(unpack_cols(conv_sums), 1)
        gate_grad = scatter_dim(unpack_rows(gj_sums[:, :chans], count), 0)
        join_grad = scatter_dim(unpack_cols(gj_sums[:, chans:]), 1)
        attn_grad = jnp.stack(
            [
                scatter_dim(unpack_rows(ap_sums[:, s * chans : (s + 1) * chans], count), 0)
                for s in range(3)
            ]
        )
        out_w_grad = scatter_dim(unpack_cols(ap_sums[:, 3 * chans :]), 1)
        up_grad = scatter_dim(unpack_rows(ud_sums[:, :hidden_width], hidden_width // LANES), 0)
        down_grad = scatter_dim(unpack_cols(ud_sums[:, hidden_width:]), 1)

    return (
        block_out.reshape(batches, rows, width),
        tokens_grad.reshape(batches, rows, width),
        hires_grad,
        ln_sums[:2],
        ln_sums[2:],
        taps_sum,
        conv_grad,
        gate_grad,
        join_grad,
        attn_grad,
        out_w_grad,
        up_grad,
        down_grad,
    )


def solution(mesh):
    placed = (
        P(None, "tiles", None),
        P(None, "tiles", "heads"),
        P(),
        P(None, "tiles", None),
        P(),
        P(),
        P(None, "heads"),
        P("heads", "tiles"),
        P("tiles", "heads"),
        P("heads", "tiles"),
        P(None, "tiles", "heads"),
        P("heads", "tiles"),
        P("tiles", "heads"),
        P("heads", "tiles"),
    )
    return jax.shard_map(
        local,
        mesh=mesh,
        in_specs=placed,
        out_specs=(
            P(None, "tiles", None),
            P(None, "tiles", None),
            P(None, "tiles", "heads"),
            P(),
            P(),
            P(None, "heads"),
            P("heads", "tiles"),
            P("tiles", "heads"),
            P("heads", "tiles"),
            P(None, "tiles", "heads"),
            P("heads", "tiles"),
            P("tiles", "heads"),
            P("heads", "tiles"),
        ),
        check_vma=False,
    )
```

```python
import jax
import jax.numpy as jnp
from jax import lax
from jax.experimental import pallas as pl
from jax.experimental.pallas import tpu as pltpu
from jax.sharding import PartitionSpec as P

HEAD_DIM = 64
GRID = 24
TILE = 12
HR_TILE = 24
PAD = 16
LANES = 128

norm_eps = 1e-05
inv_root_two = 0.7071067811865476
inv_root_two_pi = 0.3989422804014327

low = jnp.bfloat16
wide = jnp.float32
VMEM_LIMIT = 24 * 1024 * 1024


def shape(dims, kind=low):
    return jax.ShapeDtypeStruct(tuple(dims), kind)


def after(value, *others):
    return lax.optimization_barrier((value, *others))[0]


def run_kernel(body, outs, *args, scratch=(), flops=0, leave=False, fetch=False, alias=None):
    whole = pl.BlockSpec(memory_space=pltpu.VMEM)
    source = pl.BlockSpec(memory_space=pltpu.HBM) if fetch else whole
    target = pl.BlockSpec() if leave else whole
    if fetch:
        args = [pltpu.with_memory_space_constraint(arg, pltpu.HBM) for arg in args]
    traffic = sum(a.size * a.dtype.itemsize for a in args)
    traffic += sum(o.size * o.dtype.itemsize for o in outs)
    return pl.pallas_call(
        body,
        name=body.__name__,
        out_shape=tuple(outs),
        in_specs=[source] * len(args),
        out_specs=tuple([target] * len(outs)),
        scratch_shapes=[pltpu.VMEM(dims, kind) if dims else kind for dims, kind in scratch],
        input_output_aliases=alias or {},
        cost_estimate=pl.CostEstimate(flops=1, bytes_accessed=1, transcendentals=0),
        compiler_params=pltpu.CompilerParams(vmem_limit_bytes=VMEM_LIMIT),
    )(*args)


def dot(left, right, contract=(1, 0)):
    return lax.dot_general(
        left, right, (((contract[0],), (contract[1],)), ((), ())), preferred_element_type=wide
    )


def cat(parts, axis):
    return parts[0] if len(parts) == 1 else jnp.concatenate(parts, axis=axis)


def swap_with(value, axis, mask):
    pairs = [(source, source ^ mask) for source in range(lax.axis_size(axis))]
    return lax.ppermute(value, axis, pairs)


def over_core(value):
    return swap_with(value, "tiles", 1)


def over_x(value):
    return swap_with(value, "tiles", 2)


def over_y(value):
    return swap_with(value, "tiles", 4)


def fast_tiles():
    return lax.axis_size("tiles") == 8


BLOCKS = 8


def place_mask(place):
    half = BLOCKS // 2
    return ((place % half) * 2) | (place // half)


def block_at(place):
    if fast_tiles():
        return lax.axis_index("tiles") ^ place_mask(place)
    return place


def gather_first(block):
    found = [block, over_x(block), over_y(block), swap_with(block, "tiles", 6)]
    return found + [over_core(part) for part in found]


def stack_body(*refs):
    for i, ref in enumerate(refs[:-1]):
        refs[-1][i] = ref[...]


def stacked(*parts):
    return run_kernel(stack_body, [shape((len(parts), *parts[0].shape))], *parts)[0]


def stack_corner_body(*refs):
    *part_refs, upper_ref, lower_ref, out_ref = refs
    for i, ref in enumerate(part_refs):
        out_ref[i] = ref[...]
    cut = upper_ref.shape[0]
    out_ref[len(part_refs), 0:cut] = upper_ref[...]
    out_ref[len(part_refs), cut:] = lower_ref[...]


def rows_of(*stacks):
    return [ref.at[i] for ref in stacks for i in range(ref.shape[0])]


def scatter_heads(parts):
    return [parts[0]] + [swap_with(parts[j], "heads", j) for j in range(1, len(parts))]


def gather_heads(own):
    return [own] + [swap_with(own, "heads", j) for j in range(1, lax.axis_size("heads"))]


def add_rows_body(keep_ref, got_ref, *out_refs):
    for i, out_ref in enumerate(out_refs):
        total = keep_ref[i].astype(wide) + got_ref[i].astype(wide)
        out_ref[...] = total.astype(out_ref.dtype)


def add_cores(keep, got):
    return run_kernel(add_rows_body, [shape(keep.shape[1:])] * 4, keep, got)


def over_corner(value):
    return swap_with(value, "tiles", 6)


def gelu_parts(inputs):
    bell = 0.5 * (1.0 + lax.erf(inputs * inv_root_two))
    return inputs * bell, bell + inputs * inv_root_two_pi * jnp.exp(-0.5 * inputs * inputs)


def normed(values):
    centred = values - jnp.mean(values, axis=-1, keepdims=True)
    inv_std = lax.rsqrt(jnp.mean(centred * centred, axis=-1, keepdims=True) + norm_eps)
    return centred * inv_std, inv_std


def total_of(refs, at=Ellipsis):
    total = refs[0][at].astype(wide)
    for ref in refs[1:]:
        total = total + ref[at].astype(wide)
    return total


def copies(pairs, sems):
    started = [
        pltpu.make_async_copy(source, target, sems.at[i])
        for i, (source, target) in enumerate(pairs)
    ]
    for copy in started:
        copy.start()
    for copy in started:
        copy.wait()


def lane_blocks(source, target, start):
    rows, lanes = source.shape
    return [
        (
            source.at[:, pl.ds(m * LANES, LANES)],
            target.at[pl.ds(start + m * rows, rows)],
        )
        for m in range(lanes // LANES)
    ]


def pack_first_body(conv_ref, gate_ref, join_ref, out_w_ref, first_ref, cross_ref, sems):
    at = conv_ref.shape[0]
    pairs = [(conv_ref, first_ref.at[pl.ds(0, at)])]
    pairs += lane_blocks(gate_ref, first_ref, at)
    pairs += lane_blocks(gate_ref, cross_ref, 0)
    rows = join_ref.shape[0]
    pairs += [(join_ref, cross_ref.at[pl.ds(rows, rows)])]
    pairs += [(out_w_ref, cross_ref.at[pl.ds(2 * rows, rows)])]
    copies(pairs, sems)


def pack_rest_body(attn_ref, up_ref, down_ref, *refs):
    cross_refs, (second_ref, third_ref, sems) = refs[:-3], refs[-3:]
    rows = cross_refs[0].shape[0] // 3
    heads = len(cross_refs)
    pairs = []
    for j, ref in enumerate(cross_refs):
        pairs += [(ref.at[pl.ds(rows, rows)], second_ref.at[pl.ds(j * rows, rows)])]
        pairs += [(ref.at[pl.ds(2 * rows, rows)], third_ref.at[pl.ds(j * rows, rows)])]
        if j:
            at = (heads + j - 1) * rows
            pairs += [(ref.at[pl.ds(0, rows)], third_ref.at[pl.ds(at, rows)])]
    for s in range(3):
        pairs += lane_blocks(attn_ref.at[s], second_ref, (heads + s) * rows)
    pairs += lane_blocks(up_ref, third_ref, (2 * heads - 1) * rows)
    rows = down_ref.shape[0]
    pairs += [(down_ref, third_ref.at[pl.ds(third_ref.shape[0] - rows, rows)])]
    copies(pairs, sems)


def third_refs(refs, results):
    count = len(refs) - results
    if count == 2:
        pieces = rows_of(*refs[:2])
        return pieces, pieces, refs[2:]
    stack, upper, lower, core_stack, core_upper, core_lower = refs[:6]
    own, core = rows_of(stack), rows_of(core_stack)
    return own + [upper] + core + [core_upper], own + [lower] + core + [core_lower], refs[6:]


def views(refs, start, rows):
    return [ref if ref.shape[0] == rows else ref.at[pl.ds(start, rows)] for ref in refs]


def whole_number(value, parts):
    return jnp.floor((value + 0.5) * (1.0 / parts))


def pool_body(sides_ref, maps_ref, pooled_ref, pool_ref, hold, sems):
    copy = pltpu.make_async_copy(maps_ref, hold, sems.at[0])
    copy.start()
    image = lax.axis_index("tiles") // 4
    cells, pixels = pool_ref.shape[1:]
    cell = lax.broadcasted_iota(jnp.int32, (cells, pixels), 0).astype(wide)
    pixel = lax.broadcasted_iota(jnp.int32, (cells, pixels), 1).astype(wide)
    cell_row = whole_number(cell, TILE)
    pixel_row = whole_number(pixel, HR_TILE)
    spots = (
        (cell_row, pixel_row),
        (cell - TILE * cell_row, pixel - HR_TILE * pixel_row),
    )
    for batch in range(pool_ref.shape[0]):
        side = sides_ref[batch, image].astype(wide)
        weights = 1.0
        for cell_at, pixel_at in spots:
            begin = whole_number(cell_at * side, GRID)
            end = whole_number((cell_at + 1.0) * side + (GRID - 1.0), GRID)
            inside = jnp.logical_and(pixel_at >= begin, pixel_at < end)
            weights = weights * jnp.where(inside, 1.0 / (end - begin), 0.0)
        pool_ref[batch] = weights.astype(low)
    copy.wait()
    for batch in range(pool_ref.shape[0]):
        pooled = dot(pool_ref[batch], hold[batch])
        pooled_ref[batch * cells : (batch + 1) * cells] = pooled.astype(low)


def wide_rows(refs, start, count):
    return cat(
        [
            cat([ref[start + m * LANES : start + (m + 1) * LANES] for m in range(count)], 1)
            for ref in refs
        ],
        0,
    )


def wide_cols(refs, start, rows):
    return cat([ref[start : start + rows] for ref in refs], 1)


def relative_body(*refs):
    count = len(refs[:-1]) // 3
    sources, outs, found = refs[:count], refs[count : 2 * count], refs[2 * count : -1]
    copies(list(zip(sources, found)), refs[-1])
    for source, target in zip(found, outs):
        for place in range(BLOCKS):
            lanes = pl.ds(pl.multiple_of(LANES * block_at(place), LANES), LANES)
            target[:, place * LANES : (place + 1) * LANES] = source[:, lanes]


def conv_body(pooled_ref, *refs):
    piece_refs, (whole_ref, *out_refs) = refs[:BLOCKS], refs[BLOCKS:]
    head = lax.axis_index("heads")
    for place, ref in enumerate(piece_refs):
        whole_ref[block_at(place)] = ref[0 : whole_ref.shape[1]]
    per_chunk = BLOCKS // len(out_refs)
    for j, out_ref in enumerate(out_refs):
        first = per_chunk * (head ^ j)
        chunk = cat([whole_ref[first + i] for i in range(per_chunk)], 1)
        out_ref[...] = dot(pooled_ref[...], chunk).astype(low)


def edge_flags():
    tile = lax.axis_index("tiles")
    return (tile & 1) == 0, (tile & 2) == 0


def send_edges(grid, hold_ref, col_ref, row_ref, corner_ref):
    right, lower = edge_flags()
    cells = TILE * TILE
    batches = grid.shape[0] // cells
    count = batches * TILE
    for at in range(count):
        begin = at * TILE
        end = begin + TILE - 1
        hold_ref[at : at + 1] = jnp.where(right, grid[end : end + 1], grid[begin : begin + 1])
    col_ref[...] = hold_ref[0:count].astype(low)
    hold_ref[...] = jnp.zeros(hold_ref.shape, wide)
    for batch in range(batches):
        base = batch * cells
        bottom = grid[base + cells - TILE : base + cells]
        top = grid[base : base + TILE]
        edge = jnp.where(lower, bottom, top)
        hold_ref[batch * PAD : batch * PAD + TILE] = edge
    row_ref[...] = hold_ref[...].astype(low)
    hold_ref[...] = jnp.zeros(hold_ref.shape, wide)
    for batch in range(batches):
        base = batch * cells
        ends = [
            jnp.where(right, grid[at + TILE - 1 : at + TILE], grid[at : at + 1])
            for at in (base + cells - TILE, base)
        ]
        hold_ref[batch : batch + 1] = jnp.where(lower, ends[0], ends[1])
    corner_ref[...] = hold_ref[0:PAD].astype(low)


def fill_padded(grid, col_ref, row_ref, corner_ref, pad_ref, hold_ref):
    right, lower = edge_flags()
    cells = TILE * TILE
    batches = grid.shape[0] // cells
    per_batch = (TILE + 2) * PAD
    pad_ref[...] = jnp.zeros(pad_ref.shape, wide)
    hold_ref[0 : batches * TILE] = col_ref[...].astype(wide)
    for batch in range(batches):
        for a in range(TILE):
            at = batch * per_batch + (a + 1) * PAD
            source = batch * cells + a * TILE
            pad_ref[at + 1 : at + 1 + TILE] = grid[source : source + TILE]
            got = hold_ref[batch * TILE + a : batch * TILE + a + 1]
            zero = jnp.zeros_like(got)
            pad_ref[at : at + 1] = jnp.where(right, zero, got)
            pad_ref[at + TILE + 1 : at + TILE + 2] = jnp.where(right, got, zero)
    rows = row_ref[...].astype(wide)
    corners = corner_ref[...].astype(wide)
    for batch in range(batches):
        got = rows[batch * PAD : batch * PAD + TILE]
        corner = corners[batch : batch + 1]
        zero = jnp.zeros_like(got)
        nil = jnp.zeros_like(corner)
        for at, used in (
            (batch * per_batch, jnp.logical_not(lower)),
            (batch * per_batch + (TILE + 1) * PAD, lower),
        ):
            pad_ref[at + 1 : at + 1 + TILE] = jnp.where(used, got, zero)
            left = jnp.logical_and(used, jnp.logical_not(right))
            pad_ref[at : at + 1] = jnp.where(left, corner, nil)
            pad_ref[at + TILE + 1 : at + TILE + 2] = jnp.where(
                jnp.logical_and(used, right), corner, nil
            )


def map_body(*refs):
    heads = lax.axis_size("heads")
    part_refs, (map_ref, col_ref, row_ref, corner_ref, grid, hold) = refs[:heads], refs[heads:]
    mapped = total_of(part_refs).astype(low)
    map_ref[...] = mapped
    grid[...] = mapped.astype(wide)
    send_edges(grid, hold, col_ref, row_ref, corner_ref)


def gate_body(tok_ref, *refs):
    piece_refs, (gate_ref,) = refs[:BLOCKS], refs[BLOCKS:]
    chans = gate_ref.shape[1]
    start = piece_refs[0].shape[0] - chans
    weights = wide_rows(views(piece_refs, start, chans), 0, chans // LANES)
    gate_ref[...] = jnp.tanh(dot(tok_ref[...], weights)).astype(wide)


def own_rows(ref, at, rows):
    return ref[pl.ds(pl.multiple_of(rows * at, 8), rows)]


def write_chunks(total_ref, out_refs):
    head = lax.axis_index("heads")
    rows = total_ref.shape[0] // len(out_refs)
    for j, out_ref in enumerate(out_refs):
        out_ref[...] = own_rows(total_ref, head ^ j, rows).astype(low)


def whole_rows(part_refs, hold_ref, rows):
    head = lax.axis_index("heads")
    for j, ref in enumerate(part_refs):
        to = pl.ds(pl.multiple_of(rows * (head ^ j), 8), rows)
        hold_ref[to] = ref[...].astype(wide)[:rows]
    return hold_ref[...].astype(low)


def depthwise_body(map_ref, col_ref, row_ref, corner_ref, dw_ref, gate_ref, *refs):
    pad_ref, spread_ref, joined_ref, grid, hold = refs
    grid[...] = map_ref[...].astype(wide)
    fill_padded(grid, col_ref, row_ref, corner_ref, pad_ref, hold)
    cells = TILE * TILE
    batches = grid.shape[0] // cells
    per_batch = (TILE + 2) * PAD
    for batch in range(batches):
        for a in range(TILE):
            running = jnp.broadcast_to(dw_ref[9:10], (TILE, grid.shape[1]))
            for tap in range(9):
                row, col = divmod(tap, 3)
                at = batch * per_batch + (a + row) * PAD + col
                running = running + dw_ref[tap : tap + 1] * pad_ref[at : at + TILE]
            to = batch * cells + a * TILE
            spread_ref[to : to + TILE] = running
    joined_ref[...] = (gate_ref[...] * spread_ref[...]).astype(low)


def project_all(rows_refs, piece_refs, base_ref, sum_ref):
    rows = cat([ref[...] for ref in rows_refs], 1)
    for pair in range(BLOCKS // 2):
        weights = wide_cols(piece_refs[2 * pair : 2 * pair + 2], 0, rows.shape[1])
        lanes = slice(2 * pair * LANES, 2 * (pair + 1) * LANES)
        sum_ref[:, lanes] = base_ref[:, lanes].astype(wide) + dot(rows, weights)


def join_body(tok_ref, gain_ref, bias_ref, *refs):
    heads = lax.axis_size("heads")
    part_refs, piece_refs = refs[:heads], rows_of(*refs[heads : heads + 2])
    first_ref, all_ref, query_ref, kv_ref = refs[heads + 2 :]
    chans = query_ref.shape[1]
    join_refs = views(piece_refs, 0, heads * chans)
    attn_refs = views(piece_refs, heads * chans, 3 * chans)
    project_all(part_refs, join_refs, tok_ref, first_ref)
    rows = (normed(first_ref[...])[0] * gain_ref[0:1] + bias_ref[0:1]).astype(low)
    all_ref[...] = rows
    count = chans // LANES
    for s in range(3):
        result = dot(all_ref[...], wide_rows(attn_refs, s * chans, count)).astype(low)
        if s == 0:
            query_ref[...] = result
        else:
            kv_ref[:, (s - 1) * chans : s * chans] = result


def head_masks(rows):
    lane = lax.broadcasted_iota(jnp.int32, (rows, LANES), 1)
    return [lane < HEAD_DIM, lane >= HEAD_DIM]


def softmax_parts(query, keys):
    scores = dot(query, keys, (1, 1)) * HEAD_DIM ** (-0.5)
    expo = jnp.exp(scores - jnp.max(scores, axis=-1, keepdims=True))
    return expo / jnp.sum(expo, axis=-1, keepdims=True)


def attend_body(query_ref, *refs):
    kv_refs, (mixed_ref,) = refs[:4], refs[4:]
    chans = query_ref.shape[1]
    cells = TILE * TILE
    masks = head_masks(cells)
    for batch in range(query_ref.shape[0] // cells):
        at = slice(batch * cells, (batch + 1) * cells)
        for pair in range(chans // LANES):
            lanes = slice(pair * LANES, (pair + 1) * LANES)
            value_lanes = slice(chans + pair * LANES, chans + (pair + 1) * LANES)
            keys = cat([ref[at, lanes] for ref in kv_refs], 0)
            values = cat([ref[at, value_lanes] for ref in kv_refs], 0)
            query = query_ref[at, lanes]
            found = []
            for mask in masks:
                probs = softmax_parts(jnp.where(mask, query, jnp.zeros_like(query)), keys)
                found.append(dot(probs.astype(low), values))
            mixed_ref[at, lanes] = jnp.where(masks[0], found[0], found[1]).astype(low)


HIDDEN_STEP = 256


def ffn_body(upstream_ref, first_ref, gain_ref, bias_ref, *refs):
    heads = lax.axis_size("heads")
    part_refs = refs[:heads]
    out_pieces, piece_refs, refs = third_refs(refs[heads:], 5 + heads)
    second_ref, all_ref, hidden_ref, d_hidden_ref = refs[:4]
    out_refs, total_ref = refs[4:-1], refs[-1]
    hidden_width = hidden_ref.shape[1]
    depth = heads * part_refs[0].shape[1]
    start = piece_refs[0].shape[0] - 2 * hidden_width
    piece_refs = views(piece_refs, start, 2 * hidden_width)
    project_all(part_refs, views(out_pieces, 0, depth), first_ref, second_ref)
    rows = normed(second_ref[...])[0] * gain_ref[1:2] + bias_ref[1:2]
    all_ref[...] = rows.astype(low)
    total_ref[...] = jnp.zeros(total_ref.shape, wide)
    per_step = HIDDEN_STEP // LANES

    def step(m, carry):
        at = pl.multiple_of(m * HIDDEN_STEP, HIDDEN_STEP)
        up = cat(
            [
                cat([ref[pl.ds(at + i * LANES, LANES)] for i in range(per_step)], 1)
                for ref in piece_refs
            ],
            0,
        )
        down = cat([ref[pl.ds(hidden_width + at, HIDDEN_STEP)] for ref in piece_refs], 1)
        value, slope = gelu_parts(dot(all_ref[...], up))
        hidden_ref[:, pl.ds(at, HIDDEN_STEP)] = value.astype(low)
        d_hidden = (dot(upstream_ref[...], down, (1, 1)) * slope).astype(low)
        d_hidden_ref[:, pl.ds(at, HIDDEN_STEP)] = d_hidden
        total_ref[...] += dot(d_hidden, up, (1, 1))
        return carry

    lax.fori_loop(0, hidden_width // HIDDEN_STEP, step, 0)
    write_chunks(total_ref, out_refs)


def down_body(hidden_ref, *refs):
    _, piece_refs, refs = third_refs(refs, 1 + lax.axis_size("heads"))
    out_refs, total_ref = refs[:-1], refs[-1]
    width = hidden_ref.shape[1]
    piece_refs = views(piece_refs, piece_refs[0].shape[0] - 2 * width, 2 * width)
    for pair in range(BLOCKS // 2):
        weights = wide_cols(piece_refs[2 * pair : 2 * pair + 2], width, width)
        lanes = slice(2 * pair * LANES, 2 * (pair + 1) * LANES)
        total_ref[:, lanes] = dot(hidden_ref[...], weights)
    write_chunks(total_ref, out_refs)


def whole_cols_body(base_ref, *refs):
    part_refs, out_ref = refs[:-1], refs[-1]
    head = lax.axis_index("heads")
    shard = out_ref.shape[0]
    for place in range(BLOCKS):
        lanes = slice(place * LANES, (place + 1) * LANES)
        mine = base_ref[pl.ds(pl.multiple_of(shard * head, 8), shard), lanes]
        total = mine + total_of(part_refs, (slice(None), lanes))
        to = pl.ds(pl.multiple_of(LANES * block_at(place), LANES), LANES)
        out_ref[:, to] = total.astype(low)


def block_out_body(*refs):
    part_refs, out_ref, hold = refs[:-2], refs[-2], refs[-1]
    out_ref[...] = whole_rows(part_refs, hold, part_refs[0].shape[0])


def tokens_grad_body(d_first_ref, *refs):
    heads = lax.axis_size("heads")
    part_refs, own_refs = refs[:heads], refs[heads : heads + BLOCKS]
    other_refs, _, (out_ref,) = third_refs(refs[heads + BLOCKS :], 1)
    chans = part_refs[0].shape[1]
    own_refs = views(own_refs, own_refs[0].shape[0] - chans, chans)
    other_refs = views(other_refs, heads * chans, (heads - 1) * chans)
    rows = cat([ref[...] for ref in part_refs], 1)
    count = chans // LANES
    for pair in range(BLOCKS // 2):
        both = slice(2 * pair, 2 * pair + 2)
        weights = [wide_rows(own_refs[both], 0, count)]
        weights += [wide_rows(other_refs[both], j * chans, count) for j in range(heads - 1)]
        lanes = slice(2 * pair * LANES, 2 * (pair + 1) * LANES)
        grad = d_first_ref[:, lanes].astype(wide) + dot(rows, cat(weights, 1), (1, 1))
        for i in range(2):
            block = block_at(2 * pair + i)
            to = pl.ds(pl.multiple_of(LANES * block, LANES), LANES)
            out_ref[:, to] = grad[:, i * LANES : (i + 1) * LANES]


def norm_back_body(values_ref, base_ref, gain_ref, *refs):
    part_refs, (sum_ref, low_ref) = refs[:-2], refs[-2:]
    rows = sum_ref.shape[0]
    head = lax.axis_index("heads")
    scaled, inv_std = normed(own_rows(values_ref, head, rows))
    upstream = total_of(part_refs)
    weighted = upstream * gain_ref[...]
    inner = (
        weighted
        - jnp.mean(weighted, axis=-1, keepdims=True)
        - scaled * jnp.mean(weighted * scaled, axis=-1, keepdims=True)
    )
    base = base_ref[...] if base_ref.shape[0] == rows else own_rows(base_ref, head, rows)
    total = base.astype(wide) + inv_std * inner
    sum_ref[...] = total
    sums = [
        jnp.sum(upstream * scaled, axis=0, keepdims=True),
        jnp.sum(upstream, axis=0, keepdims=True),
    ]
    coarse = [each.astype(low).astype(wide) for each in sums]
    fine = [each - near for each, near in zip(sums, coarse)]
    extra = low_ref.shape[0] - rows - 4
    blank = jnp.zeros((extra, total.shape[1]), wide)
    low_ref[...] = cat([total, *coarse, *fine, blank], 0).astype(low)


def sums_from(part_refs, sums_ref, shard):
    found = total_of(part_refs, slice(shard, shard + 8))
    sums_ref[...] = found[0:2] + found[2:4]


def attend_back_body(query_ref, *refs):
    heads = lax.axis_size("heads")
    kv_refs, part_refs = refs[:4], refs[4 : 4 + heads]
    piece_refs, _, refs = third_refs(refs[4 + heads :], 7)
    all_ref, d_query_ref, keep_ref, send_ref, sums_ref, d_mixed_ref, hold = refs
    chans = query_ref.shape[1]
    cells = TILE * TILE
    scale = HEAD_DIM ** (-0.5)
    shard = all_ref.shape[0] // heads
    all_ref[...] = whole_rows(part_refs, hold, shard)
    sums_from(part_refs, sums_ref, shard)
    weights = wide_cols(views(piece_refs, 0, heads * chans), 0, chans)
    d_mixed_ref[...] = dot(all_ref[...], weights, (1, 1)).astype(low)
    masks = head_masks(cells)
    for batch in range(query_ref.shape[0] // cells):
        at = slice(batch * cells, (batch + 1) * cells)
        for pair in range(chans // LANES):
            lanes = slice(pair * LANES, (pair + 1) * LANES)
            value_lanes = slice(chans + pair * LANES, chans + (pair + 1) * LANES)
            keys = cat([ref[at, lanes] for ref in kv_refs], 0)
            values = cat([ref[at, value_lanes] for ref in kv_refs], 0)
            query = query_ref[at, lanes]
            d_mixed = d_mixed_ref[at, lanes]
            d_queries = []
            d_keys = 0.0
            d_values = 0.0
            for mask in masks:
                own_query = jnp.where(mask, query, jnp.zeros_like(query))
                own_mixed = jnp.where(mask, d_mixed, jnp.zeros_like(d_mixed))
                probs = softmax_parts(own_query, keys)
                d_probs = dot(own_mixed, values, (1, 1))
                inner = jnp.sum(probs * d_probs, axis=-1, keepdims=True)
                d_scores = (probs * (d_probs - inner)).astype(low)
                d_queries.append(dot(d_scores, keys))
                d_keys = d_keys + dot(d_scores, own_query, (0, 0))
                d_values = d_values + dot(probs.astype(low), own_mixed, (0, 0))
            d_query = jnp.where(masks[0], d_queries[0], d_queries[1]) * scale
            d_query_ref[at, lanes] = d_query.astype(low)
            d_keys = d_keys * scale
            for i in range(4):
                target = (keep_ref, send_ref)[i // 2]
                own = slice(i * cells, (i + 1) * cells)
                target[i % 2, at, lanes] = d_keys[own].astype(target.dtype)
                target[i % 2, at, value_lanes] = d_values[own].astype(target.dtype)


def add_pair_body(keep_ref, got_ref, own_ref, send_ref):
    own_ref[...] = keep_ref[0] + got_ref[0].astype(wide)
    send_ref[...] = (keep_ref[1] + got_ref[1].astype(wide)).astype(low)


def d_qkv_body(d_query_ref, own_ref, got_ref, *refs):
    piece_refs, (d_qkv_ref, *out_refs, total_ref) = rows_of(*refs[:2]), refs[2:]
    chans = d_query_ref.shape[1]
    d_qkv_ref[:, :chans] = d_query_ref[...]
    d_qkv_ref[:, chans:] = (own_ref[...] + got_ref[...].astype(wide)).astype(low)
    d_qkv = d_qkv_ref[...]
    count = 3 * chans // LANES
    piece_refs = views(piece_refs, lax.axis_size("heads") * chans, 3 * chans)
    for pair in range(BLOCKS // 2):
        weights = wide_rows(piece_refs[2 * pair : 2 * pair + 2], 0, count)
        lanes = slice(2 * pair * LANES, 2 * (pair + 1) * LANES)
        total_ref[:, lanes] = dot(d_qkv, weights, (1, 1))
    write_chunks(total_ref, out_refs)


def gate_back_body(gate_ref, spread_ref, *refs):
    heads = lax.axis_size("heads")
    head = lax.axis_index("heads")
    part_refs, piece_refs = refs[:heads], rows_of(*refs[heads : heads + 2])
    all_ref, d_gate_ref, grid_ref, sums_ref, *edge_refs, edge, hold = refs[heads + 2 :]
    shard = all_ref.shape[0] // heads
    all_ref[...] = whole_rows(part_refs, hold, shard)
    sums_from(part_refs, sums_ref, shard)
    chans = gate_ref.shape[1]
    weights = wide_cols(views(piece_refs, 0, heads * chans), 0, chans)
    d_joined = dot(all_ref[...], weights, (1, 1))
    gate = gate_ref[...]
    d_gate_ref[...] = (d_joined * spread_ref[...] * (1.0 - gate * gate)).astype(low)
    grid_ref[...] = d_joined * gate
    send_edges(grid_ref, edge, *edge_refs)


def depthwise_back_body(grid_ref, col_ref, row_ref, corner_ref, dw_ref, out_ref, d_pad, hold, flat):
    fill_padded(grid_ref, col_ref, row_ref, corner_ref, d_pad, hold)
    cells = TILE * TILE
    per_batch = (TILE + 2) * PAD
    chans = grid_ref.shape[1]
    for batch in range(grid_ref.shape[0] // cells):
        for a in range(TILE):
            running = jnp.zeros((TILE, chans), wide)
            for tap in range(9):
                row, col = divmod(tap, 3)
                at = batch * per_batch + (a + 2 - row) * PAD + 2 - col
                running = running + dw_ref[tap : tap + 1] * d_pad[at : at + TILE]
            flat[batch * cells + a * TILE : batch * cells + (a + 1) * TILE] = running
    out_ref[...] = flat[...].astype(low)


def taps_body(grid_ref, pad_ref, ln1_ref, ln2_ref, small_ref):
    cells = TILE * TILE
    per_batch = (TILE + 2) * PAD
    chans = grid_ref.shape[1]
    sums = [jnp.zeros((TILE, chans), wide) for _ in range(10)]
    for batch in range(grid_ref.shape[0] // cells):
        for a in range(TILE):
            own = grid_ref[batch * cells + a * TILE : batch * cells + (a + 1) * TILE]
            for tap in range(9):
                row, col = divmod(tap, 3)
                at = batch * per_batch + (a + row) * PAD + col
                sums[tap] = sums[tap] + own * pad_ref[at : at + TILE]
            sums[9] = sums[9] + own
    small_ref[...] = jnp.zeros(small_ref.shape, wide)
    for place in range(BLOCKS):
        lanes = slice(place * LANES, (place + 1) * LANES)
        to = pl.ds(pl.multiple_of(LANES * block_at(place), LANES), LANES)
        small_ref[0:2, to] = ln1_ref[:, lanes]
        small_ref[2:4, to] = ln2_ref[:, lanes]
    per_row = small_ref.shape[1] // chans
    for tap in range(10):
        row, lane = 4 + tap // per_row, tap % per_row * chans
        total = jnp.sum(sums[tap], axis=0, keepdims=True)
        small_ref[row : row + 1, lane : lane + chans] = total


def small_final_body(own_ref, got_ref, ln1_ref, ln2_ref, taps_ref):
    total = own_ref[...] + got_ref[...]
    ln1_ref[...] = total[0:2]
    ln2_ref[...] = total[2:4]
    chans = taps_ref.shape[1]
    per_row = total.shape[1] // chans
    for tap in range(10):
        row, lane = 4 + tap // per_row, tap % per_row * chans
        taps_ref[tap : tap + 1] = total[row : row + 1, lane : lane + chans]


def conv_back_body(pool_ref, whole_ref, *refs):
    heads = lax.axis_size("heads")
    head = lax.axis_index("heads")
    part_refs, (hires_ref,) = refs[:heads], refs[heads:]
    per_chunk = BLOCKS // heads
    d_pooled = 0.0
    for j, ref in enumerate(part_refs):
        first = per_chunk * (head ^ j)
        chunk = cat([whole_ref[first + i] for i in range(per_chunk)], 1)
        d_pooled = d_pooled + dot(ref[...], chunk, (1, 1))
    d_pooled = d_pooled.astype(low)
    batches = pool_ref.shape[0]
    rows = pool_ref.shape[1]
    for batch in range(batches):
        own = d_pooled[batch * rows : (batch + 1) * rows]
        hires_ref[batch] = dot(pool_ref[batch], own, (0, 0))


def conv_grad_body(pooled_ref, *refs):
    heads = lax.axis_size("heads")
    head = lax.axis_index("heads")
    part_refs, (keep_ref, send_ref, hold) = refs[:heads], refs[heads + 2 :]
    per_chunk = BLOCKS // heads
    for j, ref in enumerate(part_refs):
        grad = dot(pooled_ref[...], ref[...], (0, 0)).astype(low)
        for i in range(per_chunk):
            hold[per_chunk * (head ^ j) + i] = grad[:, i * LANES : (i + 1) * LANES]
    for place in range(BLOCKS):
        target = place_refs(keep_ref, send_ref, place)
        target[0 : hold.shape[1]] = hold[block_at(place)]


def place_refs(keep_ref, send_ref, place):
    return ((keep_ref, send_ref)[place // 4]).at[place % 4]


def row_grad(left_ref, right, keep_ref, send_ref, start):
    count = right.shape[1] // LANES
    for place in range(BLOCKS):
        lanes = slice(place * LANES, (place + 1) * LANES)
        grad = dot(left_ref[:, lanes], right, (0, 0)).astype(low)
        target = place_refs(keep_ref, send_ref, place)
        for m in range(count):
            target[start + m * LANES : start + (m + 1) * LANES] = grad[
                :, m * LANES : (m + 1) * LANES
            ]


def col_grad(left_ref, right_ref, keep_ref, send_ref, start):
    width = left_ref.shape[1]
    for m in range(width // LANES):
        grad = dot(left_ref[:, m * LANES : (m + 1) * LANES], right_ref[...], (0, 0)).astype(low)
        for place in range(BLOCKS):
            target = place_refs(keep_ref, send_ref, place)
            target[start + m * LANES : start + (m + 1) * LANES] = grad[
                :, place * LANES : (place + 1) * LANES
            ]


def pair_grad_body(row_left, row_right, col_left, col_right, keep_ref, send_ref):
    width = row_right.shape[1]
    start = keep_ref.shape[1] - width - col_left.shape[1]
    row_grad(row_left, row_right[...], keep_ref, send_ref, start)
    col_grad(col_left, col_right, keep_ref, send_ref, start + width)


def final_rows(refs, start, count):
    return cat(
        [total_of(refs, slice(start + m * LANES, start + (m + 1) * LANES)) for m in range(count)],
        1,
    )


def first_final_body(*refs):
    part_refs, (conv_ref, gate_ref, join_ref) = refs[:-3], refs[-3:]
    rows, chans = conv_ref.shape[0], gate_ref.shape[1]
    conv_ref[...] = total_of(part_refs, slice(0, rows))
    gate_ref[...] = final_rows(part_refs, rows, chans // LANES)
    join_ref[...] = total_of(part_refs, slice(rows + chans, rows + 2 * chans))


def up_down_final_body(*refs):
    part_refs, (up_ref, down_ref) = refs[:-2], refs[-2:]
    width = up_ref.shape[1]
    up_ref[...] = final_rows(part_refs, 0, width // LANES)
    down_ref[...] = total_of(part_refs, slice(width, width + down_ref.shape[0]))


def attn_proj_final_body(*refs):
    part_refs, (attn_ref, out_ref) = refs[:-2], refs[-2:]
    chans = attn_ref.shape[2]
    for s in range(3):
        attn_ref[s] = final_rows(part_refs, s * chans, chans // LANES)
    out_ref[...] = total_of(part_refs, slice(3 * chans, 3 * chans + out_ref.shape[0]))


def unpack_rows(packed, count):
    places = packed.shape[0]
    return (
        packed.reshape(places, count, LANES, LANES)
        .transpose(0, 2, 1, 3)
        .reshape(places * LANES, count * LANES)
    )


def unpack_cols(packed):
    return packed.transpose(1, 0, 2).reshape(packed.shape[1], -1)


def pack_rows(weights):
    count = weights.shape[1] // LANES
    return (
        weights.reshape(BLOCKS, LANES, count, LANES)
        .transpose(0, 2, 1, 3)
        .reshape(BLOCKS, count * LANES, LANES)
    )


def pack_cols(weights):
    return weights.reshape(weights.shape[0], BLOCKS, LANES).transpose(1, 0, 2)


def scatter_dim(grad, axis):
    return lax.psum_scatter(grad, "tiles", scatter_dimension=axis, tiled=True).astype(wide)


def local(
    vit_tokens,
    hires_maps,
    map_sizes,
    out_grad,
    ln_gain,
    ln_bias,
    dw_params,
    conv_w,
    gate_w,
    join_w,
    attn_in_w,
    out_w,
    up_w,
    down_w,
):
    tiles = lax.axis_size("tiles")
    heads = lax.axis_size("heads")
    fast = fast_tiles()
    batches, rows, width = vit_tokens.shape
    total = batches * rows
    shard = total // heads
    chans = dw_params.shape[1]
    hidden_width = down_w.shape[0]
    pixels, hires_chans = hires_maps.shape[1:]
    dma = pltpu.SemaphoreType.DMA

    cross = heads * chans
    lanes_of = chans // LANES
    if fast:
        first_own, cross_own = run_kernel(
            pack_first_body,
            [shape((hires_chans + chans, LANES)), shape((3 * chans, LANES))],
            conv_w,
            gate_w,
            join_w,
            out_w,
            scratch=[((), dma((3 + 2 * lanes_of,)))],
            fetch=True,
        )
        first_pieces = gather_first(first_own)
        cross_parts = gather_heads(after(cross_own, first_pieces[4]))
        second_own, third_own = run_kernel(
            pack_rest_body,
            [
                shape((cross + 3 * chans, LANES)),
                shape((2 * cross - chans + 2 * hidden_width, LANES)),
            ],
            attn_in_w,
            up_w,
            down_w,
            *cross_parts,
            scratch=[((), dma((3 * heads + 3 * lanes_of + hidden_width // LANES,)))],
            fetch=True,
        )
    else:

        def whole_of(weights, axis):
            return lax.all_gather(weights, "tiles", axis=axis, tiled=True)

        def halves(*packed):
            joint = jnp.concatenate(packed, axis=1)
            return joint[: BLOCKS // 2], joint[BLOCKS // 2 :]

        gate_all = [pack_rows(each) for each in gather_heads(whole_of(gate_w, 0))]
        join_all = [pack_cols(each) for each in gather_heads(whole_of(join_w, 1))]
        out_all = [pack_cols(each) for each in gather_heads(whole_of(out_w, 1))]
        attn_whole = whole_of(attn_in_w, 1)
        first_stack = jnp.concatenate([pack_cols(whole_of(conv_w, 1)), gate_all[0]], axis=1)
        first_pieces = [first_stack[p] for p in range(BLOCKS)]
        second = halves(*join_all, *[pack_rows(each) for each in attn_whole])
        third = halves(
            *out_all,
            *gate_all[1:],
            pack_rows(whole_of(up_w, 0)),
            pack_cols(whole_of(down_w, 1)),
        )

    inputs = (
        vit_tokens.reshape(total, width),
        out_grad.reshape(total, width),
        ln_gain,
        ln_bias,
    )
    tokens, upstream, gains, biases = run_kernel(
        relative_body,
        [shape(each.shape, each.dtype) for each in inputs],
        *inputs,
        scratch=[(each.shape, each.dtype) for each in inputs] + [((), dma((4,)))],
        fetch=True,
    )
    upstream_wide = upstream.astype(wide)

    pooled, pools = pl.pallas_call(
        pool_body,
        out_shape=(shape((total, hires_chans)), shape((batches, rows, pixels))),
        in_specs=[
            pl.BlockSpec(memory_space=pltpu.SMEM),
            pl.BlockSpec(memory_space=pl.ANY),
        ],
        out_specs=tuple([pl.BlockSpec(memory_space=pltpu.VMEM)] * 2),
        scratch_shapes=[pltpu.VMEM(hires_maps.shape, low), dma((1,))],
        compiler_params=pltpu.CompilerParams(vmem_limit_bytes=VMEM_LIMIT),
    )(map_sizes, hires_maps)
    conv_whole, *conv_parts = run_kernel(
        conv_body,
        [shape((BLOCKS, hires_chans, LANES))] + [shape((total, chans))] * heads,
        after(pooled, tokens, *(cross_parts[1:] if fast else [])),
        *first_pieces,
        flops=2 * total * hires_chans * width,
    )
    edge_shapes = [
        shape((batches * TILE, chans)),
        shape((batches * PAD, chans)),
        shape((PAD, chans)),
    ]
    edge_scratch = ((batches * PAD, chans), wide)
    grid_scratch = ((total, chans), wide)
    pad_dims = (batches * (TILE + 2) * PAD, chans)
    own_part, *other_parts = scatter_heads(conv_parts)
    mapped, *edges = run_kernel(
        map_body,
        [shape((total, chans))] + edge_shapes,
        own_part,
        *other_parts,
        scratch=[grid_scratch, edge_scratch],
    )

    def swap_edges(col, row, corner):
        return over_core(col), over_x(row), swap_with(corner, "tiles", 3)

    edges = swap_edges(*edges)
    if fast:
        second_own = after(second_own, other_parts[0])
        from_x, from_y = over_x(second_own), over_y(second_own)
        upper = over_y(after(from_x[:cross], mapped))
        lower = over_x(after(from_y[cross:], mapped))
        (second_stack,) = run_kernel(
            stack_corner_body,
            [shape((4, *second_own.shape))],
            second_own,
            from_x,
            from_y,
            upper,
            lower,
        )
        second = (second_stack, over_core(second_stack))

    (gate,) = run_kernel(
        gate_body,
        [shape((total, chans), wide)],
        tokens,
        *first_pieces,
        flops=2 * total * chans * width,
    )
    chunk_shapes = [shape((shard, width))] * heads
    padded, spread, joined = run_kernel(
        depthwise_body,
        [shape(pad_dims, wide), shape((total, chans), wide), shape((total, chans))],
        mapped,
        *edges,
        dw_params,
        gate,
        scratch=[grid_scratch, edge_scratch],
    )

    joined_parts = gather_heads(joined)
    wide_rows_shape = shape((total, width), wide)
    first, normed1, query, kv_own = run_kernel(
        join_body,
        [
            wide_rows_shape,
            shape((total, width)),
            shape((total, chans)),
            shape((total, 2 * chans)),
        ],
        tokens,
        gains,
        biases,
        *joined_parts,
        *second,
        flops=2 * total * width * (width + 3 * chans),
    )
    kv_x = over_x(kv_own)
    kv_all = [kv_own, kv_x, over_core(kv_own), over_core(kv_x)]
    if fast:
        third_own = after(third_own, joined_parts[-1])
        from_x, from_y = over_x(third_own), over_y(third_own)
        cut = 2 * cross - chans
        third_stack = stacked(third_own, from_x, from_y)
    (mixed,) = run_kernel(
        attend_body,
        [shape((total, chans))],
        query,
        *kv_all,
        flops=8 * total * 4 * rows * chans,
    )
    if fast:
        upper = over_y(after(from_x[:cut], kv_x))
        lower = over_x(after(from_y[cut:], kv_x))
        third_core = over_core(after(third_stack, kv_all[3]))
        mixed_parts = gather_heads(after(mixed, third_core))
        third = (third_stack, upper, lower, third_core)
        third += tuple(over_core(after(part, *mixed_parts[1:])) for part in (upper, lower))
    else:
        mixed_parts = gather_heads(mixed)

    wide_shape = shape((total, hidden_width))
    total_scratch = ((total, width), wide)
    second_rows, normed2, hidden, d_hidden, *ffn_parts = run_kernel(
        ffn_body,
        [wide_rows_shape, shape((total, width)), wide_shape, wide_shape] + chunk_shapes,
        upstream,
        first,
        gains,
        biases,
        *mixed_parts,
        *third,
        scratch=[total_scratch],
        flops=2 * total * width * (width + 3 * hidden_width),
    )
    back_shapes = [shape((shard, width), wide), shape((shard + 8, width))]
    d_second, d_attn_own = run_kernel(
        norm_back_body, back_shapes, second_rows, upstream_wide, gains[1:2], *scatter_heads(ffn_parts)
    )
    d_attn_parts = gather_heads(d_attn_own)
    ud_keep, ud_send = run_kernel(
        pair_grad_body,
        [shape((4, 2 * hidden_width, LANES))] * 2,
        after(normed2, d_attn_parts[1]),
        d_hidden,
        hidden,
        upstream,
        flops=4 * total * hidden_width * width,
    )

    d_attn, d_query, kv_keep, kv_send, ln2_sums = run_kernel(
        attend_back_body,
        [
            shape((total, width)),
            shape((total, chans)),
            shape((2, total, 2 * chans), wide),
            shape((2, total, 2 * chans)),
            shape((2, width), wide),
        ],
        query,
        *kv_all,
        *d_attn_parts,
        *third,
        scratch=[((total, chans), low), total_scratch],
        flops=2 * total * chans * width + 20 * total * 4 * rows * chans,
    )
    kv_got = over_core(kv_send)
    kv_mine, kv_over = run_kernel(
        add_pair_body,
        [shape((total, 2 * chans), wide), shape((total, 2 * chans))],
        kv_keep,
        kv_got,
    )
    kv_back = over_x(kv_over)
    down_parts = run_kernel(
        down_body,
        chunk_shapes,
        after(hidden, kv_got),
        *third,
        scratch=[total_scratch],
        flops=2 * total * hidden_width * width,
    )
    down_parts = scatter_heads(down_parts)
    (result_own,) = run_kernel(whole_cols_body, [shape((shard, width))], second_rows, *down_parts)
    if fast:
        ud_parts = add_cores(ud_keep, over_core(after(ud_send, kv_got)))
    d_qkv, *qkv_parts = run_kernel(
        d_qkv_body,
        [shape((total, 3 * chans))] + chunk_shapes,
        after(d_query, *down_parts),
        kv_mine,
        kv_back,
        *second,
        scratch=[total_scratch],
        flops=6 * total * chans * width,
    )
    if fast:
        ud_x = over_x(after(ud_parts[1], d_qkv))
        ud_y = over_y(after(ud_parts[2], d_qkv))
    else:
        ud_sums = jnp.concatenate([ud_keep, ud_send], axis=0)
    d_first, d_join_own = run_kernel(
        norm_back_body,
        back_shapes,
        first,
        after(d_second, *([ud_x, ud_y] if fast else [])),
        gains[0:1],
        *scatter_heads(qkv_parts),
    )
    d_join_parts = gather_heads(d_join_own)
    ap_keep, ap_send = run_kernel(
        pair_grad_body,
        [shape((4, 4 * chans, LANES))] * 2,
        after(normed1, d_join_parts[1]),
        d_qkv,
        mixed,
        d_attn,
        flops=8 * total * chans * width,
    )

    if fast:
        ud_corner = over_corner(after(ud_parts[3], d_join_own))
        ud_sums = [ud_parts[0], ud_x, ud_y, ud_corner]

    d_join, d_gate_in, d_grid, ln1_sums, *edges = run_kernel(
        gate_back_body,
        [
            shape((total, width)),
            shape((total, chans)),
            shape((total, chans), wide),
            shape((2, width), wide),
        ]
        + edge_shapes,
        gate,
        spread,
        after(d_join_parts[0], *([ud_corner] if fast else [])),
        *d_join_parts[1:],
        *second,
        scratch=[edge_scratch, total_scratch],
        flops=2 * total * chans * width,
    )
    edges = swap_edges(*edges)
    d_gate_parts = gather_heads(d_gate_in)
    (small,) = run_kernel(
        taps_body, [shape((8, width), wide)], d_grid, padded, ln1_sums, ln2_sums
    )
    small = small + over_core(small)
    (d_mapped,) = run_kernel(
        depthwise_back_body,
        [shape((total, chans))],
        d_grid,
        *edges,
        dw_params,
        scratch=[(pad_dims, wide), edge_scratch, grid_scratch],
    )
    d_mapped_parts = gather_heads(d_mapped)
    if fast:
        ap_parts = add_cores(ap_keep, over_core(after(ap_send, d_grid)))
        ap_x = over_x(after(ap_parts[1], d_mapped_parts[-1]))
        ap_y = over_y(after(ap_parts[2], d_mapped_parts[-1]))
        ap_sums = [ap_parts[0], ap_x, ap_y, over_corner(after(ap_parts[3], ap_x, ap_y))]
    else:
        ap_sums = jnp.concatenate([ap_keep, ap_send], axis=0)
    bit = 2
    while bit < tiles // 2:
        small = small + swap_with(after(small, d_mapped), "tiles", bit)
        bit *= 2
    first_shape = shape((4, hires_chans + 2 * chans, LANES))
    first_keep, first_send = run_kernel(
        pair_grad_body,
        [first_shape] * 2,
        after(tokens, d_mapped_parts[1]),
        d_gate_in,
        joined,
        d_join,
        flops=4 * total * chans * width,
    )
    first_keep, first_send = run_kernel(
        conv_grad_body,
        [first_shape] * 2,
        after(pooled, small, *(ap_sums[1:3] if fast else [])),
        *d_mapped_parts,
        first_keep,
        first_send,
        scratch=[((BLOCKS, hires_chans, LANES), low)],
        flops=2 * total * hires_chans * width,
        alias={heads + 1: 0, heads + 2: 1},
    )
    if fast:
        first_got = over_core(first_send)
        first_parts = add_cores(after(first_keep, ap_sums[3]), first_got)
        first_sums = [
            first_parts[0],
            over_x(first_parts[1]),
            over_y(first_parts[2]),
            over_corner(first_parts[3]),
        ]
    else:
        first_got = first_send
        first_sums = jnp.concatenate([first_keep, first_send], axis=0)
    (hires_grad,) = run_kernel(
        conv_back_body,
        [shape((batches, pixels, hires_chans), wide)],
        pools,
        conv_whole,
        *d_mapped_parts,
        flops=2 * total * hires_chans * width + 2 * total * pixels * hires_chans,
        leave=True,
    )
    (tokens_grad,) = run_kernel(
        tokens_grad_body,
        [shape((total, width), wide)],
        d_join,
        *d_gate_parts,
        *first_pieces,
        *third,
        flops=2 * total * width * width,
        leave=True,
    )
    (block_out,) = run_kernel(
        block_out_body,
        [shape((total, width))],
        *gather_heads(after(result_own, first_send)),
        scratch=[total_scratch],
        leave=True,
    )

    ln1_grad, ln2_grad, taps_grad = run_kernel(
        small_final_body,
        [shape((2, width), wide), shape((2, width), wide), shape(dw_params.shape, wide)],
        small,
        swap_with(after(small, first_send), "tiles", bit),
        leave=True,
    )

    if fast:
        up_grad, down_grad = run_kernel(
            up_down_final_body,
            [shape(up_w.shape, wide), shape(down_w.shape, wide)],
            *ud_sums,
            leave=True,
        )
        attn_grad, out_w_grad = run_kernel(
            attn_proj_final_body,
            [shape(attn_in_w.shape, wide), shape(out_w.shape, wide)],
            *ap_sums,
            leave=True,
        )
        first_sums[0] = after(
            first_sums[0], hires_grad, up_grad, down_grad, attn_grad, out_w_grad
        )
        conv_grad, gate_grad, join_grad = run_kernel(
            first_final_body,
            [shape(conv_w.shape, wide), shape(gate_w.shape, wide), shape(join_w.shape, wide)],
            *first_sums,
            leave=True,
        )
    else:
        count = chans // LANES
        at = hires_chans
        conv_grad = scatter_dim(unpack_cols(first_sums[:, :at]), 1)
        gate_grad = scatter_dim(unpack_rows(first_sums[:, at : at + chans], count), 0)
        join_grad = scatter_dim(unpack_cols(first_sums[:, at + chans :]), 1)
        attn_grad = jnp.stack(
            [
                scatter_dim(unpack_rows(ap_sums[:, s * chans : (s + 1) * chans], count), 0)
                for s in range(3)
            ]
        )
        out_w_grad = scatter_dim(unpack_cols(ap_sums[:, 3 * chans :]), 1)
        up_grad = scatter_dim(unpack_rows(ud_sums[:, :hidden_width], hidden_width // LANES), 0)
        down_grad = scatter_dim(unpack_cols(ud_sums[:, hidden_width:]), 1)

    return (
        block_out.reshape(batches, rows, width),
        tokens_grad.reshape(batches, rows, width),
        hires_grad,
        ln1_grad,
        ln2_grad,
        taps_grad,
        conv_grad,
        gate_grad,
        join_grad,
        attn_grad,
        out_w_grad,
        up_grad,
        down_grad,
    )


def solution(mesh):
    placed = (
        P(None, "tiles", None),
        P(None, "tiles", "heads"),
        P(),
        P(None, "tiles", None),
        P(),
        P(),
        P(None, "heads"),
        P("heads", "tiles"),
        P("tiles", "heads"),
        P("heads", "tiles"),
        P(None, "tiles", "heads"),
        P("heads", "tiles"),
        P("tiles", "heads"),
        P("heads", "tiles"),
    )
    return jax.shard_map(
        local,
        mesh=mesh,
        in_specs=placed,
        out_specs=(
            P(None, "tiles", None),
            P(None, "tiles", None),
            P(None, "tiles", "heads"),
            P(),
            P(),
            P(None, "heads"),
            P("heads", "tiles"),
            P("tiles", "heads"),
            P("heads", "tiles"),
            P(None, "tiles", "heads"),
            P("heads", "tiles"),
            P("tiles", "heads"),
            P("heads", "tiles"),
        ),
        check_vma=False,
    )
```

```python
import jax
import jax.numpy as jnp
from jax import lax
from jax.experimental import pallas as pl
from jax.experimental.pallas import tpu as pltpu
from jax.sharding import PartitionSpec as P

HEAD_DIM = 64
GRID = 24
TILE = 12
HR_TILE = 24
PAD = 16
LANES = 128

norm_eps = 1e-05
inv_root_two = 0.7071067811865476
inv_root_two_pi = 0.3989422804014327

low = jnp.bfloat16
wide = jnp.float32
VMEM_LIMIT = 24 * 1024 * 1024


STARTS = {
    "cross": "first_own_core",
    "second_x": "conv",
    "second_y": "conv",
    "second_corner": "map",
    "second_stack": "joined3",
    "third_y": "joined3",
    "upper": "kv_x",
    "lower": "join",
    "third_core": "kv_core",
    "mixed": "third_core",
    "upper_core": "second_core",
    "lower_core": "mixed2",
    "fourth_y": "ffn",
    "ud_kernel": "d_attn2",
    "fourth_stack": "kv_got",
    "ud_core": "kv_got",
    "ud_x": "down2",
    "ud_y": "d_qkv",
    "ap_kernel": "d_join1",
    "ud_corner": "qkv_z3",
    "ap_core": "gate_back",
    "small2": "d_mapped3",
    "tail": "small1",
    "first_kernel": "d_mapped1",
    "small_last": "conv_grad",
    "small1": "d_mapped3",
    "fourth_core": "attend_back",
    "conv_z": "cross3",
    "down1": "kv_got",
    "last_y": "first_own_core",
    "fourth_corner": "ffn_z3",
    "cross1": "first_own_core",
    "tail3": "conv_grad",
    "taps": "cross1",
}
FINISHES = {
    "cross1": "map",
    "cross3": "conv",
    "fourth_x": "norm2",
    "fourth_y": "norm2",
    "fourth_corner": "attend_back",
    "ud_kernel": "attend_back",
    "down_kernel": "attend_back",
    "down1": "d_qkv",
    "down2": "d_qkv",
    "down3": "d_qkv",
    "fourth_core": "d_qkv",
    "ud_x": "norm3",
    "ud_y": "norm3",
    "ud_corner": "gate_back",
    "small2": "conv_grad",
    "up_down": "conv_grad",
    "hires": "last_y",
    "d_mapped1": "dw_back",
    "small_last": "add_first",
    "block": "add_first",
    "d_attn1": "add_pair",
    "upper": "last_y",
    "mixed3": "last_y",
}
TURNS = {
    "ffn_z": (3, 1, 2),
    "d_attn": (1, 2, 3),
    "mixed": (2, 1, 3),
}


def shape(dims, kind=low):
    return jax.ShapeDtypeStruct(tuple(dims), kind)


def after(value, *others):
    return lax.optimization_barrier((value, *others))[0]


class Plan:
    def __init__(self, starts, finishes, turns):
        self.starts, self.finishes, self.turns = starts, finishes, turns
        self.events, self.held = {}, {}

    def mark(self, name, value):
        self.events[name] = value
        return value

    def start(self, name, value):
        event = self.events.get(self.starts.get(name))
        return value if event is None else after(value, event)

    def finish(self, name, value):
        self.mark(name, value)
        self.held.setdefault(self.finishes.get(name), []).append(value)
        return value

    def enter(self, name, value):
        held = self.held.pop(name, ())
        return after(value, *held) if held else value

    def over_heads(self, name, parts):
        count = len(parts)
        found = [parts[0]] * count
        for j in self.turns.get(name, range(1, count)):
            sent = self.start(name + str(j), self.start(name, parts[j]))
            found[j] = self.finish(name + str(j), swap_with(sent, "heads", j))
        return found

    def gather(self, name, own):
        return self.over_heads(name, [own] * lax.axis_size("heads"))


def run_kernel(body, outs, *args, scratch=(), flops=0, leave=False, fetch=False, alias=None):
    whole = pl.BlockSpec(memory_space=pltpu.VMEM)
    source = pl.BlockSpec(memory_space=pltpu.HBM) if fetch else whole
    target = pl.BlockSpec() if leave else whole
    if fetch:
        args = [pltpu.with_memory_space_constraint(arg, pltpu.HBM) for arg in args]
    traffic = sum(a.size * a.dtype.itemsize for a in args)
    traffic += sum(o.size * o.dtype.itemsize for o in outs)
    return pl.pallas_call(
        body,
        name=body.__name__,
        out_shape=tuple(outs),
        in_specs=[source] * len(args),
        out_specs=tuple([target] * len(outs)),
        scratch_shapes=[pltpu.VMEM(dims, kind) if dims else kind for dims, kind in scratch],
        input_output_aliases=alias or {},
        cost_estimate=pl.CostEstimate(flops=1, bytes_accessed=1, transcendentals=0),
        compiler_params=pltpu.CompilerParams(vmem_limit_bytes=VMEM_LIMIT),
    )(*args)


def dot(left, right, contract=(1, 0)):
    return lax.dot_general(
        left, right, (((contract[0],), (contract[1],)), ((), ())), preferred_element_type=wide
    )


def cat(parts, axis):
    return parts[0] if len(parts) == 1 else jnp.concatenate(parts, axis=axis)


def swap_with(value, axis, mask):
    pairs = [(source, source ^ mask) for source in range(lax.axis_size(axis))]
    return lax.ppermute(value, axis, pairs)


def over_core(value):
    return swap_with(value, "tiles", 1)


def over_x(value):
    return swap_with(value, "tiles", 2)


def over_y(value):
    return swap_with(value, "tiles", 4)


def fast_tiles():
    return lax.axis_size("tiles") == 8


BLOCKS = 8


def place_mask(place):
    half = BLOCKS // 2
    return ((place % half) * 2) | (place // half)


def block_at(place):
    if fast_tiles():
        return lax.axis_index("tiles") ^ place_mask(place)
    return place


def gather_first(block):
    found = [block, over_x(block), over_y(block), swap_with(block, "tiles", 6)]
    return found + [over_core(part) for part in found]


def stack_body(*refs):
    for i, ref in enumerate(refs[:-1]):
        refs[-1][i] = ref[...]


def stacked(*parts):
    return run_kernel(stack_body, [shape((len(parts), *parts[0].shape))], *parts)[0]


def stack_corner_body(*refs):
    *part_refs, upper_ref, lower_ref, out_ref = refs
    for i, ref in enumerate(part_refs):
        out_ref[i] = ref[...]
    cut = upper_ref.shape[0]
    out_ref[len(part_refs), 0:cut] = upper_ref[...]
    out_ref[len(part_refs), cut:] = lower_ref[...]


def rows_of(*stacks):
    return [ref.at[i] for ref in stacks for i in range(ref.shape[0])]


def gather_heads(own):
    return [own] + [swap_with(own, "heads", j) for j in range(1, lax.axis_size("heads"))]


def add_rows_body(keep_ref, got_ref, *out_refs):
    for i, out_ref in enumerate(out_refs):
        total = keep_ref[i].astype(wide) + got_ref[i].astype(wide)
        out_ref[...] = total.astype(out_ref.dtype)


def add_first_body(keep_ref, got_ref, *refs):
    more_refs, out_refs = refs[:3], refs[3:]
    rows = keep_ref.shape[1]
    for i, out_ref in enumerate(out_refs):
        total = keep_ref[i].astype(wide) + got_ref[i].astype(wide)
        out_ref[0:rows] = total.astype(out_ref.dtype)
        if i:
            out_ref[rows:] = more_refs[i - 1][...]


def add_cores(keep, got):
    return run_kernel(add_rows_body, [shape(keep.shape[1:])] * 4, keep, got)


def over_corner(value):
    return swap_with(value, "tiles", 6)


def gelu_parts(inputs):
    bell = 0.5 * (1.0 + lax.erf(inputs * inv_root_two))
    return inputs * bell, bell + inputs * inv_root_two_pi * jnp.exp(-0.5 * inputs * inputs)


def normed(values):
    centred = values - jnp.mean(values, axis=-1, keepdims=True)
    inv_std = lax.rsqrt(jnp.mean(centred * centred, axis=-1, keepdims=True) + norm_eps)
    return centred * inv_std, inv_std


def total_of(refs, at=Ellipsis):
    total = refs[0][at].astype(wide)
    for ref in refs[1:]:
        total = total + ref[at].astype(wide)
    return total


def copies(pairs, sems):
    started = [
        pltpu.make_async_copy(source, target, sems.at[i])
        for i, (source, target) in enumerate(pairs)
    ]
    for copy in started:
        copy.start()
    for copy in started:
        copy.wait()


def lane_blocks(source, target, start):
    rows, lanes = source.shape
    return [
        (
            source.at[:, pl.ds(m * LANES, LANES)],
            target.at[pl.ds(start + m * rows, rows)],
        )
        for m in range(lanes // LANES)
    ]


def pack_first_body(conv_ref, gate_ref, join_ref, out_w_ref, first_ref, cross_ref, sems):
    at = conv_ref.shape[0]
    pairs = [(conv_ref, first_ref.at[pl.ds(0, at)])]
    pairs += lane_blocks(gate_ref, first_ref, at)
    pairs += lane_blocks(gate_ref, cross_ref, 0)
    rows = join_ref.shape[0]
    pairs += [(join_ref, cross_ref.at[pl.ds(rows, rows)])]
    pairs += [(out_w_ref, cross_ref.at[pl.ds(2 * rows, rows)])]
    copies(pairs, sems)


def pack_rest_body(attn_ref, up_ref, down_ref, *refs):
    cross_refs, (second_ref, third_ref, fourth_ref, sems) = refs[:-4], refs[-4:]
    rows = cross_refs[0].shape[0] // 3
    heads = len(cross_refs)
    pairs = []
    for j, ref in enumerate(cross_refs):
        pairs += [(ref.at[pl.ds(rows, rows)], second_ref.at[pl.ds(j * rows, rows)])]
        pairs += [(ref.at[pl.ds(2 * rows, rows)], third_ref.at[pl.ds(j * rows, rows)])]
        if j:
            at = (j - 1) * rows
            pairs += [(ref.at[pl.ds(0, rows)], fourth_ref.at[pl.ds(at, rows)])]
    for s in range(3):
        pairs += lane_blocks(attn_ref.at[s], second_ref, (heads + s) * rows)
    pairs += lane_blocks(up_ref, third_ref, heads * rows)
    rows = down_ref.shape[0]
    pairs += [(down_ref, third_ref.at[pl.ds(third_ref.shape[0] - rows, rows)])]
    copies(pairs, sems)


def third_refs(refs, results):
    count = len(refs) - results
    if count == 2:
        pieces = rows_of(*refs[:2])
        return pieces, pieces, refs[2:]
    stack, upper, lower, core_stack, core_upper, core_lower = refs[:6]
    own, core = rows_of(stack), rows_of(core_stack)
    return own + [upper] + core + [core_upper], own + [lower] + core + [core_lower], refs[6:]


def views(refs, start, rows):
    return [ref if ref.shape[0] == rows else ref.at[pl.ds(start, rows)] for ref in refs]


def whole_number(value, parts):
    return jnp.floor((value + 0.5) * (1.0 / parts))


def pool_body(sides_ref, maps_ref, pooled_ref, pool_ref, hold, sems):
    copy = pltpu.make_async_copy(maps_ref, hold, sems.at[0])
    copy.start()
    image = lax.axis_index("tiles") // 4
    cells, pixels = pool_ref.shape[1:]
    cell = lax.broadcasted_iota(jnp.int32, (cells, pixels), 0).astype(wide)
    pixel = lax.broadcasted_iota(jnp.int32, (cells, pixels), 1).astype(wide)
    cell_row = whole_number(cell, TILE)
    pixel_row = whole_number(pixel, HR_TILE)
    spots = (
        (cell_row, pixel_row),
        (cell - TILE * cell_row, pixel - HR_TILE * pixel_row),
    )
    for batch in range(pool_ref.shape[0]):
        side = sides_ref[batch, image].astype(wide)
        weights = 1.0
        for cell_at, pixel_at in spots:
            begin = whole_number(cell_at * side, GRID)
            end = whole_number((cell_at + 1.0) * side + (GRID - 1.0), GRID)
            inside = jnp.logical_and(pixel_at >= begin, pixel_at < end)
            weights = weights * jnp.where(inside, 1.0 / (end - begin), 0.0)
        pool_ref[batch] = weights.astype(low)
    copy.wait()
    for batch in range(pool_ref.shape[0]):
        pooled = dot(pool_ref[batch], hold[batch])
        pooled_ref[batch * cells : (batch + 1) * cells] = pooled.astype(low)


def wide_rows(refs, start, count):
    return cat(
        [
            cat([ref[start + m * LANES : start + (m + 1) * LANES] for m in range(count)], 1)
            for ref in refs
        ],
        0,
    )


def wide_cols(refs, start, rows):
    return cat([ref[start : start + rows] for ref in refs], 1)


def relative_body(*refs):
    count = len(refs[:-1]) // 3
    sources, outs, found = refs[:count], refs[count : 2 * count], refs[2 * count : -1]
    copies(list(zip(sources, found)), refs[-1])
    for source, target in zip(found, outs):
        for place in range(BLOCKS):
            lanes = pl.ds(pl.multiple_of(LANES * block_at(place), LANES), LANES)
            target[:, place * LANES : (place + 1) * LANES] = source[:, lanes]


def conv_body(pooled_ref, *refs):
    piece_refs, (whole_ref, *out_refs) = refs[:BLOCKS], refs[BLOCKS:]
    head = lax.axis_index("heads")
    for place, ref in enumerate(piece_refs):
        whole_ref[block_at(place)] = ref[0 : whole_ref.shape[1]]
    per_chunk = BLOCKS // len(out_refs)
    for j, out_ref in enumerate(out_refs):
        first = per_chunk * (head ^ j)
        chunk = cat([whole_ref[first + i] for i in range(per_chunk)], 1)
        out_ref[...] = dot(pooled_ref[...], chunk).astype(low)


def edge_flags():
    tile = lax.axis_index("tiles")
    return (tile & 1) == 0, (tile & 2) == 0


def send_edges(grid, hold_ref, col_ref, row_ref, corner_ref):
    right, lower = edge_flags()
    cells = TILE * TILE
    batches = grid.shape[0] // cells
    count = batches * TILE
    for at in range(count):
        begin = at * TILE
        end = begin + TILE - 1
        hold_ref[at : at + 1] = jnp.where(right, grid[end : end + 1], grid[begin : begin + 1])
    col_ref[...] = hold_ref[0:count].astype(low)
    hold_ref[...] = jnp.zeros(hold_ref.shape, wide)
    for batch in range(batches):
        base = batch * cells
        bottom = grid[base + cells - TILE : base + cells]
        top = grid[base : base + TILE]
        edge = jnp.where(lower, bottom, top)
        hold_ref[batch * PAD : batch * PAD + TILE] = edge
    row_ref[...] = hold_ref[...].astype(low)
    hold_ref[...] = jnp.zeros(hold_ref.shape, wide)
    for batch in range(batches):
        base = batch * cells
        ends = [
            jnp.where(right, grid[at + TILE - 1 : at + TILE], grid[at : at + 1])
            for at in (base + cells - TILE, base)
        ]
        hold_ref[batch : batch + 1] = jnp.where(lower, ends[0], ends[1])
    corner_ref[...] = hold_ref[0:PAD].astype(low)


def fill_padded(grid, col_ref, row_ref, corner_ref, pad_ref, hold_ref):
    right, lower = edge_flags()
    cells = TILE * TILE
    batches = grid.shape[0] // cells
    per_batch = (TILE + 2) * PAD
    pad_ref[...] = jnp.zeros(pad_ref.shape, wide)
    hold_ref[0 : batches * TILE] = col_ref[...].astype(wide)
    for batch in range(batches):
        for a in range(TILE):
            at = batch * per_batch + (a + 1) * PAD
            source = batch * cells + a * TILE
            pad_ref[at + 1 : at + 1 + TILE] = grid[source : source + TILE]
            got = hold_ref[batch * TILE + a : batch * TILE + a + 1]
            zero = jnp.zeros_like(got)
            pad_ref[at : at + 1] = jnp.where(right, zero, got)
            pad_ref[at + TILE + 1 : at + TILE + 2] = jnp.where(right, got, zero)
    rows = row_ref[...].astype(wide)
    corners = corner_ref[...].astype(wide)
    for batch in range(batches):
        got = rows[batch * PAD : batch * PAD + TILE]
        corner = corners[batch : batch + 1]
        zero = jnp.zeros_like(got)
        nil = jnp.zeros_like(corner)
        for at, used in (
            (batch * per_batch, jnp.logical_not(lower)),
            (batch * per_batch + (TILE + 1) * PAD, lower),
        ):
            pad_ref[at + 1 : at + 1 + TILE] = jnp.where(used, got, zero)
            left = jnp.logical_and(used, jnp.logical_not(right))
            pad_ref[at : at + 1] = jnp.where(left, corner, nil)
            pad_ref[at + TILE + 1 : at + TILE + 2] = jnp.where(
                jnp.logical_and(used, right), corner, nil
            )


def map_body(*refs):
    heads = lax.axis_size("heads")
    part_refs, (map_ref, col_ref, row_ref, corner_ref, grid, hold) = refs[:heads], refs[heads:]
    mapped = total_of(part_refs).astype(low)
    map_ref[...] = mapped
    grid[...] = mapped.astype(wide)
    send_edges(grid, hold, col_ref, row_ref, corner_ref)


def gate_body(tok_ref, *refs):
    piece_refs, (gate_ref,) = refs[:BLOCKS], refs[BLOCKS:]
    chans = gate_ref.shape[1]
    start = piece_refs[0].shape[0] - chans
    weights = wide_rows(views(piece_refs, start, chans), 0, chans // LANES)
    gate_ref[...] = jnp.tanh(dot(tok_ref[...], weights)).astype(wide)


def own_rows(ref, at, rows):
    return ref[pl.ds(pl.multiple_of(rows * at, 8), rows)]


def write_chunks(total_ref, out_refs):
    head = lax.axis_index("heads")
    rows = total_ref.shape[0] // len(out_refs)
    for j, out_ref in enumerate(out_refs):
        out_ref[...] = own_rows(total_ref, head ^ j, rows).astype(low)


def whole_rows(part_refs, hold_ref, rows):
    head = lax.axis_index("heads")
    for j, ref in enumerate(part_refs):
        to = pl.ds(pl.multiple_of(rows * (head ^ j), 8), rows)
        hold_ref[to] = ref[...].astype(wide)[:rows]
    return hold_ref[...].astype(low)


def depthwise_body(map_ref, col_ref, row_ref, corner_ref, dw_ref, gate_ref, *refs):
    pad_ref, spread_ref, joined_ref, grid, hold = refs
    grid[...] = map_ref[...].astype(wide)
    fill_padded(grid, col_ref, row_ref, corner_ref, pad_ref, hold)
    cells = TILE * TILE
    batches = grid.shape[0] // cells
    per_batch = (TILE + 2) * PAD
    for batch in range(batches):
        for a in range(TILE):
            running = jnp.broadcast_to(dw_ref[9:10], (TILE, grid.shape[1]))
            for tap in range(9):
                row, col = divmod(tap, 3)
                at = batch * per_batch + (a + row) * PAD + col
                running = running + dw_ref[tap : tap + 1] * pad_ref[at : at + TILE]
            to = batch * cells + a * TILE
            spread_ref[to : to + TILE] = running
    joined_ref[...] = (gate_ref[...] * spread_ref[...]).astype(low)


def project_all(rows_refs, piece_refs, base_ref, sum_ref):
    rows = cat([ref[...] for ref in rows_refs], 1)
    for pair in range(BLOCKS // 2):
        weights = wide_cols(piece_refs[2 * pair : 2 * pair + 2], 0, rows.shape[1])
        lanes = slice(2 * pair * LANES, 2 * (pair + 1) * LANES)
        sum_ref[:, lanes] = base_ref[:, lanes].astype(wide) + dot(rows, weights)


def join_body(tok_ref, gain_ref, bias_ref, *refs):
    heads = lax.axis_size("heads")
    part_refs, piece_refs = refs[:heads], rows_of(*refs[heads : heads + 2])
    first_ref, all_ref, query_ref, kv_ref = refs[heads + 2 :]
    chans = query_ref.shape[1]
    join_refs = views(piece_refs, 0, heads * chans)
    attn_refs = views(piece_refs, heads * chans, 3 * chans)
    project_all(part_refs, join_refs, tok_ref, first_ref)
    rows = (normed(first_ref[...])[0] * gain_ref[0:1] + bias_ref[0:1]).astype(low)
    all_ref[...] = rows
    count = chans // LANES
    for s in range(3):
        result = dot(all_ref[...], wide_rows(attn_refs, s * chans, count)).astype(low)
        if s == 0:
            query_ref[...] = result
        else:
            kv_ref[:, (s - 1) * chans : s * chans] = result


def head_masks(rows):
    lane = lax.broadcasted_iota(jnp.int32, (rows, LANES), 1)
    return [lane < HEAD_DIM, lane >= HEAD_DIM]


def softmax_parts(query, keys):
    scores = dot(query, keys, (1, 1)) * HEAD_DIM ** (-0.5)
    expo = jnp.exp(scores - jnp.max(scores, axis=-1, keepdims=True))
    return expo / jnp.sum(expo, axis=-1, keepdims=True)


def attend_body(query_ref, *refs):
    kv_refs, (mixed_ref,) = refs[:4], refs[4:]
    chans = query_ref.shape[1]
    cells = TILE * TILE
    masks = head_masks(cells)
    for batch in range(query_ref.shape[0] // cells):
        at = slice(batch * cells, (batch + 1) * cells)
        for pair in range(chans // LANES):
            lanes = slice(pair * LANES, (pair + 1) * LANES)
            value_lanes = slice(chans + pair * LANES, chans + (pair + 1) * LANES)
            keys = cat([ref[at, lanes] for ref in kv_refs], 0)
            values = cat([ref[at, value_lanes] for ref in kv_refs], 0)
            query = query_ref[at, lanes]
            found = []
            for mask in masks:
                probs = softmax_parts(jnp.where(mask, query, jnp.zeros_like(query)), keys)
                found.append(dot(probs.astype(low), values))
            mixed_ref[at, lanes] = jnp.where(masks[0], found[0], found[1]).astype(low)


HIDDEN_STEP = 256


def ffn_body(upstream_ref, first_ref, gain_ref, bias_ref, *refs):
    heads = lax.axis_size("heads")
    part_refs = refs[:heads]
    out_pieces, piece_refs, refs = third_refs(refs[heads:], 5 + heads)
    second_ref, all_ref, hidden_ref, d_hidden_ref = refs[:4]
    out_refs, total_ref = refs[4:-1], refs[-1]
    hidden_width = hidden_ref.shape[1]
    depth = heads * part_refs[0].shape[1]
    start = piece_refs[0].shape[0] - 2 * hidden_width
    piece_refs = views(piece_refs, start, 2 * hidden_width)
    project_all(part_refs, views(out_pieces, 0, depth), first_ref, second_ref)
    rows = normed(second_ref[...])[0] * gain_ref[1:2] + bias_ref[1:2]
    all_ref[...] = rows.astype(low)
    total_ref[...] = jnp.zeros(total_ref.shape, wide)
    per_step = HIDDEN_STEP // LANES

    def step(m, carry):
        at = pl.multiple_of(m * HIDDEN_STEP, HIDDEN_STEP)
        up = cat(
            [
                cat([ref[pl.ds(at + i * LANES, LANES)] for i in range(per_step)], 1)
                for ref in piece_refs
            ],
            0,
        )
        down = cat([ref[pl.ds(hidden_width + at, HIDDEN_STEP)] for ref in piece_refs], 1)
        value, slope = gelu_parts(dot(all_ref[...], up))
        hidden_ref[:, pl.ds(at, HIDDEN_STEP)] = value.astype(low)
        d_hidden = (dot(upstream_ref[...], down, (1, 1)) * slope).astype(low)
        d_hidden_ref[:, pl.ds(at, HIDDEN_STEP)] = d_hidden
        total_ref[...] += dot(d_hidden, up, (1, 1))
        return carry

    lax.fori_loop(0, hidden_width // HIDDEN_STEP, step, 0)
    write_chunks(total_ref, out_refs)


def down_body(hidden_ref, *refs):
    _, piece_refs, refs = third_refs(refs, 1 + lax.axis_size("heads"))
    out_refs, total_ref = refs[:-1], refs[-1]
    width = hidden_ref.shape[1]
    piece_refs = views(piece_refs, piece_refs[0].shape[0] - 2 * width, 2 * width)
    for pair in range(BLOCKS // 2):
        weights = wide_cols(piece_refs[2 * pair : 2 * pair + 2], width, width)
        lanes = slice(2 * pair * LANES, 2 * (pair + 1) * LANES)
        total_ref[:, lanes] = dot(hidden_ref[...], weights)
    write_chunks(total_ref, out_refs)


def whole_cols_body(base_ref, *refs):
    part_refs, out_ref = refs[:-1], refs[-1]
    head = lax.axis_index("heads")
    shard = out_ref.shape[0]
    for place in range(BLOCKS):
        lanes = slice(place * LANES, (place + 1) * LANES)
        mine = base_ref[pl.ds(pl.multiple_of(shard * head, 8), shard), lanes]
        total = mine + total_of(part_refs, (slice(None), lanes))
        to = pl.ds(pl.multiple_of(LANES * block_at(place), LANES), LANES)
        out_ref[:, to] = total.astype(low)


def block_out_body(*refs):
    part_refs, out_ref, hold = refs[:-2], refs[-2], refs[-1]
    head = lax.axis_index("heads")
    shard = out_ref.shape[0] // len(part_refs)
    for j, ref in enumerate(part_refs):
        to = pl.ds(pl.multiple_of(shard * (head ^ j), 8), shard)
        chans = ref.shape[1]
        rows = ref[...].astype(wide)[out_ref.shape[0] :]
        for m in range(out_ref.shape[1] // chans):
            hold[to, m * chans : (m + 1) * chans] = rows[m * shard : (m + 1) * shard]
    out_ref[...] = hold[...].astype(out_ref.dtype)


def tokens_grad_body(d_first_ref, *refs):
    heads = lax.axis_size("heads")
    part_refs, own_refs = refs[:heads], refs[heads : heads + BLOCKS]
    other_refs, out_ref = rows_of(*refs[heads + BLOCKS : -1]), refs[-1]
    chans = part_refs[0].shape[1]
    own_refs = views(own_refs, own_refs[0].shape[0] - chans, chans)
    rows = cat([ref[0 : out_ref.shape[0]] for ref in part_refs], 1)
    count = chans // LANES
    for pair in range(BLOCKS // 2):
        both = slice(2 * pair, 2 * pair + 2)
        weights = [wide_rows(own_refs[both], 0, count)]
        weights += [wide_rows(other_refs[both], j * chans, count) for j in range(heads - 1)]
        lanes = slice(2 * pair * LANES, 2 * (pair + 1) * LANES)
        grad = d_first_ref[:, lanes].astype(wide) + dot(rows, cat(weights, 1), (1, 1))
        for i in range(2):
            block = block_at(2 * pair + i)
            to = pl.ds(pl.multiple_of(LANES * block, LANES), LANES)
            out_ref[:, to] = grad[:, i * LANES : (i + 1) * LANES]


def norm_back_body(values_ref, base_ref, gain_ref, *refs):
    part_refs, (sum_ref, low_ref) = refs[:-2], refs[-2:]
    rows = sum_ref.shape[0]
    head = lax.axis_index("heads")
    scaled, inv_std = normed(own_rows(values_ref, head, rows))
    upstream = total_of(part_refs)
    weighted = upstream * gain_ref[...]
    inner = (
        weighted
        - jnp.mean(weighted, axis=-1, keepdims=True)
        - scaled * jnp.mean(weighted * scaled, axis=-1, keepdims=True)
    )
    base = base_ref[...] if base_ref.shape[0] == rows else own_rows(base_ref, head, rows)
    total = base.astype(wide) + inv_std * inner
    sum_ref[...] = total
    sums = [
        jnp.sum(upstream * scaled, axis=0, keepdims=True),
        jnp.sum(upstream, axis=0, keepdims=True),
    ]
    coarse = [each.astype(low).astype(wide) for each in sums]
    fine = [each - near for each, near in zip(sums, coarse)]
    extra = low_ref.shape[0] - rows - 4
    blank = jnp.zeros((extra, total.shape[1]), wide)
    low_ref[...] = cat([total, *coarse, *fine, blank], 0).astype(low)


def sums_from(part_refs, sums_ref, shard):
    found = total_of(part_refs, slice(shard, shard + 8))
    sums_ref[...] = found[0:2] + found[2:4]


def attend_back_body(query_ref, *refs):
    heads = lax.axis_size("heads")
    kv_refs, part_refs = refs[:4], refs[4 : 4 + heads]
    piece_refs, _, refs = third_refs(refs[4 + heads :], 7)
    all_ref, d_query_ref, keep_ref, send_ref, sums_ref, d_mixed_ref, hold = refs
    chans = query_ref.shape[1]
    cells = TILE * TILE
    scale = HEAD_DIM ** (-0.5)
    shard = all_ref.shape[0] // heads
    all_ref[...] = whole_rows(part_refs, hold, shard)
    sums_from(part_refs, sums_ref, shard)
    weights = wide_cols(views(piece_refs, 0, heads * chans), 0, chans)
    d_mixed_ref[...] = dot(all_ref[...], weights, (1, 1)).astype(low)
    masks = head_masks(cells)
    for batch in range(query_ref.shape[0] // cells):
        at = slice(batch * cells, (batch + 1) * cells)
        for pair in range(chans // LANES):
            lanes = slice(pair * LANES, (pair + 1) * LANES)
            value_lanes = slice(chans + pair * LANES, chans + (pair + 1) * LANES)
            keys = cat([ref[at, lanes] for ref in kv_refs], 0)
            values = cat([ref[at, value_lanes] for ref in kv_refs], 0)
            query = query_ref[at, lanes]
            d_mixed = d_mixed_ref[at, lanes]
            d_queries = []
            d_keys = 0.0
            d_values = 0.0
            for mask in masks:
                own_query = jnp.where(mask, query, jnp.zeros_like(query))
                own_mixed = jnp.where(mask, d_mixed, jnp.zeros_like(d_mixed))
                probs = softmax_parts(own_query, keys)
                d_probs = dot(own_mixed, values, (1, 1))
                inner = jnp.sum(probs * d_probs, axis=-1, keepdims=True)
                d_scores = (probs * (d_probs - inner)).astype(low)
                d_queries.append(dot(d_scores, keys))
                d_keys = d_keys + dot(d_scores, own_query, (0, 0))
                d_values = d_values + dot(probs.astype(low), own_mixed, (0, 0))
            d_query = jnp.where(masks[0], d_queries[0], d_queries[1]) * scale
            d_query_ref[at, lanes] = d_query.astype(low)
            d_keys = d_keys * scale
            for i in range(4):
                target = (keep_ref, send_ref)[i // 2]
                own = slice(i * cells, (i + 1) * cells)
                target[i % 2, at, lanes] = d_keys[own].astype(target.dtype)
                target[i % 2, at, value_lanes] = d_values[own].astype(target.dtype)


def add_pair_body(keep_ref, got_ref, own_ref, send_ref):
    own_ref[...] = keep_ref[0] + got_ref[0].astype(wide)
    send_ref[...] = (keep_ref[1] + got_ref[1].astype(wide)).astype(low)


def d_qkv_body(d_query_ref, own_ref, got_ref, *refs):
    piece_refs, (d_qkv_ref, *out_refs, total_ref) = rows_of(*refs[:2]), refs[2:]
    chans = d_query_ref.shape[1]
    d_qkv_ref[:, :chans] = d_query_ref[...]
    d_qkv_ref[:, chans:] = (own_ref[...] + got_ref[...].astype(wide)).astype(low)
    d_qkv = d_qkv_ref[...]
    count = 3 * chans // LANES
    piece_refs = views(piece_refs, lax.axis_size("heads") * chans, 3 * chans)
    for pair in range(BLOCKS // 2):
        weights = wide_rows(piece_refs[2 * pair : 2 * pair + 2], 0, count)
        lanes = slice(2 * pair * LANES, 2 * (pair + 1) * LANES)
        total_ref[:, lanes] = dot(d_qkv, weights, (1, 1))
    write_chunks(total_ref, out_refs)


def gate_back_body(gate_ref, spread_ref, result_ref, *refs):
    heads = lax.axis_size("heads")
    head = lax.axis_index("heads")
    part_refs, piece_refs = refs[:heads], rows_of(*refs[heads : heads + 2])
    all_ref, d_gate_ref, tail_ref, grid_ref, sums_ref, *edge_refs, edge, hold = refs[heads + 2 :]
    shard = all_ref.shape[0] // heads
    all_ref[...] = whole_rows(part_refs, hold, shard)
    sums_from(part_refs, sums_ref, shard)
    chans = gate_ref.shape[1]
    weights = wide_cols(views(piece_refs, 0, heads * chans), 0, chans)
    d_joined = dot(all_ref[...], weights, (1, 1))
    gate = gate_ref[...]
    d_gate = d_joined * spread_ref[...] * (1.0 - gate * gate)
    d_gate_ref[...] = d_gate.astype(low)
    result = result_ref[...].astype(wide)
    folded = [result[:, m * chans : (m + 1) * chans] for m in range(result.shape[1] // chans)]
    tail_ref[...] = cat([d_gate, *folded], 0).astype(low)
    grid_ref[...] = d_joined * gate
    send_edges(grid_ref, edge, *edge_refs)


def depthwise_back_body(grid_ref, col_ref, row_ref, corner_ref, dw_ref, out_ref, d_pad, hold, flat):
    fill_padded(grid_ref, col_ref, row_ref, corner_ref, d_pad, hold)
    cells = TILE * TILE
    per_batch = (TILE + 2) * PAD
    chans = grid_ref.shape[1]
    for batch in range(grid_ref.shape[0] // cells):
        for a in range(TILE):
            running = jnp.zeros((TILE, chans), wide)
            for tap in range(9):
                row, col = divmod(tap, 3)
                at = batch * per_batch + (a + 2 - row) * PAD + 2 - col
                running = running + dw_ref[tap : tap + 1] * d_pad[at : at + TILE]
            flat[batch * cells + a * TILE : batch * cells + (a + 1) * TILE] = running
    out_ref[...] = flat[...].astype(low)


def taps_body(grid_ref, pad_ref, ln1_ref, ln2_ref, small_ref):
    cells = TILE * TILE
    per_batch = (TILE + 2) * PAD
    chans = grid_ref.shape[1]
    sums = [jnp.zeros((TILE, chans), wide) for _ in range(10)]
    for batch in range(grid_ref.shape[0] // cells):
        for a in range(TILE):
            own = grid_ref[batch * cells + a * TILE : batch * cells + (a + 1) * TILE]
            for tap in range(9):
                row, col = divmod(tap, 3)
                at = batch * per_batch + (a + row) * PAD + col
                sums[tap] = sums[tap] + own * pad_ref[at : at + TILE]
            sums[9] = sums[9] + own
    small_ref[...] = jnp.zeros(small_ref.shape, wide)
    for place in range(BLOCKS):
        lanes = slice(place * LANES, (place + 1) * LANES)
        to = pl.ds(pl.multiple_of(LANES * block_at(place), LANES), LANES)
        small_ref[0:2, to] = ln1_ref[:, lanes]
        small_ref[2:4, to] = ln2_ref[:, lanes]
    per_row = small_ref.shape[1] // chans
    for tap in range(10):
        row, lane = 4 + tap // per_row, tap % per_row * chans
        total = jnp.sum(sums[tap], axis=0, keepdims=True)
        small_ref[row : row + 1, lane : lane + chans] = total


def small_final_body(own_ref, got_ref, ln1_ref, ln2_ref, taps_ref):
    total = own_ref[...] + got_ref[...]
    ln1_ref[...] = total[0:2]
    ln2_ref[...] = total[2:4]
    chans = taps_ref.shape[1]
    per_row = total.shape[1] // chans
    for tap in range(10):
        row, lane = 4 + tap // per_row, tap % per_row * chans
        taps_ref[tap : tap + 1] = total[row : row + 1, lane : lane + chans]


def conv_back_body(pool_ref, whole_ref, *refs):
    heads = lax.axis_size("heads")
    head = lax.axis_index("heads")
    part_refs, (hires_ref,) = refs[:heads], refs[heads:]
    per_chunk = BLOCKS // heads
    d_pooled = 0.0
    for j, ref in enumerate(part_refs):
        first = per_chunk * (head ^ j)
        chunk = cat([whole_ref[first + i] for i in range(per_chunk)], 1)
        d_pooled = d_pooled + dot(ref[...], chunk, (1, 1))
    d_pooled = d_pooled.astype(low)
    batches = pool_ref.shape[0]
    rows = pool_ref.shape[1]
    for batch in range(batches):
        own = d_pooled[batch * rows : (batch + 1) * rows]
        hires_ref[batch] = dot(pool_ref[batch], own, (0, 0))


def conv_grad_body(pooled_ref, *refs):
    heads = lax.axis_size("heads")
    head = lax.axis_index("heads")
    part_refs, (keep_ref, send_ref, hold) = refs[:heads], refs[heads + 2 :]
    per_chunk = BLOCKS // heads
    for j, ref in enumerate(part_refs):
        grad = dot(pooled_ref[...], ref[...], (0, 0)).astype(low)
        for i in range(per_chunk):
            hold[per_chunk * (head ^ j) + i] = grad[:, i * LANES : (i + 1) * LANES]
    for place in range(BLOCKS):
        target = place_refs(keep_ref, send_ref, place)
        target[0 : hold.shape[1]] = hold[block_at(place)]


def place_refs(keep_ref, send_ref, place):
    return ((keep_ref, send_ref)[place // 4]).at[place % 4]


def row_grad(left_ref, right, keep_ref, send_ref, start):
    count = right.shape[1] // LANES
    for place in range(BLOCKS):
        lanes = slice(place * LANES, (place + 1) * LANES)
        grad = dot(left_ref[:, lanes], right, (0, 0)).astype(low)
        target = place_refs(keep_ref, send_ref, place)
        for m in range(count):
            target[start + m * LANES : start + (m + 1) * LANES] = grad[
                :, m * LANES : (m + 1) * LANES
            ]


def col_grad(left_ref, right_ref, keep_ref, send_ref, start):
    width = left_ref.shape[1]
    for m in range(width // LANES):
        grad = dot(left_ref[:, m * LANES : (m + 1) * LANES], right_ref[...], (0, 0)).astype(low)
        for place in range(BLOCKS):
            target = place_refs(keep_ref, send_ref, place)
            target[start + m * LANES : start + (m + 1) * LANES] = grad[
                :, place * LANES : (place + 1) * LANES
            ]


def pair_grad_body(row_left, row_right, col_left, col_right, keep_ref, send_ref):
    width = row_right.shape[1]
    start = keep_ref.shape[1] - width - col_left.shape[1]
    row_grad(row_left, row_right[...], keep_ref, send_ref, start)
    col_grad(col_left, col_right, keep_ref, send_ref, start + width)


def final_rows(refs, start, count):
    return cat(
        [total_of(refs, slice(start + m * LANES, start + (m + 1) * LANES)) for m in range(count)],
        1,
    )


def last_final_body(*refs):
    first_refs, rest_ref, results = refs[:4], refs[4], refs[5:]
    conv_ref, gate_ref, join_ref, attn_ref, out_ref = results
    rows, chans = conv_ref.shape[0], gate_ref.shape[1]
    conv_ref[...] = total_of(first_refs, slice(0, rows))
    gate_ref[...] = final_rows(first_refs, rows, chans // LANES)
    join_ref[...] = total_of(first_refs, slice(rows + chans, rows + 2 * chans))
    at = first_refs[0].shape[0]
    behind = pl.ds(at, rest_ref.shape[0])
    part_refs = [rest_ref, *[ref.at[behind] for ref in first_refs[1:]]]
    for s in range(3):
        attn_ref[s] = final_rows(part_refs, s * chans, chans // LANES)
    out_ref[...] = total_of(part_refs, slice(3 * chans, 3 * chans + out_ref.shape[0]))


def up_down_final_body(*refs):
    part_refs, (up_ref, down_ref) = refs[:-2], refs[-2:]
    width = up_ref.shape[1]
    up_ref[...] = final_rows(part_refs, 0, width // LANES)
    down_ref[...] = total_of(part_refs, slice(width, width + down_ref.shape[0]))


def unpack_rows(packed, count):
    places = packed.shape[0]
    return (
        packed.reshape(places, count, LANES, LANES)
        .transpose(0, 2, 1, 3)
        .reshape(places * LANES, count * LANES)
    )


def unpack_cols(packed):
    return packed.transpose(1, 0, 2).reshape(packed.shape[1], -1)


def pack_rows(weights):
    count = weights.shape[1] // LANES
    return (
        weights.reshape(BLOCKS, LANES, count, LANES)
        .transpose(0, 2, 1, 3)
        .reshape(BLOCKS, count * LANES, LANES)
    )


def pack_cols(weights):
    return weights.reshape(weights.shape[0], BLOCKS, LANES).transpose(1, 0, 2)


def scatter_dim(grad, axis):
    return lax.psum_scatter(grad, "tiles", scatter_dimension=axis, tiled=True).astype(wide)


def local(
    vit_tokens,
    hires_maps,
    map_sizes,
    out_grad,
    ln_gain,
    ln_bias,
    dw_params,
    conv_w,
    gate_w,
    join_w,
    attn_in_w,
    out_w,
    up_w,
    down_w,
):
    tiles = lax.axis_size("tiles")
    heads = lax.axis_size("heads")
    fast = fast_tiles()
    batches, rows, width = vit_tokens.shape
    total = batches * rows
    shard = total // heads
    chans = dw_params.shape[1]
    hidden_width = down_w.shape[0]
    pixels, hires_chans = hires_maps.shape[1:]
    dma = pltpu.SemaphoreType.DMA
    plan = Plan(STARTS, FINISHES, TURNS)

    cross = heads * chans
    lanes_of = chans // LANES
    if fast:
        first_own, cross_own = run_kernel(
            pack_first_body,
            [shape((hires_chans + chans, LANES)), shape((3 * chans, LANES))],
            conv_w,
            gate_w,
            join_w,
            out_w,
            scratch=[((), dma((3 + 2 * lanes_of,)))],
            fetch=True,
        )
        first_pieces = gather_first(first_own)
        for i, name in enumerate(("own", "x", "y", "corner")):
            plan.mark("first_" + name + "_core", first_pieces[4 + i])
            if i:
                plan.mark("first_" + name, first_pieces[i])
        cross_parts = plan.gather("cross", cross_own)
        second_own, third_own, fourth_own = run_kernel(
            pack_rest_body,
            [
                shape((cross + 3 * chans, LANES)),
                shape((cross + 2 * hidden_width, LANES)),
                shape((cross - chans, LANES)),
            ],
            attn_in_w,
            up_w,
            down_w,
            *cross_parts,
            scratch=[((), dma((3 * heads + 3 * lanes_of + hidden_width // LANES,)))],
            fetch=True,
        )
    else:

        def whole_of(weights, axis):
            return lax.all_gather(weights, "tiles", axis=axis, tiled=True)

        def halves(*packed):
            joint = jnp.concatenate(packed, axis=1)
            return joint[: BLOCKS // 2], joint[BLOCKS // 2 :]

        gate_all = [pack_rows(each) for each in gather_heads(whole_of(gate_w, 0))]
        join_all = [pack_cols(each) for each in gather_heads(whole_of(join_w, 1))]
        out_all = [pack_cols(each) for each in gather_heads(whole_of(out_w, 1))]
        attn_whole = whole_of(attn_in_w, 1)
        first_stack = jnp.concatenate([pack_cols(whole_of(conv_w, 1)), gate_all[0]], axis=1)
        first_pieces = [first_stack[p] for p in range(BLOCKS)]
        second = halves(*join_all, *[pack_rows(each) for each in attn_whole])
        third = halves(
            *out_all,
            pack_rows(whole_of(up_w, 0)),
            pack_cols(whole_of(down_w, 1)),
        )
        fourth = halves(*gate_all[1:])

    inputs = (
        vit_tokens.reshape(total, width),
        out_grad.reshape(total, width),
        ln_gain,
        ln_bias,
    )
    tokens, upstream, gains, biases = run_kernel(
        relative_body,
        [shape(each.shape, each.dtype) for each in inputs],
        *inputs,
        scratch=[(each.shape, each.dtype) for each in inputs] + [((), dma((4,)))],
        fetch=True,
    )
    upstream_wide = upstream.astype(wide)

    pooled, pools = pl.pallas_call(
        pool_body,
        out_shape=(shape((total, hires_chans)), shape((batches, rows, pixels))),
        in_specs=[
            pl.BlockSpec(memory_space=pltpu.SMEM),
            pl.BlockSpec(memory_space=pl.ANY),
        ],
        out_specs=tuple([pl.BlockSpec(memory_space=pltpu.VMEM)] * 2),
        scratch_shapes=[pltpu.VMEM(hires_maps.shape, low), dma((1,))],
        compiler_params=pltpu.CompilerParams(vmem_limit_bytes=VMEM_LIMIT),
    )(map_sizes, hires_maps)
    conv_whole, *conv_parts = run_kernel(
        conv_body,
        [shape((BLOCKS, hires_chans, LANES))] + [shape((total, chans))] * heads,
        plan.enter("conv", after(pooled, tokens)),
        *first_pieces,
        flops=2 * total * hires_chans * width,
    )
    edge_shapes = [
        shape((batches * TILE, chans)),
        shape((batches * PAD, chans)),
        shape((PAD, chans)),
    ]
    edge_scratch = ((batches * PAD, chans), wide)
    grid_scratch = ((total, chans), wide)
    pad_dims = (batches * (TILE + 2) * PAD, chans)
    plan.mark("conv", conv_whole)
    own_part, *other_parts = plan.over_heads("conv_z", conv_parts)
    mapped, *edges = run_kernel(
        map_body,
        [shape((total, chans))] + edge_shapes,
        plan.enter("map", own_part),
        *other_parts,
        scratch=[grid_scratch, edge_scratch],
    )

    def swap_edges(name, col, row, corner):
        return (
            plan.mark(name + "_c", over_core(col)),
            plan.mark(name + "_x", over_x(row)),
            plan.mark(name + "_xc", swap_with(corner, "tiles", 3)),
        )

    plan.mark("map", mapped)
    edges = swap_edges("edge", *edges)

    (gate,) = run_kernel(
        gate_body,
        [shape((total, chans), wide)],
        tokens,
        *first_pieces,
        flops=2 * total * chans * width,
    )
    chunk_shapes = [shape((shard, width))] * heads
    padded, spread, joined = run_kernel(
        depthwise_body,
        [shape(pad_dims, wide), shape((total, chans), wide), shape((total, chans))],
        plan.enter("depthwise", mapped),
        *edges,
        dw_params,
        gate,
        scratch=[grid_scratch, edge_scratch],
    )

    plan.mark("depthwise", joined)
    joined_parts = plan.gather("joined", joined)
    if fast:
        second_x = plan.finish("second_x", over_x(plan.start("second_x", second_own)))
        second_y = plan.finish("second_y", over_y(plan.start("second_y", second_own)))
        corner = over_y(plan.start("second_corner", second_x))
        plan.finish("second_corner", corner)
        second_stack = stacked(
            plan.start("second_stack", second_own), second_x, second_y, corner
        )
        second_core = over_core(plan.start("second_core", second_stack))
        second = (second_stack, plan.finish("second_core", second_core))
    wide_rows_shape = shape((total, width), wide)
    first, normed1, query, kv_own = run_kernel(
        join_body,
        [
            wide_rows_shape,
            shape((total, width)),
            shape((total, chans)),
            shape((total, 2 * chans)),
        ],
        tokens,
        gains,
        biases,
        plan.enter("join", joined_parts[0]),
        *joined_parts[1:],
        *second,
        flops=2 * total * width * (width + 3 * chans),
    )
    plan.mark("join", kv_own)
    kv_x = plan.mark("kv_x", over_x(kv_own))
    kv_all = [
        kv_own,
        kv_x,
        plan.mark("kv_core", over_core(kv_own)),
        plan.mark("kv_x_core", over_core(kv_x)),
    ]
    (mixed,) = run_kernel(
        attend_body,
        [shape((total, chans))],
        plan.enter("attend", query),
        *kv_all,
        flops=8 * total * 4 * rows * chans,
    )
    plan.mark("attend", mixed)
    if fast:
        third_x = plan.finish("third_x", over_x(plan.start("third_x", third_own)))
        third_y = plan.finish("third_y", over_y(plan.start("third_y", third_own)))
        third_stack = stacked(third_own, third_x, third_y)
        upper = over_y(plan.start("upper", third_x[:cross]))
        lower = over_x(plan.start("lower", third_y[cross:]))
        plan.finish("upper", upper)
        plan.finish("lower", lower)
        third_core = over_core(plan.start("third_core", third_stack))
        plan.finish("third_core", third_core)
    mixed_parts = plan.gather("mixed", mixed)
    if fast:
        third = (
            third_stack,
            upper,
            lower,
            third_core,
            over_core(plan.start("upper_core", upper)),
            over_core(plan.start("lower_core", lower)),
        )

    wide_shape = shape((total, hidden_width))
    total_scratch = ((total, width), wide)
    second_rows, normed2, hidden, d_hidden, *ffn_parts = run_kernel(
        ffn_body,
        [wide_rows_shape, shape((total, width)), wide_shape, wide_shape] + chunk_shapes,
        upstream,
        first,
        gains,
        biases,
        plan.enter("ffn", mixed_parts[0]),
        *mixed_parts[1:],
        *third,
        scratch=[total_scratch],
        flops=2 * total * width * (width + 3 * hidden_width),
    )
    plan.mark("ffn", normed2)
    ffn_parts = plan.over_heads("ffn_z", ffn_parts)
    if fast:
        fourth_x = plan.finish("fourth_x", over_x(plan.start("fourth_x", fourth_own)))
        fourth_y = plan.finish("fourth_y", over_y(plan.start("fourth_y", fourth_own)))
    back_shapes = [shape((shard, width), wide), shape((shard + 8, width))]
    d_second, d_attn_own = run_kernel(
        norm_back_body,
        back_shapes,
        plan.enter("norm2", second_rows),
        upstream_wide,
        gains[1:2],
        *ffn_parts,
    )
    plan.mark("norm2", d_attn_own)
    d_attn_parts = plan.gather("d_attn", d_attn_own)
    if fast:
        fourth_corner = over_y(plan.start("fourth_corner", fourth_x))
        plan.finish("fourth_corner", fourth_corner)
    ud_keep, ud_send = run_kernel(
        pair_grad_body,
        [shape((4, 2 * hidden_width, LANES))] * 2,
        plan.start("ud_kernel", normed2),
        d_hidden,
        hidden,
        upstream,
        flops=4 * total * hidden_width * width,
    )
    plan.finish("ud_kernel", ud_keep)

    down_parts = run_kernel(
        down_body,
        chunk_shapes,
        plan.start("down_kernel", hidden),
        *third,
        scratch=[total_scratch],
        flops=2 * total * hidden_width * width,
    )
    plan.finish("down_kernel", down_parts[0])

    d_attn, d_query, kv_keep, kv_send, ln2_sums = run_kernel(
        attend_back_body,
        [
            shape((total, width)),
            shape((total, chans)),
            shape((2, total, 2 * chans), wide),
            shape((2, total, 2 * chans)),
            shape((2, width), wide),
        ],
        plan.enter("attend_back", query),
        *kv_all,
        *d_attn_parts,
        *third,
        scratch=[((total, chans), low), total_scratch],
        flops=2 * total * chans * width + 20 * total * 4 * rows * chans,
    )
    plan.mark("attend_back", kv_keep)
    kv_got = plan.mark("kv_got", over_core(kv_send))
    kv_mine, kv_over = run_kernel(
        add_pair_body,
        [shape((total, 2 * chans), wide), shape((total, 2 * chans))],
        plan.enter("add_pair", kv_keep),
        kv_got,
    )
    plan.mark("add_pair", kv_over)
    kv_back = plan.mark("kv_back", over_x(kv_over))
    down_parts = plan.over_heads("down", down_parts)
    (result_own,) = run_kernel(whole_cols_body, [shape((shard, width))], second_rows, *down_parts)
    if fast:
        fourth_stack = stacked(
            plan.start("fourth_stack", fourth_own), fourth_x, fourth_y, fourth_corner
        )
        fourth_core = over_core(plan.start("fourth_core", fourth_stack))
        fourth = (fourth_stack, plan.finish("fourth_core", fourth_core))
    d_qkv, *qkv_parts = run_kernel(
        d_qkv_body,
        [shape((total, 3 * chans))] + chunk_shapes,
        plan.enter("d_qkv", d_query),
        kv_mine,
        kv_back,
        *second,
        scratch=[total_scratch],
        flops=6 * total * chans * width,
    )
    plan.mark("d_qkv", d_qkv)
    qkv_parts = plan.over_heads("qkv_z", qkv_parts)
    if fast:
        ud_got = plan.finish("ud_core", over_core(plan.start("ud_core", ud_send)))
        ud_parts = add_cores(ud_keep, ud_got)
        ud_x = plan.finish("ud_x", over_x(plan.start("ud_x", ud_parts[1])))
        ud_y = plan.finish("ud_y", over_y(plan.start("ud_y", ud_parts[2])))
    else:
        ud_sums = jnp.concatenate([ud_keep, ud_send], axis=0)
    d_first, d_join_own = run_kernel(
        norm_back_body, back_shapes, first, plan.enter("norm3", d_second), gains[0:1], *qkv_parts
    )
    plan.mark("norm3", d_join_own)
    d_join_parts = plan.gather("d_join", d_join_own)
    ap_keep, ap_send = run_kernel(
        pair_grad_body,
        [shape((4, 4 * chans, LANES))] * 2,
        plan.start("ap_kernel", normed1),
        d_qkv,
        mixed,
        d_attn,
        flops=8 * total * chans * width,
    )
    plan.finish("ap_kernel", ap_keep)

    d_join, d_gate_in, tail, d_grid, ln1_sums, *edges = run_kernel(
        gate_back_body,
        [
            shape((total, width)),
            shape((total, chans)),
            shape((total + shard * (width // chans), chans)),
            shape((total, chans), wide),
            shape((2, width), wide),
        ]
        + edge_shapes,
        gate,
        spread,
        result_own,
        plan.enter("gate_back", d_join_parts[0]),
        *d_join_parts[1:],
        *second,
        scratch=[edge_scratch, total_scratch],
        flops=2 * total * chans * width,
    )
    plan.mark("gate_back", d_grid)
    edges = swap_edges("back", *edges)
    (d_mapped,) = run_kernel(
        depthwise_back_body,
        [shape((total, chans))],
        plan.enter("dw_back", d_grid),
        *edges,
        dw_params,
        scratch=[(pad_dims, wide), edge_scratch, grid_scratch],
    )
    plan.mark("dw_back", d_mapped)
    d_mapped_parts = plan.gather("d_mapped", d_mapped)
    if fast:
        ud_corner = over_corner(plan.start("ud_corner", ud_parts[3]))
        ud_sums = [ud_parts[0], ud_x, ud_y, plan.finish("ud_corner", ud_corner)]
        ap_got = plan.finish("ap_core", over_core(plan.start("ap_core", ap_send)))
        ap_parts = add_cores(ap_keep, ap_got)
    else:
        ap_sums = jnp.concatenate([ap_keep, ap_send], axis=0)
    (small,) = run_kernel(
        taps_body,
        [shape((8, width), wide)],
        plan.start("taps", d_grid),
        padded,
        ln1_sums,
        ln2_sums,
    )
    bit = 1
    while bit < tiles // 2:
        name = "small" + str(bit)
        got = swap_with(plan.start(name, small), "tiles", bit)
        small = small + plan.finish(name, got)
        bit *= 2
    small_got = swap_with(plan.start("small_last", small), "tiles", bit)
    plan.finish("small_last", small_got)
    if fast:
        up_grad, down_grad = run_kernel(
            up_down_final_body,
            [shape(up_w.shape, wide), shape(down_w.shape, wide)],
            *ud_sums,
            leave=True,
        )
        plan.finish("up_down", up_grad)
    first_shape = shape((4, hires_chans + 2 * chans, LANES))
    first_keep, first_send = run_kernel(
        pair_grad_body,
        [first_shape] * 2,
        plan.start("first_kernel", tokens),
        d_gate_in,
        joined,
        d_join,
        flops=4 * total * chans * width,
    )
    first_keep, first_send = run_kernel(
        conv_grad_body,
        [first_shape] * 2,
        plan.enter("conv_grad", pooled),
        *d_mapped_parts,
        first_keep,
        first_send,
        scratch=[((BLOCKS, hires_chans, LANES), low)],
        flops=2 * total * hires_chans * width,
        alias={heads + 1: 0, heads + 2: 1},
    )
    plan.mark("conv_grad", first_send)
    tail_parts = plan.gather("tail", tail)
    (hires_grad,) = run_kernel(
        conv_back_body,
        [shape((batches, pixels, hires_chans), wide)],
        plan.start("hires", pools),
        conv_whole,
        *d_mapped_parts,
        flops=2 * total * hires_chans * width + 2 * total * pixels * hires_chans,
        leave=True,
    )
    plan.finish("hires", hires_grad)
    if fast:
        first_got = plan.mark("first_got", over_core(first_send))
        first_rows = first_keep.shape[1]
        first_parts = run_kernel(
            add_first_body,
            [shape((first_rows, LANES))] + [shape((first_rows + 4 * chans, LANES))] * 3,
            plan.enter("add_first", first_keep),
            first_got,
            *ap_parts[1:],
        )
        plan.mark("add_first", first_parts[0])
        first_sums = [
            first_parts[0],
            over_x(plan.start("last_x", plan.enter("last_x", first_parts[1]))),
            over_y(plan.start("last_y", plan.enter("last_y", first_parts[2]))),
            over_corner(plan.start("last_corner", plan.enter("last_corner", first_parts[3]))),
        ]
    else:
        first_sums = jnp.concatenate([first_keep, first_send], axis=0)
    (tokens_grad,) = run_kernel(
        tokens_grad_body,
        [shape((total, width), wide)],
        d_join,
        *tail_parts,
        *first_pieces,
        *fourth,
        flops=2 * total * width * width,
        leave=True,
    )
    (block_out,) = run_kernel(
        block_out_body,
        [shape((total, width))],
        *tail_parts,
        scratch=[total_scratch],
        leave=True,
    )

    plan.finish("tokens", tokens_grad)
    plan.finish("block", block_out)
    ln1_grad, ln2_grad, taps_grad = run_kernel(
        small_final_body,
        [shape((2, width), wide), shape((2, width), wide), shape(dw_params.shape, wide)],
        small,
        small_got,
        leave=True,
    )

    if fast:
        results = (conv_w, gate_w, join_w, attn_in_w, out_w)
        conv_grad, gate_grad, join_grad, attn_grad, out_w_grad = run_kernel(
            last_final_body,
            [shape(each.shape, wide) for each in results],
            plan.enter("last", first_sums[0]),
            *first_sums[1:],
            ap_parts[0],
            leave=True,
        )
    else:
        count = chans // LANES
        at = hires_chans
        conv_grad = scatter_dim(unpack_cols(first_sums[:, :at]), 1)
        gate_grad = scatter_dim(unpack_rows(first_sums[:, at : at + chans], count), 0)
        join_grad = scatter_dim(unpack_cols(first_sums[:, at + chans :]), 1)
        attn_grad = jnp.stack(
            [
                scatter_dim(unpack_rows(ap_sums[:, s * chans : (s + 1) * chans], count), 0)
                for s in range(3)
            ]
        )
        out_w_grad = scatter_dim(unpack_cols(ap_sums[:, 3 * chans :]), 1)
        up_grad = scatter_dim(unpack_rows(ud_sums[:, :hidden_width], hidden_width // LANES), 0)
        down_grad = scatter_dim(unpack_cols(ud_sums[:, hidden_width:]), 1)

    return (
        block_out.reshape(batches, rows, width),
        tokens_grad.reshape(batches, rows, width),
        hires_grad,
        ln1_grad,
        ln2_grad,
        taps_grad,
        conv_grad,
        gate_grad,
        join_grad,
        attn_grad,
        out_w_grad,
        up_grad,
        down_grad,
    )


def solution(mesh):
    placed = (
        P(None, "tiles", None),
        P(None, "tiles", "heads"),
        P(),
        P(None, "tiles", None),
        P(),
        P(),
        P(None, "heads"),
        P("heads", "tiles"),
        P("tiles", "heads"),
        P("heads", "tiles"),
        P(None, "tiles", "heads"),
        P("heads", "tiles"),
        P("tiles", "heads"),
        P("heads", "tiles"),
    )
    return jax.shard_map(
        local,
        mesh=mesh,
        in_specs=placed,
        out_specs=(
            P(None, "tiles", None),
            P(None, "tiles", None),
            P(None, "tiles", "heads"),
            P(),
            P(),
            P(None, "heads"),
            P("heads", "tiles"),
            P("tiles", "heads"),
            P("heads", "tiles"),
            P(None, "tiles", "heads"),
            P("heads", "tiles"),
            P("tiles", "heads"),
            P("heads", "tiles"),
        ),
        check_vma=False,
    )
```

```python
import jax
import jax.numpy as jnp
from jax import lax
from jax.experimental import pallas as pl
from jax.experimental.pallas import tpu as pltpu
from jax.sharding import PartitionSpec as P

HEAD_DIM = 64
GRID = 24
TILE = 12
HR_TILE = 24
PAD = 16
LANES = 128

norm_eps = 1e-05
inv_root_two = 0.7071067811865476
inv_root_two_pi = 0.3989422804014327

low = jnp.bfloat16
wide = jnp.float32
VMEM_LIMIT = 24 * 1024 * 1024


class At:
    (
        d_mix, d_mix1, d_mix2, d_mix3, d_jo, d_jo1, d_jo2, d_jo3, cross, cross1, cross2,
        cross3, conv_z, conv_z1, conv_z2, conv_z3, joined, joined1, joined2, joined3, mixed,
        mixed1, mixed2, mixed3, ffn_z, ffn_z1, ffn_z2, ffn_z3, d_attn, d_attn1, d_attn2,
        d_attn3, down, down1, down2, down3, qkv_z, qkv_z1, qkv_z2, qkv_z3, d_join, d_join1,
        d_join2, d_join3, d_mapped, d_mapped1, d_mapped2, d_mapped3, tail, tail1, tail2, tail3,
        edge, edge_c, edge_x, edge_xc, back, back_c, back_x, back_xc, first_x, first_y,
        first_corner, relative, pool, first_own_core, first_x_core, first_y_core,
        first_corner_core, conv, map, depthwise, pack_rest, second_x, second_y, second_corner,
        second_stack, second_core, join, kv_x, kv_core, kv_x_core, attend, third_x, third_y,
        upper, lower, third_core, upper_core, lower_core, ffn, fourth_x, fourth_y, norm2,
        fourth_corner, ud_kernel, down_kernel, attend_back, kv_got, add_pair, kv_back,
        fourth_stack, fourth_core, d_qkv, ud_core, ud_x, ud_y, norm3, ap_kernel, gate_back,
        dw_back, ud_corner, ap_core, taps, small1, small2, small_last, up_down, first_kernel,
        conv_grad, hires, first_got, add_first, last_x, last_y, last_corner, tokens, block,
        last,
    ) = range(129)


STARTS = {
    At.second_x: At.conv,
    At.second_y: At.conv,
    At.second_corner: At.map,
    At.second_stack: At.joined3,
    At.third_y: At.joined3,
    At.upper: At.kv_x,
    At.lower: At.join,
    At.third_core: At.kv_core,
    At.mixed: At.third_core,
    At.upper_core: At.second_core,
    At.lower_core: At.mixed2,
    At.fourth_y: At.ffn,
    At.ud_kernel: At.fourth_corner,
    At.fourth_stack: At.kv_got,
    At.ud_core: At.kv_got,
    At.ud_x: At.down2,
    At.ud_y: At.d_qkv,
    At.ap_kernel: At.d_join1,
    At.ud_corner: At.qkv_z3,
    At.ap_core: At.gate_back,
    At.tail: At.small1,
    At.first_kernel: At.d_mapped1,
    At.small_last: At.conv_grad,
    At.small1: At.d_mapped3,
    At.fourth_core: At.fourth_corner,
    At.conv_z: At.cross3,
    At.down1: At.kv_got,
    At.last_y: At.first_own_core,
    At.fourth_corner: At.ffn_z3,
    At.cross1: At.first_own_core,
    At.tail3: At.conv_grad,
    At.taps: At.cross1,
    At.fourth_x: At.attend,
    At.small2: At.back_c,
    At.pack_rest: At.first_own_core,
    At.first_x_core: At.pool,
    At.first_y_core: At.pool,
    At.first_corner_core: At.pool,
}
FINISHES = {
    At.cross1: At.map,
    At.cross3: At.conv,
    At.fourth_x: At.norm2,
    At.fourth_y: At.norm2,
    At.fourth_corner: At.attend_back,
    At.ud_kernel: At.attend_back,
    At.down_kernel: At.attend_back,
    At.down1: At.d_qkv,
    At.down2: At.d_qkv,
    At.down3: At.add_pair,
    At.fourth_core: At.d_qkv,
    At.ud_x: At.dw_back,
    At.ud_y: At.norm3,
    At.ud_corner: At.gate_back,
    At.small2: At.conv_grad,
    At.up_down: At.conv_grad,
    At.hires: At.last_y,
    At.d_mapped1: At.dw_back,
    At.small_last: At.add_first,
    At.block: At.add_first,
    At.d_attn1: At.add_pair,
    At.upper: At.last_y,
    At.mixed3: At.last_y,
    At.ap_kernel: At.add_first,
    At.second_corner: At.last_y,
}
TURNS = {
    At.ffn_z: (3, 1, 2),
    At.d_attn: (1, 2, 3),
    At.mixed: (2, 1, 3),
    At.conv_z: (1, 3, 2),
    At.joined: (1, 2, 3),
}


def shape(dims, kind=low):
    return jax.ShapeDtypeStruct(tuple(dims), kind)


def after(value, *others):
    return lax.optimization_barrier((value, *others))[0]


class Plan:
    def __init__(self, starts, finishes, turns):
        self.starts, self.finishes, self.turns = starts, finishes, turns
        self.events, self.held = {}, {}

    def mark(self, name, value):
        self.events[name] = value
        return value

    def start(self, name, value):
        event = self.events.get(self.starts.get(name))
        return value if event is None else after(value, event)

    def finish(self, name, value):
        self.mark(name, value)
        self.held.setdefault(self.finishes.get(name), []).append(value)
        return value

    def enter(self, name, value):
        held = self.held.pop(name, ())
        return after(value, *held) if held else value

    def over_heads(self, name, parts):
        count = len(parts)
        found = [parts[0]] * count
        for j in self.turns.get(name, range(1, count)):
            sent = self.start(name + j, self.start(name, parts[j]))
            found[j] = self.finish(name + j, swap_with(sent, "heads", j))
        return found

    def gather(self, name, own):
        return self.over_heads(name, [own] * lax.axis_size("heads"))


def run_kernel(body, outs, *args, scratch=(), flops=0, leave=False, fetch=False, alias=None):
    whole = pl.BlockSpec(memory_space=pltpu.VMEM)
    source = pl.BlockSpec(memory_space=pl.ANY) if fetch else whole
    target = pl.BlockSpec() if leave else whole
    if fetch:
        count = len(args) if fetch is True else fetch
        held = [pltpu.with_memory_space_constraint(arg, pltpu.HBM) for arg in args[:count]]
        args = [*held, *args[count:]]
    traffic = sum(a.size * a.dtype.itemsize for a in args)
    traffic += sum(o.size * o.dtype.itemsize for o in outs)
    return pl.pallas_call(
        body,
        name=body.__name__,
        out_shape=tuple(outs),
        in_specs=[source] * len(args),
        out_specs=tuple([target] * len(outs)),
        scratch_shapes=[pltpu.VMEM(dims, kind) if dims else kind for dims, kind in scratch],
        input_output_aliases=alias or {},
        cost_estimate=pl.CostEstimate(flops=1, bytes_accessed=1, transcendentals=0),
        compiler_params=pltpu.CompilerParams(vmem_limit_bytes=VMEM_LIMIT),
    )(*args)


def dot(left, right, contract=(1, 0)):
    return lax.dot_general(
        left, right, (((contract[0],), (contract[1],)), ((), ())), preferred_element_type=wide
    )


def cat(parts, axis):
    return parts[0] if len(parts) == 1 else jnp.concatenate(parts, axis=axis)


def swap_with(value, axis, mask):
    pairs = [(source, source ^ mask) for source in range(lax.axis_size(axis))]
    return lax.ppermute(value, axis, pairs)


def over_core(value):
    return swap_with(value, "tiles", 1)


def over_x(value):
    return swap_with(value, "tiles", 2)


def over_y(value):
    return swap_with(value, "tiles", 4)


def fast_tiles():
    return lax.axis_size("tiles") == 8


BLOCKS = 8


def place_mask(place):
    half = BLOCKS // 2
    return ((place % half) * 2) | (place // half)


def block_at(place):
    if fast_tiles():
        return lax.axis_index("tiles") ^ place_mask(place)
    return place


def gather_first(block):
    found = [block, over_x(block), over_y(block), swap_with(block, "tiles", 6)]
    return found + [over_core(part) for part in found]


def stack_body(*refs):
    for i, ref in enumerate(refs[:-1]):
        refs[-1][i] = ref[...]


def stacked(*parts):
    return run_kernel(stack_body, [shape((len(parts), *parts[0].shape))], *parts)[0]


def stack_corner_body(*refs):
    *part_refs, upper_ref, lower_ref, out_ref = refs
    for i, ref in enumerate(part_refs):
        out_ref[i] = ref[...]
    cut = upper_ref.shape[0]
    out_ref[len(part_refs), 0:cut] = upper_ref[...]
    out_ref[len(part_refs), cut:] = lower_ref[...]


def rows_of(*stacks):
    return [ref.at[i] for ref in stacks for i in range(ref.shape[0])]


def gather_heads(own):
    return [own] + [swap_with(own, "heads", j) for j in range(1, lax.axis_size("heads"))]


def add_rows_body(keep_ref, got_ref, *out_refs):
    for i, out_ref in enumerate(out_refs):
        total = keep_ref[i].astype(wide) + got_ref[i].astype(wide)
        out_ref[...] = total.astype(out_ref.dtype)


def add_first_body(keep_ref, got_ref, *refs):
    more_refs, out_refs = refs[:3], refs[3:]
    rows = keep_ref.shape[1]
    for i, out_ref in enumerate(out_refs):
        total = keep_ref[i].astype(wide) + got_ref[i].astype(wide)
        out_ref[0:rows] = total.astype(out_ref.dtype)
        if i:
            out_ref[rows:] = more_refs[i - 1][...]


def add_cores(keep, got):
    return run_kernel(add_rows_body, [shape(keep.shape[1:])] * 4, keep, got)


def over_corner(value):
    return swap_with(value, "tiles", 6)


def gelu_parts(inputs):
    bell = 0.5 * (1.0 + lax.erf(inputs * inv_root_two))
    return inputs * bell, bell + inputs * inv_root_two_pi * jnp.exp(-0.5 * inputs * inputs)


def normed(values):
    centred = values - jnp.mean(values, axis=-1, keepdims=True)
    inv_std = lax.rsqrt(jnp.mean(centred * centred, axis=-1, keepdims=True) + norm_eps)
    return centred * inv_std, inv_std


def total_of(refs, at=Ellipsis):
    total = refs[0][at].astype(wide)
    for ref in refs[1:]:
        total = total + ref[at].astype(wide)
    return total


def copies(pairs, sems):
    started = [
        pltpu.make_async_copy(source, target, sems.at[i])
        for i, (source, target) in enumerate(pairs)
    ]
    for copy in started:
        copy.start()
    for copy in started:
        copy.wait()


def lane_blocks(source, target, start):
    rows, lanes = source.shape
    return [
        (
            source.at[:, pl.ds(m * LANES, LANES)],
            target.at[pl.ds(start + m * rows, rows)],
        )
        for m in range(lanes // LANES)
    ]


def pack_first_body(conv_ref, gate_ref, join_ref, out_w_ref, first_ref, cross_ref, sems):
    at = conv_ref.shape[0]
    pairs = [(conv_ref, first_ref.at[pl.ds(0, at)])]
    pairs += lane_blocks(gate_ref, first_ref, at)
    pairs += lane_blocks(gate_ref, cross_ref, 0)
    rows = join_ref.shape[0]
    pairs += [(join_ref, cross_ref.at[pl.ds(rows, rows)])]
    pairs += [(out_w_ref, cross_ref.at[pl.ds(2 * rows, rows)])]
    copies(pairs, sems)


def pack_rest_body(attn_ref, up_ref, down_ref, *refs):
    cross_refs, (second_ref, third_ref, fourth_ref, sems) = refs[:-4], refs[-4:]
    rows = cross_refs[0].shape[0] // 3
    heads = len(cross_refs)
    pairs = []
    for j, ref in enumerate(cross_refs):
        pairs += [(ref.at[pl.ds(rows, rows)], second_ref.at[pl.ds(j * rows, rows)])]
        pairs += [(ref.at[pl.ds(2 * rows, rows)], third_ref.at[pl.ds(j * rows, rows)])]
        if j:
            at = (j - 1) * rows
            pairs += [(ref.at[pl.ds(0, rows)], fourth_ref.at[pl.ds(at, rows)])]
    for s in range(3):
        pairs += lane_blocks(attn_ref.at[s], second_ref, (heads + s) * rows)
    pairs += lane_blocks(up_ref, third_ref, heads * rows)
    rows = down_ref.shape[0]
    pairs += [(down_ref, third_ref.at[pl.ds(third_ref.shape[0] - rows, rows)])]
    copies(pairs, sems)


def third_refs(refs, results):
    count = len(refs) - results
    if count == 2:
        pieces = rows_of(*refs[:2])
        return pieces, pieces, refs[2:]
    stack, upper, lower, core_stack, core_upper, core_lower = refs[:6]
    own, core = rows_of(stack), rows_of(core_stack)
    return own + [upper] + core + [core_upper], own + [lower] + core + [core_lower], refs[6:]


def views(refs, start, rows):
    return [ref if ref.shape[0] == rows else ref.at[pl.ds(start, rows)] for ref in refs]


def whole_number(value, parts):
    return jnp.floor((value + 0.5) * (1.0 / parts))


def pool_body(sides_ref, maps_ref, pooled_ref, pool_ref, hold, sems):
    copy = pltpu.make_async_copy(maps_ref, hold, sems.at[0])
    copy.start()
    image = lax.axis_index("tiles") // 4
    cells, pixels = pool_ref.shape[1:]
    cell = lax.broadcasted_iota(jnp.int32, (cells, pixels), 0).astype(wide)
    pixel = lax.broadcasted_iota(jnp.int32, (cells, pixels), 1).astype(wide)
    cell_row = whole_number(cell, TILE)
    pixel_row = whole_number(pixel, HR_TILE)
    spots = (
        (cell_row, pixel_row),
        (cell - TILE * cell_row, pixel - HR_TILE * pixel_row),
    )
    for batch in range(pool_ref.shape[0]):
        side = sides_ref[batch, image].astype(wide)
        weights = 1.0
        for cell_at, pixel_at in spots:
            begin = whole_number(cell_at * side, GRID)
            end = whole_number((cell_at + 1.0) * side + (GRID - 1.0), GRID)
            inside = jnp.logical_and(pixel_at >= begin, pixel_at < end)
            weights = weights * jnp.where(inside, 1.0 / (end - begin), 0.0)
        pool_ref[batch] = weights.astype(low)
    copy.wait()
    for batch in range(pool_ref.shape[0]):
        pooled = dot(pool_ref[batch], hold[batch])
        pooled_ref[batch * cells : (batch + 1) * cells] = pooled.astype(low)


def wide_rows(refs, start, count):
    return cat(
        [
            cat([ref[start + m * LANES : start + (m + 1) * LANES] for m in range(count)], 1)
            for ref in refs
        ],
        0,
    )


def wide_cols(refs, start, rows):
    return cat([ref[start : start + rows] for ref in refs], 1)


def relative_body(*refs):
    count = len(refs[:-1]) // 3
    sources, outs, found = refs[:count], refs[count : 2 * count], refs[2 * count : -1]
    copies(list(zip(sources, found)), refs[-1])
    for source, target in zip(found, outs):
        for place in range(BLOCKS):
            lanes = pl.ds(pl.multiple_of(LANES * block_at(place), LANES), LANES)
            target[:, place * LANES : (place + 1) * LANES] = source[:, lanes]


def conv_body(pooled_ref, *refs):
    piece_refs, (whole_ref, *out_refs) = refs[:BLOCKS], refs[BLOCKS:]
    head = lax.axis_index("heads")
    for place, ref in enumerate(piece_refs):
        whole_ref[block_at(place)] = ref[0 : whole_ref.shape[1]]
    per_chunk = BLOCKS // len(out_refs)
    for j, out_ref in enumerate(out_refs):
        first = per_chunk * (head ^ j)
        chunk = cat([whole_ref[first + i] for i in range(per_chunk)], 1)
        out_ref[...] = dot(pooled_ref[...], chunk).astype(low)


def edge_flags():
    tile = lax.axis_index("tiles")
    return (tile & 1) == 0, (tile & 2) == 0


def send_edges(grid, hold_ref, col_ref, row_ref, corner_ref):
    right, lower = edge_flags()
    cells = TILE * TILE
    batches = grid.shape[0] // cells
    count = batches * TILE
    for at in range(count):
        begin = at * TILE
        end = begin + TILE - 1
        hold_ref[at : at + 1] = jnp.where(right, grid[end : end + 1], grid[begin : begin + 1])
    col_ref[...] = hold_ref[0:count].astype(low)
    hold_ref[...] = jnp.zeros(hold_ref.shape, wide)
    for batch in range(batches):
        base = batch * cells
        bottom = grid[base + cells - TILE : base + cells]
        top = grid[base : base + TILE]
        edge = jnp.where(lower, bottom, top)
        hold_ref[batch * PAD : batch * PAD + TILE] = edge
    row_ref[...] = hold_ref[...].astype(low)
    hold_ref[...] = jnp.zeros(hold_ref.shape, wide)
    for batch in range(batches):
        base = batch * cells
        ends = [
            jnp.where(right, grid[at + TILE - 1 : at + TILE], grid[at : at + 1])
            for at in (base + cells - TILE, base)
        ]
        hold_ref[batch : batch + 1] = jnp.where(lower, ends[0], ends[1])
    corner_ref[...] = hold_ref[0:PAD].astype(low)


def fill_padded(grid, col_ref, row_ref, corner_ref, pad_ref, hold_ref):
    right, lower = edge_flags()
    cells = TILE * TILE
    batches = grid.shape[0] // cells
    per_batch = (TILE + 2) * PAD
    pad_ref[...] = jnp.zeros(pad_ref.shape, wide)
    hold_ref[0 : batches * TILE] = col_ref[...].astype(wide)
    for batch in range(batches):
        for a in range(TILE):
            at = batch * per_batch + (a + 1) * PAD
            source = batch * cells + a * TILE
            pad_ref[at + 1 : at + 1 + TILE] = grid[source : source + TILE]
            got = hold_ref[batch * TILE + a : batch * TILE + a + 1]
            zero = jnp.zeros_like(got)
            pad_ref[at : at + 1] = jnp.where(right, zero, got)
            pad_ref[at + TILE + 1 : at + TILE + 2] = jnp.where(right, got, zero)
    rows = row_ref[...].astype(wide)
    corners = corner_ref[...].astype(wide)
    for batch in range(batches):
        got = rows[batch * PAD : batch * PAD + TILE]
        corner = corners[batch : batch + 1]
        zero = jnp.zeros_like(got)
        nil = jnp.zeros_like(corner)
        for at, used in (
            (batch * per_batch, jnp.logical_not(lower)),
            (batch * per_batch + (TILE + 1) * PAD, lower),
        ):
            pad_ref[at + 1 : at + 1 + TILE] = jnp.where(used, got, zero)
            left = jnp.logical_and(used, jnp.logical_not(right))
            pad_ref[at : at + 1] = jnp.where(left, corner, nil)
            pad_ref[at + TILE + 1 : at + TILE + 2] = jnp.where(
                jnp.logical_and(used, right), corner, nil
            )


def map_body(*refs):
    heads = lax.axis_size("heads")
    part_refs, (map_ref, col_ref, row_ref, corner_ref, grid, hold) = refs[:heads], refs[heads:]
    mapped = total_of(part_refs).astype(low)
    map_ref[...] = mapped
    grid[...] = mapped.astype(wide)
    send_edges(grid, hold, col_ref, row_ref, corner_ref)


def gate_body(tok_ref, *refs):
    piece_refs, (gate_ref,) = refs[:BLOCKS], refs[BLOCKS:]
    chans = gate_ref.shape[1]
    start = piece_refs[0].shape[0] - chans
    weights = wide_rows(views(piece_refs, start, chans), 0, chans // LANES)
    gate_ref[...] = jnp.tanh(dot(tok_ref[...], weights)).astype(wide)


def own_rows(ref, at, rows):
    return ref[pl.ds(pl.multiple_of(rows * at, 8), rows)]


def write_chunks(total_ref, out_refs):
    head = lax.axis_index("heads")
    rows = total_ref.shape[0] // len(out_refs)
    for j, out_ref in enumerate(out_refs):
        out_ref[...] = own_rows(total_ref, head ^ j, rows).astype(low)


def whole_rows(part_refs, hold_ref, rows):
    head = lax.axis_index("heads")
    for j, ref in enumerate(part_refs):
        to = pl.ds(pl.multiple_of(rows * (head ^ j), 8), rows)
        hold_ref[to] = ref[...].astype(wide)[:rows]
    return hold_ref[...].astype(low)


def depthwise_body(map_ref, col_ref, row_ref, corner_ref, dw_ref, gate_ref, *refs):
    pad_ref, spread_ref, joined_ref, grid, hold = refs
    grid[...] = map_ref[...].astype(wide)
    fill_padded(grid, col_ref, row_ref, corner_ref, pad_ref, hold)
    cells = TILE * TILE
    batches = grid.shape[0] // cells
    per_batch = (TILE + 2) * PAD
    for batch in range(batches):
        for a in range(TILE):
            running = jnp.broadcast_to(dw_ref[9:10], (TILE, grid.shape[1]))
            for tap in range(9):
                row, col = divmod(tap, 3)
                at = batch * per_batch + (a + row) * PAD + col
                running = running + dw_ref[tap : tap + 1] * pad_ref[at : at + TILE]
            to = batch * cells + a * TILE
            spread_ref[to : to + TILE] = running
    joined_ref[...] = (gate_ref[...] * spread_ref[...]).astype(low)


def project_all(rows_refs, piece_refs, base_ref, sum_ref):
    rows = cat([ref[...] for ref in rows_refs], 1)
    for pair in range(BLOCKS // 2):
        weights = wide_cols(piece_refs[2 * pair : 2 * pair + 2], 0, rows.shape[1])
        lanes = slice(2 * pair * LANES, 2 * (pair + 1) * LANES)
        sum_ref[:, lanes] = base_ref[:, lanes].astype(wide) + dot(rows, weights)


def join_body(tok_ref, gain_ref, bias_ref, *refs):
    heads = lax.axis_size("heads")
    part_refs, piece_refs = refs[:heads], rows_of(*refs[heads : heads + 2])
    first_ref, all_ref, query_ref, kv_ref = refs[heads + 2 :]
    chans = query_ref.shape[1]
    join_refs = views(piece_refs, 0, heads * chans)
    attn_refs = views(piece_refs, heads * chans, 3 * chans)
    project_all(part_refs, join_refs, tok_ref, first_ref)
    rows = (normed(first_ref[...])[0] * gain_ref[0:1] + bias_ref[0:1]).astype(low)
    all_ref[...] = rows
    count = chans // LANES
    for s in range(3):
        result = dot(all_ref[...], wide_rows(attn_refs, s * chans, count)).astype(low)
        if s == 0:
            query_ref[...] = result
        else:
            kv_ref[:, (s - 1) * chans : s * chans] = result


def head_masks(rows):
    lane = lax.broadcasted_iota(jnp.int32, (rows, LANES), 1)
    return [lane < HEAD_DIM, lane >= HEAD_DIM]


def softmax_parts(query, keys):
    scores = dot(query, keys, (1, 1)) * HEAD_DIM ** (-0.5)
    expo = jnp.exp(scores - jnp.max(scores, axis=-1, keepdims=True))
    return expo / jnp.sum(expo, axis=-1, keepdims=True)


def attend_body(query_ref, *refs):
    kv_refs, (mixed_ref,) = refs[:4], refs[4:]
    chans = query_ref.shape[1]
    cells = TILE * TILE
    masks = head_masks(cells)
    for batch in range(query_ref.shape[0] // cells):
        at = slice(batch * cells, (batch + 1) * cells)
        for pair in range(chans // LANES):
            lanes = slice(pair * LANES, (pair + 1) * LANES)
            value_lanes = slice(chans + pair * LANES, chans + (pair + 1) * LANES)
            keys = cat([ref[at, lanes] for ref in kv_refs], 0)
            values = cat([ref[at, value_lanes] for ref in kv_refs], 0)
            query = query_ref[at, lanes]
            found = []
            for mask in masks:
                probs = softmax_parts(jnp.where(mask, query, jnp.zeros_like(query)), keys)
                found.append(dot(probs.astype(low), values))
            mixed_ref[at, lanes] = jnp.where(masks[0], found[0], found[1]).astype(low)


HIDDEN_STEP = 256


def ffn_body(upstream_ref, first_ref, gain_ref, bias_ref, *refs):
    heads = lax.axis_size("heads")
    part_refs = refs[:heads]
    out_pieces, piece_refs, refs = third_refs(refs[heads:], 5 + heads)
    second_ref, all_ref, hidden_ref, d_hidden_ref = refs[:4]
    out_refs, total_ref = refs[4:-1], refs[-1]
    hidden_width = hidden_ref.shape[1]
    depth = heads * part_refs[0].shape[1]
    start = piece_refs[0].shape[0] - 2 * hidden_width
    piece_refs = views(piece_refs, start, 2 * hidden_width)
    project_all(part_refs, views(out_pieces, 0, depth), first_ref, second_ref)
    rows = normed(second_ref[...])[0] * gain_ref[1:2] + bias_ref[1:2]
    all_ref[...] = rows.astype(low)
    total_ref[...] = jnp.zeros(total_ref.shape, wide)
    per_step = HIDDEN_STEP // LANES

    def step(m, carry):
        at = pl.multiple_of(m * HIDDEN_STEP, HIDDEN_STEP)
        up = cat(
            [
                cat([ref[pl.ds(at + i * LANES, LANES)] for i in range(per_step)], 1)
                for ref in piece_refs
            ],
            0,
        )
        down = cat([ref[pl.ds(hidden_width + at, HIDDEN_STEP)] for ref in piece_refs], 1)
        value, slope = gelu_parts(dot(all_ref[...], up))
        hidden_ref[:, pl.ds(at, HIDDEN_STEP)] = value.astype(low)
        d_hidden = (dot(upstream_ref[...], down, (1, 1)) * slope).astype(low)
        d_hidden_ref[:, pl.ds(at, HIDDEN_STEP)] = d_hidden
        total_ref[...] += dot(d_hidden, up, (1, 1))
        return carry

    lax.fori_loop(0, hidden_width // HIDDEN_STEP, step, 0)
    write_chunks(total_ref, out_refs)


def down_body(hidden_ref, *refs):
    _, piece_refs, refs = third_refs(refs, 1 + lax.axis_size("heads"))
    out_refs, total_ref = refs[:-1], refs[-1]
    width = hidden_ref.shape[1]
    piece_refs = views(piece_refs, piece_refs[0].shape[0] - 2 * width, 2 * width)
    for pair in range(BLOCKS // 2):
        weights = wide_cols(piece_refs[2 * pair : 2 * pair + 2], width, width)
        lanes = slice(2 * pair * LANES, 2 * (pair + 1) * LANES)
        total_ref[:, lanes] = dot(hidden_ref[...], weights)
    write_chunks(total_ref, out_refs)


def whole_cols_body(base_ref, *refs):
    part_refs, out_ref = refs[:-1], refs[-1]
    head = lax.axis_index("heads")
    shard = out_ref.shape[0]
    for place in range(BLOCKS):
        lanes = slice(place * LANES, (place + 1) * LANES)
        mine = base_ref[pl.ds(pl.multiple_of(shard * head, 8), shard), lanes]
        total = mine + total_of(part_refs, (slice(None), lanes))
        to = pl.ds(pl.multiple_of(LANES * block_at(place), LANES), LANES)
        out_ref[:, to] = total.astype(low)


def block_out_body(*refs):
    part_refs, out_ref, hold = refs[:-2], refs[-2], refs[-1]
    head = lax.axis_index("heads")
    shard = out_ref.shape[0] // len(part_refs)
    for j, ref in enumerate(part_refs):
        to = pl.ds(pl.multiple_of(shard * (head ^ j), 8), shard)
        chans = ref.shape[1]
        rows = ref[...].astype(wide)[out_ref.shape[0] :]
        for m in range(out_ref.shape[1] // chans):
            hold[to, m * chans : (m + 1) * chans] = rows[m * shard : (m + 1) * shard]
    out_ref[...] = hold[...].astype(out_ref.dtype)


def tokens_grad_body(d_first_ref, *refs):
    heads = lax.axis_size("heads")
    part_refs, own_refs = refs[:heads], refs[heads : heads + BLOCKS]
    other_refs, out_ref = rows_of(*refs[heads + BLOCKS : -1]), refs[-1]
    chans = part_refs[0].shape[1]
    own_refs = views(own_refs, own_refs[0].shape[0] - chans, chans)
    rows = cat([ref[0 : out_ref.shape[0]] for ref in part_refs], 1)
    count = chans // LANES
    for pair in range(BLOCKS // 2):
        both = slice(2 * pair, 2 * pair + 2)
        weights = [wide_rows(own_refs[both], 0, count)]
        weights += [wide_rows(other_refs[both], j * chans, count) for j in range(heads - 1)]
        lanes = slice(2 * pair * LANES, 2 * (pair + 1) * LANES)
        grad = d_first_ref[:, lanes].astype(wide) + dot(rows, cat(weights, 1), (1, 1))
        for i in range(2):
            block = block_at(2 * pair + i)
            to = pl.ds(pl.multiple_of(LANES * block, LANES), LANES)
            out_ref[:, to] = grad[:, i * LANES : (i + 1) * LANES]


def norm_back_body(values_ref, base_ref, gain_ref, *refs):
    part_refs, (sum_ref, low_ref) = refs[:-2], refs[-2:]
    rows = sum_ref.shape[0]
    head = lax.axis_index("heads")
    scaled, inv_std = normed(own_rows(values_ref, head, rows))
    upstream = total_of(part_refs)
    weighted = upstream * gain_ref[...]
    inner = (
        weighted
        - jnp.mean(weighted, axis=-1, keepdims=True)
        - scaled * jnp.mean(weighted * scaled, axis=-1, keepdims=True)
    )
    base = base_ref[...] if base_ref.shape[0] == rows else own_rows(base_ref, head, rows)
    total = base.astype(wide) + inv_std * inner
    sum_ref[...] = total
    sums = [
        jnp.sum(upstream * scaled, axis=0, keepdims=True),
        jnp.sum(upstream, axis=0, keepdims=True),
    ]
    coarse = [each.astype(low).astype(wide) for each in sums]
    fine = [each - near for each, near in zip(sums, coarse)]
    extra = low_ref.shape[0] - rows - 4
    blank = jnp.zeros((extra, total.shape[1]), wide)
    low_ref[...] = cat([total, *coarse, *fine, blank], 0).astype(low)


def sums_from(part_refs, sums_ref, shard):
    found = total_of(part_refs, slice(shard, shard + 8))
    sums_ref[...] = found[0:2] + found[2:4]


def attend_back_body(query_ref, *refs):
    heads = lax.axis_size("heads")
    kv_refs, part_refs = refs[:4], refs[4 : 4 + heads]
    piece_refs, _, refs = third_refs(refs[4 + heads :], 7)
    all_ref, d_query_ref, keep_ref, send_ref, sums_ref, d_mixed_ref, hold = refs
    chans = query_ref.shape[1]
    cells = TILE * TILE
    scale = HEAD_DIM ** (-0.5)
    shard = all_ref.shape[0] // heads
    all_ref[...] = whole_rows(part_refs, hold, shard)
    sums_from(part_refs, sums_ref, shard)
    weights = wide_cols(views(piece_refs, 0, heads * chans), 0, chans)
    d_mixed_ref[...] = dot(all_ref[...], weights, (1, 1)).astype(low)
    masks = head_masks(cells)
    for batch in range(query_ref.shape[0] // cells):
        at = slice(batch * cells, (batch + 1) * cells)
        for pair in range(chans // LANES):
            lanes = slice(pair * LANES, (pair + 1) * LANES)
            value_lanes = slice(chans + pair * LANES, chans + (pair + 1) * LANES)
            keys = cat([ref[at, lanes] for ref in kv_refs], 0)
            values = cat([ref[at, value_lanes] for ref in kv_refs], 0)
            query = query_ref[at, lanes]
            d_mixed = d_mixed_ref[at, lanes]
            d_queries = []
            d_keys = 0.0
            d_values = 0.0
            for mask in masks:
                own_query = jnp.where(mask, query, jnp.zeros_like(query))
                own_mixed = jnp.where(mask, d_mixed, jnp.zeros_like(d_mixed))
                probs = softmax_parts(own_query, keys)
                d_probs = dot(own_mixed, values, (1, 1))
                inner = jnp.sum(probs * d_probs, axis=-1, keepdims=True)
                d_scores = (probs * (d_probs - inner)).astype(low)
                d_queries.append(dot(d_scores, keys))
                d_keys = d_keys + dot(d_scores, own_query, (0, 0))
                d_values = d_values + dot(probs.astype(low), own_mixed, (0, 0))
            d_query = jnp.where(masks[0], d_queries[0], d_queries[1]) * scale
            d_query_ref[at, lanes] = d_query.astype(low)
            d_keys = d_keys * scale
            for i in range(4):
                target = (keep_ref, send_ref)[i // 2]
                own = slice(i * cells, (i + 1) * cells)
                target[i % 2, at, lanes] = d_keys[own].astype(target.dtype)
                target[i % 2, at, value_lanes] = d_values[own].astype(target.dtype)


def add_pair_body(keep_ref, got_ref, own_ref, send_ref):
    own_ref[...] = keep_ref[0] + got_ref[0].astype(wide)
    send_ref[...] = (keep_ref[1] + got_ref[1].astype(wide)).astype(low)


def d_qkv_body(d_query_ref, own_ref, got_ref, *refs):
    piece_refs, (d_qkv_ref, *out_refs, total_ref) = rows_of(*refs[:2]), refs[2:]
    chans = d_query_ref.shape[1]
    d_qkv_ref[:, :chans] = d_query_ref[...]
    d_qkv_ref[:, chans:] = (own_ref[...] + got_ref[...].astype(wide)).astype(low)
    d_qkv = d_qkv_ref[...]
    count = 3 * chans // LANES
    piece_refs = views(piece_refs, lax.axis_size("heads") * chans, 3 * chans)
    for pair in range(BLOCKS // 2):
        weights = wide_rows(piece_refs[2 * pair : 2 * pair + 2], 0, count)
        lanes = slice(2 * pair * LANES, 2 * (pair + 1) * LANES)
        total_ref[:, lanes] = dot(d_qkv, weights, (1, 1))
    write_chunks(total_ref, out_refs)


def gate_back_body(gate_ref, spread_ref, result_ref, *refs):
    heads = lax.axis_size("heads")
    head = lax.axis_index("heads")
    part_refs, piece_refs = refs[:heads], rows_of(*refs[heads : heads + 2])
    all_ref, d_gate_ref, tail_ref, grid_ref, sums_ref, *edge_refs, edge, hold = refs[heads + 2 :]
    shard = all_ref.shape[0] // heads
    all_ref[...] = whole_rows(part_refs, hold, shard)
    sums_from(part_refs, sums_ref, shard)
    chans = gate_ref.shape[1]
    weights = wide_cols(views(piece_refs, 0, heads * chans), 0, chans)
    d_joined = dot(all_ref[...], weights, (1, 1))
    gate = gate_ref[...]
    d_gate = d_joined * spread_ref[...] * (1.0 - gate * gate)
    d_gate_ref[...] = d_gate.astype(low)
    result = result_ref[...].astype(wide)
    folded = [result[:, m * chans : (m + 1) * chans] for m in range(result.shape[1] // chans)]
    tail_ref[...] = cat([d_gate, *folded], 0).astype(low)
    grid_ref[...] = d_joined * gate
    send_edges(grid_ref, edge, *edge_refs)


def depthwise_back_body(grid_ref, col_ref, row_ref, corner_ref, dw_ref, out_ref, d_pad, hold, flat):
    fill_padded(grid_ref, col_ref, row_ref, corner_ref, d_pad, hold)
    cells = TILE * TILE
    per_batch = (TILE + 2) * PAD
    chans = grid_ref.shape[1]
    for batch in range(grid_ref.shape[0] // cells):
        for a in range(TILE):
            running = jnp.zeros((TILE, chans), wide)
            for tap in range(9):
                row, col = divmod(tap, 3)
                at = batch * per_batch + (a + 2 - row) * PAD + 2 - col
                running = running + dw_ref[tap : tap + 1] * d_pad[at : at + TILE]
            flat[batch * cells + a * TILE : batch * cells + (a + 1) * TILE] = running
    out_ref[...] = flat[...].astype(low)


def taps_body(grid_ref, pad_ref, ln1_ref, ln2_ref, small_ref):
    cells = TILE * TILE
    per_batch = (TILE + 2) * PAD
    chans = grid_ref.shape[1]
    sums = [jnp.zeros((TILE, chans), wide) for _ in range(10)]
    for batch in range(grid_ref.shape[0] // cells):
        for a in range(TILE):
            own = grid_ref[batch * cells + a * TILE : batch * cells + (a + 1) * TILE]
            for tap in range(9):
                row, col = divmod(tap, 3)
                at = batch * per_batch + (a + row) * PAD + col
                sums[tap] = sums[tap] + own * pad_ref[at : at + TILE]
            sums[9] = sums[9] + own
    small_ref[...] = jnp.zeros(small_ref.shape, wide)
    for place in range(BLOCKS):
        lanes = slice(place * LANES, (place + 1) * LANES)
        to = pl.ds(pl.multiple_of(LANES * block_at(place), LANES), LANES)
        small_ref[0:2, to] = ln1_ref[:, lanes]
        small_ref[2:4, to] = ln2_ref[:, lanes]
    per_row = small_ref.shape[1] // chans
    for tap in range(10):
        row, lane = 4 + tap // per_row, tap % per_row * chans
        total = jnp.sum(sums[tap], axis=0, keepdims=True)
        small_ref[row : row + 1, lane : lane + chans] = total


def small_final_body(own_ref, got_ref, ln1_ref, ln2_ref, taps_ref):
    total = own_ref[...] + got_ref[...]
    ln1_ref[...] = total[0:2]
    ln2_ref[...] = total[2:4]
    chans = taps_ref.shape[1]
    per_row = total.shape[1] // chans
    for tap in range(10):
        row, lane = 4 + tap // per_row, tap % per_row * chans
        taps_ref[tap : tap + 1] = total[row : row + 1, lane : lane + chans]


def conv_back_body(pool_ref, whole_ref, *refs):
    heads = lax.axis_size("heads")
    head = lax.axis_index("heads")
    part_refs, (hires_ref,) = refs[:heads], refs[heads:]
    per_chunk = BLOCKS // heads
    d_pooled = 0.0
    for j, ref in enumerate(part_refs):
        first = per_chunk * (head ^ j)
        chunk = cat([whole_ref[first + i] for i in range(per_chunk)], 1)
        d_pooled = d_pooled + dot(ref[...], chunk, (1, 1))
    d_pooled = d_pooled.astype(low)
    batches = pool_ref.shape[0]
    rows = pool_ref.shape[1]
    for batch in range(batches):
        own = d_pooled[batch * rows : (batch + 1) * rows]
        hires_ref[batch] = dot(pool_ref[batch], own, (0, 0))


def conv_grad_body(pooled_ref, *refs):
    heads = lax.axis_size("heads")
    head = lax.axis_index("heads")
    part_refs, (keep_ref, send_ref, hold) = refs[:heads], refs[heads + 2 :]
    per_chunk = BLOCKS // heads
    for j, ref in enumerate(part_refs):
        grad = dot(pooled_ref[...], ref[...], (0, 0)).astype(low)
        for i in range(per_chunk):
            hold[per_chunk * (head ^ j) + i] = grad[:, i * LANES : (i + 1) * LANES]
    for place in range(BLOCKS):
        target = place_refs(keep_ref, send_ref, place)
        target[0 : hold.shape[1]] = hold[block_at(place)]


def place_refs(keep_ref, send_ref, place):
    return ((keep_ref, send_ref)[place // 4]).at[place % 4]


def row_grad(left_ref, right, keep_ref, send_ref, start):
    count = right.shape[1] // LANES
    for place in range(BLOCKS):
        lanes = slice(place * LANES, (place + 1) * LANES)
        grad = dot(left_ref[:, lanes], right, (0, 0)).astype(low)
        target = place_refs(keep_ref, send_ref, place)
        for m in range(count):
            target[start + m * LANES : start + (m + 1) * LANES] = grad[
                :, m * LANES : (m + 1) * LANES
            ]


def col_grad(left_ref, right_ref, keep_ref, send_ref, start):
    width = left_ref.shape[1]
    for m in range(width // LANES):
        grad = dot(left_ref[:, m * LANES : (m + 1) * LANES], right_ref[...], (0, 0)).astype(low)
        for place in range(BLOCKS):
            target = place_refs(keep_ref, send_ref, place)
            target[start + m * LANES : start + (m + 1) * LANES] = grad[
                :, place * LANES : (place + 1) * LANES
            ]


def pair_grad_body(row_left, row_right, col_left, col_right, keep_ref, send_ref):
    width = row_right.shape[1]
    start = keep_ref.shape[1] - width - col_left.shape[1]
    row_grad(row_left, row_right[...], keep_ref, send_ref, start)
    col_grad(col_left, col_right, keep_ref, send_ref, start + width)


def final_rows(refs, start, count):
    return cat(
        [total_of(refs, slice(start + m * LANES, start + (m + 1) * LANES)) for m in range(count)],
        1,
    )


def last_final_body(*refs):
    first_refs, rest_ref, results = refs[:4], refs[4], refs[5:]
    conv_ref, gate_ref, join_ref, attn_ref, out_ref = results
    rows, chans = conv_ref.shape[0], gate_ref.shape[1]
    conv_ref[...] = total_of(first_refs, slice(0, rows))
    gate_ref[...] = final_rows(first_refs, rows, chans // LANES)
    join_ref[...] = total_of(first_refs, slice(rows + chans, rows + 2 * chans))
    at = first_refs[0].shape[0]
    behind = pl.ds(at, rest_ref.shape[0])
    part_refs = [rest_ref, *[ref.at[behind] for ref in first_refs[1:]]]
    for s in range(3):
        attn_ref[s] = final_rows(part_refs, s * chans, chans // LANES)
    out_ref[...] = total_of(part_refs, slice(3 * chans, 3 * chans + out_ref.shape[0]))


def up_down_final_body(*refs):
    part_refs, (up_ref, down_ref) = refs[:-2], refs[-2:]
    width = up_ref.shape[1]
    up_ref[...] = final_rows(part_refs, 0, width // LANES)
    down_ref[...] = total_of(part_refs, slice(width, width + down_ref.shape[0]))


def unpack_rows(packed, count):
    places = packed.shape[0]
    return (
        packed.reshape(places, count, LANES, LANES)
        .transpose(0, 2, 1, 3)
        .reshape(places * LANES, count * LANES)
    )


def unpack_cols(packed):
    return packed.transpose(1, 0, 2).reshape(packed.shape[1], -1)


def pack_rows(weights):
    count = weights.shape[1] // LANES
    return (
        weights.reshape(BLOCKS, LANES, count, LANES)
        .transpose(0, 2, 1, 3)
        .reshape(BLOCKS, count * LANES, LANES)
    )


def pack_cols(weights):
    return weights.reshape(weights.shape[0], BLOCKS, LANES).transpose(1, 0, 2)


def scatter_dim(grad, axis):
    return lax.psum_scatter(grad, "tiles", scatter_dimension=axis, tiled=True).astype(wide)


def local(
    vit_tokens,
    hires_maps,
    map_sizes,
    out_grad,
    ln_gain,
    ln_bias,
    dw_params,
    conv_w,
    gate_w,
    join_w,
    attn_in_w,
    out_w,
    up_w,
    down_w,
):
    tiles = lax.axis_size("tiles")
    heads = lax.axis_size("heads")
    fast = fast_tiles()
    batches, rows, width = vit_tokens.shape
    total = batches * rows
    shard = total // heads
    chans = dw_params.shape[1]
    hidden_width = down_w.shape[0]
    pixels, hires_chans = hires_maps.shape[1:]
    dma = pltpu.SemaphoreType.DMA
    plan = Plan(STARTS, FINISHES, TURNS)

    cross = heads * chans
    lanes_of = chans // LANES
    if fast:
        first_own, cross_own = run_kernel(
            pack_first_body,
            [shape((hires_chans + chans, LANES)), shape((3 * chans, LANES))],
            conv_w,
            gate_w,
            join_w,
            out_w,
            scratch=[((), dma((3 + 2 * lanes_of,)))],
            fetch=True,
        )
        found = [first_own, over_x(first_own), over_y(first_own), over_corner(first_own)]
        for name, piece in zip((At.first_x, At.first_y, At.first_corner), found[1:]):
            plan.mark(name, piece)
    else:

        def whole_of(weights, axis):
            return lax.all_gather(weights, "tiles", axis=axis, tiled=True)

        def halves(*packed):
            joint = jnp.concatenate(packed, axis=1)
            return joint[: BLOCKS // 2], joint[BLOCKS // 2 :]

        gate_all = [pack_rows(each) for each in gather_heads(whole_of(gate_w, 0))]
        join_all = [pack_cols(each) for each in gather_heads(whole_of(join_w, 1))]
        out_all = [pack_cols(each) for each in gather_heads(whole_of(out_w, 1))]
        attn_whole = whole_of(attn_in_w, 1)
        first_stack = jnp.concatenate([pack_cols(whole_of(conv_w, 1)), gate_all[0]], axis=1)
        first_pieces = [first_stack[p] for p in range(BLOCKS)]
        second = halves(*join_all, *[pack_rows(each) for each in attn_whole])
        third = halves(
            *out_all,
            pack_rows(whole_of(up_w, 0)),
            pack_cols(whole_of(down_w, 1)),
        )
        fourth = halves(*gate_all[1:])

    inputs = (
        vit_tokens.reshape(total, width),
        out_grad.reshape(total, width),
        ln_gain,
        ln_bias,
    )
    tokens, upstream, gains, biases = run_kernel(
        relative_body,
        [shape(each.shape, each.dtype) for each in inputs],
        *inputs,
        scratch=[(each.shape, each.dtype) for each in inputs] + [((), dma((4,)))],
        fetch=True,
    )
    upstream_wide = upstream.astype(wide)
    plan.mark(At.relative, tokens)

    pooled, pools = pl.pallas_call(
        pool_body,
        out_shape=(shape((total, hires_chans)), shape((batches, rows, pixels))),
        in_specs=[
            pl.BlockSpec(memory_space=pltpu.SMEM),
            pl.BlockSpec(memory_space=pl.ANY),
        ],
        out_specs=tuple([pl.BlockSpec(memory_space=pltpu.VMEM)] * 2),
        scratch_shapes=[pltpu.VMEM(hires_maps.shape, low), dma((1,))],
        compiler_params=pltpu.CompilerParams(vmem_limit_bytes=VMEM_LIMIT),
    )(map_sizes, pltpu.with_memory_space_constraint(hires_maps, pltpu.HBM))
    plan.mark(At.pool, pooled)
    if fast:
        first_pieces = list(found)
        events = (At.first_own_core, At.first_x_core, At.first_y_core, At.first_corner_core)
        for name, piece in zip(events, found):
            first_pieces.append(plan.mark(name, over_core(plan.start(name, piece))))
        cross_parts = plan.gather(At.cross, cross_own)

    conv_whole, *conv_parts = run_kernel(
        conv_body,
        [shape((BLOCKS, hires_chans, LANES))] + [shape((total, chans))] * heads,
        plan.enter(At.conv, after(pooled, tokens)),
        *first_pieces,
        flops=2 * total * hires_chans * width,
    )
    edge_shapes = [
        shape((batches * TILE, chans)),
        shape((batches * PAD, chans)),
        shape((PAD, chans)),
    ]
    edge_scratch = ((batches * PAD, chans), wide)
    grid_scratch = ((total, chans), wide)
    pad_dims = (batches * (TILE + 2) * PAD, chans)
    plan.mark(At.conv, conv_whole)
    own_part, *other_parts = plan.over_heads(At.conv_z, conv_parts)
    mapped, *edges = run_kernel(
        map_body,
        [shape((total, chans))] + edge_shapes,
        plan.enter(At.map, own_part),
        *other_parts,
        scratch=[grid_scratch, edge_scratch],
    )

    def swap_edges(name, col, row, corner):
        return (
            plan.mark(name + 1, over_core(col)),
            plan.mark(name + 2, over_x(row)),
            plan.mark(name + 3, swap_with(corner, "tiles", 3)),
        )

    plan.mark(At.map, mapped)
    edges = swap_edges(At.edge, *edges)

    (gate,) = run_kernel(
        gate_body,
        [shape((total, chans), wide)],
        tokens,
        *first_pieces,
        flops=2 * total * chans * width,
    )
    chunk_shapes = [shape((shard, width))] * heads
    padded, spread, joined = run_kernel(
        depthwise_body,
        [shape(pad_dims, wide), shape((total, chans), wide), shape((total, chans))],
        plan.enter(At.depthwise, mapped),
        *edges,
        dw_params,
        gate,
        scratch=[grid_scratch, edge_scratch],
    )

    plan.mark(At.depthwise, joined)
    joined_parts = plan.gather(At.joined, joined)
    if fast:
        second_own, third_own, fourth_own = run_kernel(
            pack_rest_body,
            [
                shape((cross + 3 * chans, LANES)),
                shape((cross + 2 * hidden_width, LANES)),
                shape((cross - chans, LANES)),
            ],
            attn_in_w,
            up_w,
            down_w,
            plan.start(At.pack_rest, cross_parts[0]),
            *cross_parts[1:],
            scratch=[((), dma((3 * heads + 3 * lanes_of + hidden_width // LANES,)))],
            fetch=3,
        )
        second_x = plan.finish(At.second_x, over_x(plan.start(At.second_x, second_own)))
        second_y = plan.finish(At.second_y, over_y(plan.start(At.second_y, second_own)))
        corner = over_y(plan.start(At.second_corner, second_x))
        plan.finish(At.second_corner, corner)
        second_stack = stacked(
            plan.start(At.second_stack, second_own), second_x, second_y, corner
        )
        second_core = over_core(plan.start(At.second_core, second_stack))
        second = (second_stack, plan.finish(At.second_core, second_core))
    wide_rows_shape = shape((total, width), wide)
    first, normed1, query, kv_own = run_kernel(
        join_body,
        [
            wide_rows_shape,
            shape((total, width)),
            shape((total, chans)),
            shape((total, 2 * chans)),
        ],
        tokens,
        gains,
        biases,
        plan.enter(At.join, joined_parts[0]),
        *joined_parts[1:],
        *second,
        flops=2 * total * width * (width + 3 * chans),
    )
    plan.mark(At.join, kv_own)
    kv_x = plan.mark(At.kv_x, over_x(kv_own))
    kv_all = [
        kv_own,
        kv_x,
        plan.mark(At.kv_core, over_core(kv_own)),
        plan.mark(At.kv_x_core, over_core(kv_x)),
    ]
    (mixed,) = run_kernel(
        attend_body,
        [shape((total, chans))],
        plan.enter(At.attend, query),
        *kv_all,
        flops=8 * total * 4 * rows * chans,
    )
    plan.mark(At.attend, mixed)
    if fast:
        third_x = plan.finish(At.third_x, over_x(plan.start(At.third_x, third_own)))
        third_y = plan.finish(At.third_y, over_y(plan.start(At.third_y, third_own)))
        third_stack = stacked(third_own, third_x, third_y)
        upper = over_y(plan.start(At.upper, third_x[:cross]))
        lower = over_x(plan.start(At.lower, third_y[cross:]))
        plan.finish(At.upper, upper)
        plan.finish(At.lower, lower)
        third_core = over_core(plan.start(At.third_core, third_stack))
        plan.finish(At.third_core, third_core)
    mixed_parts = plan.gather(At.mixed, mixed)
    if fast:
        third = (
            third_stack,
            upper,
            lower,
            third_core,
            over_core(plan.start(At.upper_core, upper)),
            over_core(plan.start(At.lower_core, lower)),
        )

    wide_shape = shape((total, hidden_width))
    total_scratch = ((total, width), wide)
    second_rows, normed2, hidden, d_hidden, *ffn_parts = run_kernel(
        ffn_body,
        [wide_rows_shape, shape((total, width)), wide_shape, wide_shape] + chunk_shapes,
        upstream,
        first,
        gains,
        biases,
        plan.enter(At.ffn, mixed_parts[0]),
        *mixed_parts[1:],
        *third,
        scratch=[total_scratch],
        flops=2 * total * width * (width + 3 * hidden_width),
    )
    plan.mark(At.ffn, normed2)
    ffn_parts = plan.over_heads(At.ffn_z, ffn_parts)
    if fast:
        fourth_x = plan.finish(At.fourth_x, over_x(plan.start(At.fourth_x, fourth_own)))
        fourth_y = plan.finish(At.fourth_y, over_y(plan.start(At.fourth_y, fourth_own)))
    back_shapes = [shape((shard, width), wide), shape((shard + 8, width))]
    d_second, d_attn_own = run_kernel(
        norm_back_body,
        back_shapes,
        plan.enter(At.norm2, second_rows),
        upstream_wide,
        gains[1:2],
        *ffn_parts,
    )
    plan.mark(At.norm2, d_attn_own)
    d_attn_parts = plan.gather(At.d_attn, d_attn_own)
    if fast:
        fourth_corner = over_y(plan.start(At.fourth_corner, fourth_x))
        plan.finish(At.fourth_corner, fourth_corner)
    ud_keep, ud_send = run_kernel(
        pair_grad_body,
        [shape((4, 2 * hidden_width, LANES))] * 2,
        plan.start(At.ud_kernel, normed2),
        d_hidden,
        hidden,
        upstream,
        flops=4 * total * hidden_width * width,
    )
    plan.finish(At.ud_kernel, ud_keep)

    down_parts = run_kernel(
        down_body,
        chunk_shapes,
        plan.start(At.down_kernel, hidden),
        *third,
        scratch=[total_scratch],
        flops=2 * total * hidden_width * width,
    )
    plan.finish(At.down_kernel, down_parts[0])

    d_attn, d_query, kv_keep, kv_send, ln2_sums = run_kernel(
        attend_back_body,
        [
            shape((total, width)),
            shape((total, chans)),
            shape((2, total, 2 * chans), wide),
            shape((2, total, 2 * chans)),
            shape((2, width), wide),
        ],
        plan.enter(At.attend_back, query),
        *kv_all,
        *d_attn_parts,
        *third,
        scratch=[((total, chans), low), total_scratch],
        flops=2 * total * chans * width + 20 * total * 4 * rows * chans,
    )
    plan.mark(At.attend_back, kv_keep)
    kv_got = plan.mark(At.kv_got, over_core(kv_send))
    kv_mine, kv_over = run_kernel(
        add_pair_body,
        [shape((total, 2 * chans), wide), shape((total, 2 * chans))],
        plan.enter(At.add_pair, kv_keep),
        kv_got,
    )
    plan.mark(At.add_pair, kv_over)
    kv_back = plan.mark(At.kv_back, over_x(kv_over))
    down_parts = plan.over_heads(At.down, down_parts)
    (result_own,) = run_kernel(whole_cols_body, [shape((shard, width))], second_rows, *down_parts)
    if fast:
        fourth_stack = stacked(
            plan.start(At.fourth_stack, fourth_own), fourth_x, fourth_y, fourth_corner
        )
        fourth_core = over_core(plan.start(At.fourth_core, fourth_stack))
        fourth = (fourth_stack, plan.finish(At.fourth_core, fourth_core))
    d_qkv, *qkv_parts = run_kernel(
        d_qkv_body,
        [shape((total, 3 * chans))] + chunk_shapes,
        plan.enter(At.d_qkv, d_query),
        kv_mine,
        kv_back,
        *second,
        scratch=[total_scratch],
        flops=6 * total * chans * width,
    )
    plan.mark(At.d_qkv, d_qkv)
    qkv_parts = plan.over_heads(At.qkv_z, qkv_parts)
    if fast:
        ud_got = plan.finish(At.ud_core, over_core(plan.start(At.ud_core, ud_send)))
        ud_parts = add_cores(ud_keep, ud_got)
        ud_x = plan.finish(At.ud_x, over_x(plan.start(At.ud_x, ud_parts[1])))
        ud_y = plan.finish(At.ud_y, over_y(plan.start(At.ud_y, ud_parts[2])))
    else:
        ud_sums = jnp.concatenate([ud_keep, ud_send], axis=0)
    d_first, d_join_own = run_kernel(
        norm_back_body, back_shapes, first, plan.enter(At.norm3, d_second), gains[0:1], *qkv_parts
    )
    plan.mark(At.norm3, d_join_own)
    d_join_parts = plan.gather(At.d_join, d_join_own)
    ap_keep, ap_send = run_kernel(
        pair_grad_body,
        [shape((4, 4 * chans, LANES))] * 2,
        plan.start(At.ap_kernel, normed1),
        d_qkv,
        mixed,
        d_attn,
        flops=8 * total * chans * width,
    )
    plan.finish(At.ap_kernel, ap_keep)

    d_join, d_gate_in, tail, d_grid, ln1_sums, *edges = run_kernel(
        gate_back_body,
        [
            shape((total, width)),
            shape((total, chans)),
            shape((total + shard * (width // chans), chans)),
            shape((total, chans), wide),
            shape((2, width), wide),
        ]
        + edge_shapes,
        gate,
        spread,
        result_own,
        plan.enter(At.gate_back, d_join_parts[0]),
        *d_join_parts[1:],
        *second,
        scratch=[edge_scratch, total_scratch],
        flops=2 * total * chans * width,
    )
    plan.mark(At.gate_back, d_grid)
    edges = swap_edges(At.back, *edges)
    (d_mapped,) = run_kernel(
        depthwise_back_body,
        [shape((total, chans))],
        plan.enter(At.dw_back, d_grid),
        *edges,
        dw_params,
        scratch=[(pad_dims, wide), edge_scratch, grid_scratch],
    )
    plan.mark(At.dw_back, d_mapped)
    d_mapped_parts = plan.gather(At.d_mapped, d_mapped)
    if fast:
        ud_corner = over_corner(plan.start(At.ud_corner, ud_parts[3]))
        ud_sums = [ud_parts[0], ud_x, ud_y, plan.finish(At.ud_corner, ud_corner)]
        ap_got = plan.finish(At.ap_core, over_core(plan.start(At.ap_core, ap_send)))
        ap_parts = add_cores(ap_keep, ap_got)
    else:
        ap_sums = jnp.concatenate([ap_keep, ap_send], axis=0)
    (small,) = run_kernel(
        taps_body,
        [shape((8, width), wide)],
        plan.start(At.taps, d_grid),
        padded,
        ln1_sums,
        ln2_sums,
    )
    bit = 1
    while bit < tiles // 2:
        name = {1: At.small1, 2: At.small2}.get(bit)
        got = swap_with(plan.start(name, small), "tiles", bit)
        small = small + plan.finish(name, got)
        bit *= 2
    small_got = swap_with(plan.start(At.small_last, small), "tiles", bit)
    plan.finish(At.small_last, small_got)
    if fast:
        up_grad, down_grad = run_kernel(
            up_down_final_body,
            [shape(up_w.shape, wide), shape(down_w.shape, wide)],
            *ud_sums,
            leave=True,
        )
        plan.finish(At.up_down, up_grad)
    first_shape = shape((4, hires_chans + 2 * chans, LANES))
    first_keep, first_send = run_kernel(
        pair_grad_body,
        [first_shape] * 2,
        plan.start(At.first_kernel, tokens),
        d_gate_in,
        joined,
        d_join,
        flops=4 * total * chans * width,
    )
    first_keep, first_send = run_kernel(
        conv_grad_body,
        [first_shape] * 2,
        plan.enter(At.conv_grad, pooled),
        *d_mapped_parts,
        first_keep,
        first_send,
        scratch=[((BLOCKS, hires_chans, LANES), low)],
        flops=2 * total * hires_chans * width,
        alias={heads + 1: 0, heads + 2: 1},
    )
    plan.mark(At.conv_grad, first_send)
    tail_parts = plan.gather(At.tail, tail)
    (hires_grad,) = run_kernel(
        conv_back_body,
        [shape((batches, pixels, hires_chans), wide)],
        plan.start(At.hires, pools),
        conv_whole,
        *d_mapped_parts,
        flops=2 * total * hires_chans * width + 2 * total * pixels * hires_chans,
        leave=True,
    )
    plan.finish(At.hires, hires_grad)
    if fast:
        first_got = plan.mark(At.first_got, over_core(first_send))
        first_rows = first_keep.shape[1]
        first_parts = run_kernel(
            add_first_body,
            [shape((first_rows, LANES))] + [shape((first_rows + 4 * chans, LANES))] * 3,
            plan.enter(At.add_first, first_keep),
            first_got,
            *ap_parts[1:],
        )
        plan.mark(At.add_first, first_parts[0])
        first_sums = [
            first_parts[0],
            over_x(plan.start(At.last_x, plan.enter(At.last_x, first_parts[1]))),
            over_y(plan.start(At.last_y, plan.enter(At.last_y, first_parts[2]))),
            over_corner(plan.start(At.last_corner, plan.enter(At.last_corner, first_parts[3]))),
        ]
    else:
        first_sums = jnp.concatenate([first_keep, first_send], axis=0)
    (tokens_grad,) = run_kernel(
        tokens_grad_body,
        [shape((total, width), wide)],
        plan.enter(At.tokens, d_join),
        *tail_parts,
        *first_pieces,
        *fourth,
        flops=2 * total * width * width,
        leave=True,
    )
    (block_out,) = run_kernel(
        block_out_body,
        [shape((total, width))],
        *tail_parts,
        scratch=[total_scratch],
        leave=True,
    )

    plan.finish(At.tokens, tokens_grad)
    plan.finish(At.block, block_out)
    ln1_grad, ln2_grad, taps_grad = run_kernel(
        small_final_body,
        [shape((2, width), wide), shape((2, width), wide), shape(dw_params.shape, wide)],
        small,
        small_got,
        leave=True,
    )

    if fast:
        results = (conv_w, gate_w, join_w, attn_in_w, out_w)
        conv_grad, gate_grad, join_grad, attn_grad, out_w_grad = run_kernel(
            last_final_body,
            [shape(each.shape, wide) for each in results],
            plan.enter(At.last, first_sums[0]),
            *first_sums[1:],
            ap_parts[0],
            leave=True,
        )
    else:
        count = chans // LANES
        at = hires_chans
        conv_grad = scatter_dim(unpack_cols(first_sums[:, :at]), 1)
        gate_grad = scatter_dim(unpack_rows(first_sums[:, at : at + chans], count), 0)
        join_grad = scatter_dim(unpack_cols(first_sums[:, at + chans :]), 1)
        attn_grad = jnp.stack(
            [
                scatter_dim(unpack_rows(ap_sums[:, s * chans : (s + 1) * chans], count), 0)
                for s in range(3)
            ]
        )
        out_w_grad = scatter_dim(unpack_cols(ap_sums[:, 3 * chans :]), 1)
        up_grad = scatter_dim(unpack_rows(ud_sums[:, :hidden_width], hidden_width // LANES), 0)
        down_grad = scatter_dim(unpack_cols(ud_sums[:, hidden_width:]), 1)

    return (
        block_out.reshape(batches, rows, width),
        tokens_grad.reshape(batches, rows, width),
        hires_grad,
        ln1_grad,
        ln2_grad,
        taps_grad,
        conv_grad,
        gate_grad,
        join_grad,
        attn_grad,
        out_w_grad,
        up_grad,
        down_grad,
    )


def solution(mesh):
    placed = (
        P(None, "tiles", None),
        P(None, "tiles", "heads"),
        P(),
        P(None, "tiles", None),
        P(),
        P(),
        P(None, "heads"),
        P("heads", "tiles"),
        P("tiles", "heads"),
        P("heads", "tiles"),
        P(None, "tiles", "heads"),
        P("heads", "tiles"),
        P("tiles", "heads"),
        P("heads", "tiles"),
    )
    return jax.shard_map(
        local,
        mesh=mesh,
        in_specs=placed,
        out_specs=(
            P(None, "tiles", None),
            P(None, "tiles", None),
            P(None, "tiles", "heads"),
            P(),
            P(),
            P(None, "heads"),
            P("heads", "tiles"),
            P("tiles", "heads"),
            P("heads", "tiles"),
            P(None, "tiles", "heads"),
            P("heads", "tiles"),
            P("tiles", "heads"),
            P("heads", "tiles"),
        ),
        check_vma=False,
    )
```

```python
import jax
import jax.numpy as jnp
from jax import lax
from jax.experimental import pallas as pl
from jax.experimental.pallas import tpu as pltpu
from jax.sharding import PartitionSpec as P

HEAD_DIM = 64
GRID = 24
TILE = 12
HR_TILE = 24
PAD = 16
LANES = 128

norm_eps = 1e-05
inv_root_two = 0.7071067811865476
inv_root_two_pi = 0.3989422804014327

low = jnp.bfloat16
wide = jnp.float32
VMEM_LIMIT = 24 * 1024 * 1024


class At:
    (
        d_mix, d_mix1, d_mix2, d_mix3, d_jo, d_jo1, d_jo2, d_jo3, cross, cross1, cross2,
        cross3, conv_z, conv_z1, conv_z2, conv_z3, joined, joined1, joined2, joined3, mixed,
        mixed1, mixed2, mixed3, ffn_z, ffn_z1, ffn_z2, ffn_z3, d_attn, d_attn1, d_attn2,
        d_attn3, down, down1, down2, down3, qkv_z, qkv_z1, qkv_z2, qkv_z3, d_join, d_join1,
        d_join2, d_join3, d_mapped, d_mapped1, d_mapped2, d_mapped3, tail, tail1, tail2, tail3,
        edge, edge_c, edge_x, edge_xc, back, back_c, back_x, back_xc, first_x, first_y,
        first_corner, relative, pool, first_own_core, first_x_core, first_y_core,
        first_corner_core, conv, map, depthwise, pack_rest, second_x, second_y, second_corner,
        second_stack, second_core, join, kv_x, kv_core, kv_x_core, attend, third_x, third_y,
        upper, lower, third_core, upper_core, lower_core, ffn, fourth_x, fourth_y, norm2,
        fourth_corner, ud_kernel, down_kernel, attend_back, kv_got, add_pair, kv_back,
        fourth_stack, fourth_core, d_qkv, ud_core, ud_x, ud_y, norm3, ap_kernel, gate_back,
        dw_back, ud_corner, ap_core, taps, small1, small2, small_last, up_down, first_kernel,
        conv_grad, hires, first_got, add_first, last_x, last_y, last_corner, tokens, block,
        last,
    ) = range(129)


STARTS = {
    At.second_x: At.conv,
    At.second_y: At.conv,
    At.second_corner: At.map,
    At.second_stack: At.joined3,
    At.third_y: At.joined3,
    At.upper: At.kv_x,
    At.lower: At.join,
    At.third_core: At.kv_core,
    At.mixed: At.third_core,
    At.upper_core: At.second_core,
    At.lower_core: At.mixed2,
    At.fourth_y: At.ffn,
    At.ud_kernel: At.fourth_corner,
    At.fourth_stack: At.kv_got,
    At.ud_core: At.kv_got,
    At.ud_x: At.down2,
    At.ud_y: At.d_qkv,
    At.ap_kernel: At.d_join1,
    At.ud_corner: At.qkv_z3,
    At.ap_core: At.gate_back,
    At.tail: At.small1,
    At.first_kernel: At.d_mapped1,
    At.small_last: At.conv_grad,
    At.small1: At.d_mapped3,
    At.fourth_core: At.fourth_corner,
    At.conv_z: At.cross3,
    At.down1: At.kv_got,
    At.last_y: At.first_own_core,
    At.fourth_corner: At.ffn_z3,
    At.cross1: At.first_own_core,
    At.tail3: At.conv_grad,
    At.taps: At.cross1,
    At.fourth_x: At.attend,
    At.small2: At.back_c,
    At.pack_rest: At.first_own_core,
    At.first_x_core: At.pool,
    At.first_y_core: At.pool,
    At.first_corner_core: At.pool,
}
FINISHES = {
    At.cross1: At.map,
    At.cross3: At.conv,
    At.fourth_x: At.norm2,
    At.fourth_y: At.norm2,
    At.fourth_corner: At.attend_back,
    At.ud_kernel: At.attend_back,
    At.down_kernel: At.attend_back,
    At.down1: At.d_qkv,
    At.down2: At.d_qkv,
    At.down3: At.add_pair,
    At.fourth_core: At.d_qkv,
    At.ud_x: At.dw_back,
    At.ud_y: At.norm3,
    At.ud_corner: At.gate_back,
    At.small2: At.conv_grad,
    At.up_down: At.conv_grad,
    At.hires: At.last_y,
    At.d_mapped1: At.dw_back,
    At.small_last: At.add_first,
    At.block: At.add_first,
    At.d_attn1: At.add_pair,
    At.upper: At.last_y,
    At.mixed3: At.last_y,
    At.ap_kernel: At.add_first,
    At.second_corner: At.last_y,
}
TURNS = {
    At.ffn_z: (3, 1, 2),
    At.d_attn: (1, 2, 3),
    At.mixed: (2, 1, 3),
    At.conv_z: (1, 3, 2),
    At.joined: (1, 2, 3),
}


def shape(dims, kind=low):
    return jax.ShapeDtypeStruct(tuple(dims), kind)


def after(value, *others):
    return lax.optimization_barrier((value, *others))[0]


class Plan:
    def __init__(self, starts, finishes, turns):
        self.starts, self.finishes, self.turns = starts, finishes, turns
        self.events, self.held = {}, {}

    def mark(self, name, value):
        self.events[name] = value
        return value

    def start(self, name, value):
        event = self.events.get(self.starts.get(name))
        return value if event is None else after(value, event)

    def finish(self, name, value):
        self.mark(name, value)
        self.held.setdefault(self.finishes.get(name), []).append(value)
        return value

    def enter(self, name, value):
        held = self.held.pop(name, ())
        return after(value, *held) if held else value

    def over_heads(self, name, parts):
        count = len(parts)
        found = [parts[0]] * count
        for j in self.turns.get(name, range(1, count)):
            sent = self.start(name + j, self.start(name, parts[j]))
            found[j] = self.finish(name + j, swap_with(sent, "heads", j))
        return found

    def gather(self, name, own):
        return self.over_heads(name, [own] * lax.axis_size("heads"))


def run_kernel(body, outs, *args, scratch=(), flops=0, leave=False, fetch=False, alias=None):
    whole = pl.BlockSpec(memory_space=pltpu.VMEM)
    source = pl.BlockSpec(memory_space=pl.ANY) if fetch else whole
    target = pl.BlockSpec() if leave else whole
    if fetch:
        count = len(args) if fetch is True else fetch
        held = [pltpu.with_memory_space_constraint(arg, pltpu.HBM) for arg in args[:count]]
        args = [*held, *args[count:]]
    traffic = sum(a.size * a.dtype.itemsize for a in args)
    traffic += sum(o.size * o.dtype.itemsize for o in outs)
    return pl.pallas_call(
        body,
        name=body.__name__,
        out_shape=tuple(outs),
        in_specs=[source] * len(args),
        out_specs=tuple([target] * len(outs)),
        scratch_shapes=[pltpu.VMEM(dims, kind) if dims else kind for dims, kind in scratch],
        input_output_aliases=alias or {},
        cost_estimate=pl.CostEstimate(flops=1, bytes_accessed=1, transcendentals=0),
        compiler_params=pltpu.CompilerParams(vmem_limit_bytes=VMEM_LIMIT),
    )(*args)


def dot(left, right, contract=(1, 0)):
    return lax.dot_general(
        left, right, (((contract[0],), (contract[1],)), ((), ())), preferred_element_type=wide
    )


def cat(parts, axis):
    return parts[0] if len(parts) == 1 else jnp.concatenate(parts, axis=axis)


def swap_with(value, axis, mask):
    pairs = [(source, source ^ mask) for source in range(lax.axis_size(axis))]
    return lax.ppermute(value, axis, pairs)


def over_core(value):
    return swap_with(value, "tiles", 1)


def over_x(value):
    return swap_with(value, "tiles", 2)


def over_y(value):
    return swap_with(value, "tiles", 4)


def fast_tiles():
    return lax.axis_size("tiles") == 8


BLOCKS = 8


def place_mask(place):
    half = BLOCKS // 2
    return ((place % half) * 2) | (place // half)


def block_at(place):
    if fast_tiles():
        return lax.axis_index("tiles") ^ place_mask(place)
    return place


def gather_first(block):
    found = [block, over_x(block), over_y(block), swap_with(block, "tiles", 6)]
    return found + [over_core(part) for part in found]


def stack_body(*refs):
    for i, ref in enumerate(refs[:-1]):
        refs[-1][i] = ref[...]


def stacked(*parts):
    return run_kernel(stack_body, [shape((len(parts), *parts[0].shape))], *parts)[0]


def stack_corner_body(*refs):
    *part_refs, upper_ref, lower_ref, out_ref = refs
    for i, ref in enumerate(part_refs):
        out_ref[i] = ref[...]
    cut = upper_ref.shape[0]
    out_ref[len(part_refs), 0:cut] = upper_ref[...]
    out_ref[len(part_refs), cut:] = lower_ref[...]


def rows_of(*stacks):
    return [ref.at[i] for ref in stacks for i in range(ref.shape[0])]


def gather_heads(own):
    return [own] + [swap_with(own, "heads", j) for j in range(1, lax.axis_size("heads"))]


def add_rows_body(keep_ref, got_ref, *out_refs):
    for i, out_ref in enumerate(out_refs):
        total = keep_ref[i].astype(wide) + got_ref[i].astype(wide)
        out_ref[...] = total.astype(out_ref.dtype)


def add_first_body(keep_ref, got_ref, *refs):
    more_refs, out_refs = refs[:3], refs[3:]
    rows = keep_ref.shape[1]
    for i, out_ref in enumerate(out_refs):
        total = keep_ref[i].astype(wide) + got_ref[i].astype(wide)
        out_ref[0:rows] = total.astype(out_ref.dtype)
        if i:
            out_ref[rows:] = more_refs[i - 1][...]


def add_cores(keep, got):
    return run_kernel(add_rows_body, [shape(keep.shape[1:])] * 4, keep, got)


def over_corner(value):
    return swap_with(value, "tiles", 6)


def gelu_parts(inputs):
    bell = 0.5 * (1.0 + lax.erf(inputs * inv_root_two))
    return inputs * bell, bell + inputs * inv_root_two_pi * jnp.exp(-0.5 * inputs * inputs)


def normed(values):
    centred = values - jnp.mean(values, axis=-1, keepdims=True)
    inv_std = lax.rsqrt(jnp.mean(centred * centred, axis=-1, keepdims=True) + norm_eps)
    return centred * inv_std, inv_std


def total_of(refs, at=Ellipsis):
    total = refs[0][at].astype(wide)
    for ref in refs[1:]:
        total = total + ref[at].astype(wide)
    return total


def copies(pairs, sems):
    started = [
        pltpu.make_async_copy(source, target, sems.at[i])
        for i, (source, target) in enumerate(pairs)
    ]
    for copy in started:
        copy.start()
    for copy in started:
        copy.wait()


def lane_blocks(source, target, start):
    rows, lanes = source.shape
    return [
        (
            source.at[:, pl.ds(m * LANES, LANES)],
            target.at[pl.ds(start + m * rows, rows)],
        )
        for m in range(lanes // LANES)
    ]


def pack_first_body(conv_ref, gate_ref, join_ref, out_w_ref, first_ref, cross_ref, sems):
    at = conv_ref.shape[0]
    pairs = [(conv_ref, first_ref.at[pl.ds(0, at)])]
    pairs += lane_blocks(gate_ref, first_ref, at)
    pairs += lane_blocks(gate_ref, cross_ref, 0)
    rows = join_ref.shape[0]
    pairs += [(join_ref, cross_ref.at[pl.ds(rows, rows)])]
    pairs += [(out_w_ref, cross_ref.at[pl.ds(2 * rows, rows)])]
    copies(pairs, sems)


def pack_rest_body(attn_ref, up_ref, down_ref, *refs):
    cross_refs, (second_ref, third_ref, fourth_ref, sems) = refs[:-4], refs[-4:]
    rows = cross_refs[0].shape[0] // 3
    heads = len(cross_refs)
    pairs = []
    for j, ref in enumerate(cross_refs):
        pairs += [(ref.at[pl.ds(rows, rows)], second_ref.at[pl.ds(j * rows, rows)])]
        pairs += [(ref.at[pl.ds(2 * rows, rows)], third_ref.at[pl.ds(j * rows, rows)])]
        if j:
            at = (j - 1) * rows
            pairs += [(ref.at[pl.ds(0, rows)], fourth_ref.at[pl.ds(at, rows)])]
    for s in range(3):
        pairs += lane_blocks(attn_ref.at[s], second_ref, (heads + s) * rows)
    pairs += lane_blocks(up_ref, third_ref, heads * rows)
    rows = down_ref.shape[0]
    pairs += [(down_ref, third_ref.at[pl.ds(third_ref.shape[0] - rows, rows)])]
    copies(pairs, sems)


def third_refs(refs, results):
    count = len(refs) - results
    if count == 2:
        pieces = rows_of(*refs[:2])
        return pieces, pieces, refs[2:]
    stack, upper, lower, core_stack, core_upper, core_lower = refs[:6]
    own, core = rows_of(stack), rows_of(core_stack)
    return own + [upper] + core + [core_upper], own + [lower] + core + [core_lower], refs[6:]


def views(refs, start, rows):
    return [ref if ref.shape[0] == rows else ref.at[pl.ds(start, rows)] for ref in refs]


def whole_number(value, parts):
    return jnp.floor((value + 0.5) * (1.0 / parts))


def pool_body(sides_ref, maps_ref, pooled_ref, pool_ref, hold, sems):
    copy = pltpu.make_async_copy(maps_ref, hold, sems.at[0])
    copy.start()
    image = lax.axis_index("tiles") // 4
    cells, pixels = pool_ref.shape[1:]
    cell = lax.broadcasted_iota(jnp.int32, (cells, pixels), 0).astype(wide)
    pixel = lax.broadcasted_iota(jnp.int32, (cells, pixels), 1).astype(wide)
    cell_row = whole_number(cell, TILE)
    pixel_row = whole_number(pixel, HR_TILE)
    spots = (
        (cell_row, pixel_row),
        (cell - TILE * cell_row, pixel - HR_TILE * pixel_row),
    )
    for batch in range(pool_ref.shape[0]):
        side = sides_ref[batch, image].astype(wide)
        weights = 1.0
        for cell_at, pixel_at in spots:
            begin = whole_number(cell_at * side, GRID)
            end = whole_number((cell_at + 1.0) * side + (GRID - 1.0), GRID)
            inside = jnp.logical_and(pixel_at >= begin, pixel_at < end)
            weights = weights * jnp.where(inside, 1.0 / (end - begin), 0.0)
        pool_ref[batch] = weights.astype(low)
    copy.wait()
    for batch in range(pool_ref.shape[0]):
        pooled = dot(pool_ref[batch], hold[batch])
        pooled_ref[batch * cells : (batch + 1) * cells] = pooled.astype(low)


def wide_rows(refs, start, count):
    return cat(
        [
            cat([ref[start + m * LANES : start + (m + 1) * LANES] for m in range(count)], 1)
            for ref in refs
        ],
        0,
    )


def wide_cols(refs, start, rows):
    return cat([ref[start : start + rows] for ref in refs], 1)


def relative_body(*refs):
    count = len(refs[:-1]) // 3
    sources, outs, found = refs[:count], refs[count : 2 * count], refs[2 * count : -1]
    copies(list(zip(sources, found)), refs[-1])
    for source, target in zip(found, outs):
        for place in range(BLOCKS):
            lanes = pl.ds(pl.multiple_of(LANES * block_at(place), LANES), LANES)
            target[:, place * LANES : (place + 1) * LANES] = source[:, lanes]


def conv_body(pooled_ref, *refs):
    piece_refs, (whole_ref, *out_refs) = refs[:BLOCKS], refs[BLOCKS:]
    head = lax.axis_index("heads")
    for place, ref in enumerate(piece_refs):
        whole_ref[block_at(place)] = ref[0 : whole_ref.shape[1]]
    per_chunk = BLOCKS // len(out_refs)
    for j, out_ref in enumerate(out_refs):
        first = per_chunk * (head ^ j)
        chunk = cat([whole_ref[first + i] for i in range(per_chunk)], 1)
        out_ref[...] = dot(pooled_ref[...], chunk).astype(low)


def edge_flags():
    tile = lax.axis_index("tiles")
    return (tile & 1) == 0, (tile & 2) == 0


def send_edges(grid, hold_ref, col_ref, row_ref, corner_ref):
    right, lower = edge_flags()
    cells = TILE * TILE
    batches = grid.shape[0] // cells
    count = batches * TILE
    for at in range(count):
        begin = at * TILE
        end = begin + TILE - 1
        hold_ref[at : at + 1] = jnp.where(right, grid[end : end + 1], grid[begin : begin + 1])
    col_ref[...] = hold_ref[0:count].astype(low)
    hold_ref[...] = jnp.zeros(hold_ref.shape, wide)
    for batch in range(batches):
        base = batch * cells
        bottom = grid[base + cells - TILE : base + cells]
        top = grid[base : base + TILE]
        edge = jnp.where(lower, bottom, top)
        hold_ref[batch * PAD : batch * PAD + TILE] = edge
    row_ref[...] = hold_ref[...].astype(low)
    hold_ref[...] = jnp.zeros(hold_ref.shape, wide)
    for batch in range(batches):
        base = batch * cells
        ends = [
            jnp.where(right, grid[at + TILE - 1 : at + TILE], grid[at : at + 1])
            for at in (base + cells - TILE, base)
        ]
        hold_ref[batch : batch + 1] = jnp.where(lower, ends[0], ends[1])
    corner_ref[...] = hold_ref[0:PAD].astype(low)


def fill_padded(grid, col_ref, row_ref, corner_ref, pad_ref, hold_ref):
    right, lower = edge_flags()
    cells = TILE * TILE
    batches = grid.shape[0] // cells
    per_batch = (TILE + 2) * PAD
    pad_ref[...] = jnp.zeros(pad_ref.shape, wide)
    hold_ref[0 : batches * TILE] = col_ref[...].astype(wide)
    for batch in range(batches):
        for a in range(TILE):
            at = batch * per_batch + (a + 1) * PAD
            source = batch * cells + a * TILE
            pad_ref[at + 1 : at + 1 + TILE] = grid[source : source + TILE]
            got = hold_ref[batch * TILE + a : batch * TILE + a + 1]
            zero = jnp.zeros_like(got)
            pad_ref[at : at + 1] = jnp.where(right, zero, got)
            pad_ref[at + TILE + 1 : at + TILE + 2] = jnp.where(right, got, zero)
    rows = row_ref[...].astype(wide)
    corners = corner_ref[...].astype(wide)
    for batch in range(batches):
        got = rows[batch * PAD : batch * PAD + TILE]
        corner = corners[batch : batch + 1]
        zero = jnp.zeros_like(got)
        nil = jnp.zeros_like(corner)
        for at, used in (
            (batch * per_batch, jnp.logical_not(lower)),
            (batch * per_batch + (TILE + 1) * PAD, lower),
        ):
            pad_ref[at + 1 : at + 1 + TILE] = jnp.where(used, got, zero)
            left = jnp.logical_and(used, jnp.logical_not(right))
            pad_ref[at : at + 1] = jnp.where(left, corner, nil)
            pad_ref[at + TILE + 1 : at + TILE + 2] = jnp.where(
                jnp.logical_and(used, right), corner, nil
            )


def map_body(*refs):
    heads = lax.axis_size("heads")
    part_refs, (map_ref, col_ref, row_ref, corner_ref, grid, hold) = refs[:heads], refs[heads:]
    mapped = total_of(part_refs).astype(low)
    map_ref[...] = mapped
    grid[...] = mapped.astype(wide)
    send_edges(grid, hold, col_ref, row_ref, corner_ref)


def gate_body(tok_ref, *refs):
    piece_refs, (gate_ref,) = refs[:BLOCKS], refs[BLOCKS:]
    chans = gate_ref.shape[1]
    start = piece_refs[0].shape[0] - chans
    weights = wide_rows(views(piece_refs, start, chans), 0, chans // LANES)
    gate_ref[...] = jnp.tanh(dot(tok_ref[...], weights)).astype(wide)


def own_rows(ref, at, rows):
    return ref[pl.ds(pl.multiple_of(rows * at, 8), rows)]


def write_chunks(total_ref, out_refs):
    head = lax.axis_index("heads")
    rows = total_ref.shape[0] // len(out_refs)
    for j, out_ref in enumerate(out_refs):
        out_ref[...] = own_rows(total_ref, head ^ j, rows).astype(low)


def whole_rows(part_refs, hold_ref, rows):
    head = lax.axis_index("heads")
    for j, ref in enumerate(part_refs):
        to = pl.ds(pl.multiple_of(rows * (head ^ j), 8), rows)
        hold_ref[to] = ref[...].astype(wide)[:rows]
    return hold_ref[...].astype(low)


def depthwise_body(map_ref, col_ref, row_ref, corner_ref, dw_ref, gate_ref, *refs):
    pad_ref, spread_ref, joined_ref, grid, hold = refs
    grid[...] = map_ref[...].astype(wide)
    fill_padded(grid, col_ref, row_ref, corner_ref, pad_ref, hold)
    cells = TILE * TILE
    batches = grid.shape[0] // cells
    per_batch = (TILE + 2) * PAD
    for batch in range(batches):
        for a in range(TILE):
            running = jnp.broadcast_to(dw_ref[9:10], (TILE, grid.shape[1]))
            for tap in range(9):
                row, col = divmod(tap, 3)
                at = batch * per_batch + (a + row) * PAD + col
                running = running + dw_ref[tap : tap + 1] * pad_ref[at : at + TILE]
            to = batch * cells + a * TILE
            spread_ref[to : to + TILE] = running
    joined_ref[...] = (gate_ref[...] * spread_ref[...]).astype(low)


def project_all(rows_refs, piece_refs, base_ref, sum_ref):
    rows = cat([ref[...] for ref in rows_refs], 1)
    for pair in range(BLOCKS // 2):
        weights = wide_cols(piece_refs[2 * pair : 2 * pair + 2], 0, rows.shape[1])
        lanes = slice(2 * pair * LANES, 2 * (pair + 1) * LANES)
        sum_ref[:, lanes] = base_ref[:, lanes].astype(wide) + dot(rows, weights)


def join_body(tok_ref, gain_ref, bias_ref, *refs):
    heads = lax.axis_size("heads")
    part_refs, piece_refs = refs[:heads], rows_of(*refs[heads : heads + 2])
    first_ref, all_ref, query_ref, kv_ref = refs[heads + 2 :]
    chans = query_ref.shape[1]
    join_refs = views(piece_refs, 0, heads * chans)
    attn_refs = views(piece_refs, heads * chans, 3 * chans)
    project_all(part_refs, join_refs, tok_ref, first_ref)
    rows = (normed(first_ref[...])[0] * gain_ref[0:1] + bias_ref[0:1]).astype(low)
    all_ref[...] = rows
    count = chans // LANES
    for s in range(3):
        result = dot(all_ref[...], wide_rows(attn_refs, s * chans, count)).astype(low)
        if s == 0:
            query_ref[...] = result
        else:
            kv_ref[:, (s - 1) * chans : s * chans] = result


def head_masks(rows):
    lane = lax.broadcasted_iota(jnp.int32, (rows, LANES), 1)
    return [lane < HEAD_DIM, lane >= HEAD_DIM]


def softmax_parts(query, keys):
    scores = dot(query, keys, (1, 1)) * HEAD_DIM ** (-0.5)
    expo = jnp.exp(scores - jnp.max(scores, axis=-1, keepdims=True))
    return expo / jnp.sum(expo, axis=-1, keepdims=True)


def attend_body(query_ref, *refs):
    kv_refs, (mixed_ref,) = refs[:4], refs[4:]
    chans = query_ref.shape[1]
    cells = TILE * TILE
    masks = head_masks(cells)
    for batch in range(query_ref.shape[0] // cells):
        at = slice(batch * cells, (batch + 1) * cells)
        for pair in range(chans // LANES):
            lanes = slice(pair * LANES, (pair + 1) * LANES)
            value_lanes = slice(chans + pair * LANES, chans + (pair + 1) * LANES)
            keys = cat([ref[at, lanes] for ref in kv_refs], 0)
            values = cat([ref[at, value_lanes] for ref in kv_refs], 0)
            query = query_ref[at, lanes]
            found = []
            for mask in masks:
                probs = softmax_parts(jnp.where(mask, query, jnp.zeros_like(query)), keys)
                found.append(dot(probs.astype(low), values))
            mixed_ref[at, lanes] = jnp.where(masks[0], found[0], found[1]).astype(low)


HIDDEN_STEP = 256


def ffn_body(upstream_ref, first_ref, gain_ref, bias_ref, *refs):
    heads = lax.axis_size("heads")
    part_refs = refs[:heads]
    out_pieces, piece_refs, refs = third_refs(refs[heads:], 5 + heads)
    second_ref, all_ref, hidden_ref, d_hidden_ref = refs[:4]
    out_refs, total_ref = refs[4:-1], refs[-1]
    hidden_width = hidden_ref.shape[1]
    depth = heads * part_refs[0].shape[1]
    start = piece_refs[0].shape[0] - 2 * hidden_width
    piece_refs = views(piece_refs, start, 2 * hidden_width)
    project_all(part_refs, views(out_pieces, 0, depth), first_ref, second_ref)
    rows = normed(second_ref[...])[0] * gain_ref[1:2] + bias_ref[1:2]
    all_ref[...] = rows.astype(low)
    total_ref[...] = jnp.zeros(total_ref.shape, wide)
    per_step = HIDDEN_STEP // LANES

    def step(m, carry):
        at = pl.multiple_of(m * HIDDEN_STEP, HIDDEN_STEP)
        up = cat(
            [
                cat([ref[pl.ds(at + i * LANES, LANES)] for i in range(per_step)], 1)
                for ref in piece_refs
            ],
            0,
        )
        down = cat([ref[pl.ds(hidden_width + at, HIDDEN_STEP)] for ref in piece_refs], 1)
        value, slope = gelu_parts(dot(all_ref[...], up))
        hidden_ref[:, pl.ds(at, HIDDEN_STEP)] = value.astype(low)
        d_hidden = (dot(upstream_ref[...], down, (1, 1)) * slope).astype(low)
        d_hidden_ref[:, pl.ds(at, HIDDEN_STEP)] = d_hidden
        total_ref[...] += dot(d_hidden, up, (1, 1))
        return carry

    lax.fori_loop(0, hidden_width // HIDDEN_STEP, step, 0)
    write_chunks(total_ref, out_refs)


def down_body(hidden_ref, *refs):
    _, piece_refs, refs = third_refs(refs, 1 + lax.axis_size("heads"))
    out_refs, total_ref = refs[:-1], refs[-1]
    width = hidden_ref.shape[1]
    piece_refs = views(piece_refs, piece_refs[0].shape[0] - 2 * width, 2 * width)
    for pair in range(BLOCKS // 2):
        weights = wide_cols(piece_refs[2 * pair : 2 * pair + 2], width, width)
        lanes = slice(2 * pair * LANES, 2 * (pair + 1) * LANES)
        total_ref[:, lanes] = dot(hidden_ref[...], weights)
    write_chunks(total_ref, out_refs)


def whole_cols_body(base_ref, *refs):
    part_refs, out_ref = refs[:-1], refs[-1]
    head = lax.axis_index("heads")
    shard = out_ref.shape[0]
    for place in range(BLOCKS):
        lanes = slice(place * LANES, (place + 1) * LANES)
        mine = base_ref[pl.ds(pl.multiple_of(shard * head, 8), shard), lanes]
        total = mine + total_of(part_refs, (slice(None), lanes))
        to = pl.ds(pl.multiple_of(LANES * block_at(place), LANES), LANES)
        out_ref[:, to] = total.astype(low)


def block_out_body(*refs):
    part_refs, out_ref, hold = refs[:-2], refs[-2], refs[-1]
    head = lax.axis_index("heads")
    shard = out_ref.shape[0] // len(part_refs)
    for j, ref in enumerate(part_refs):
        to = pl.ds(pl.multiple_of(shard * (head ^ j), 8), shard)
        chans = ref.shape[1]
        rows = ref[...].astype(wide)[out_ref.shape[0] :]
        for m in range(out_ref.shape[1] // chans):
            hold[to, m * chans : (m + 1) * chans] = rows[m * shard : (m + 1) * shard]
    out_ref[...] = hold[...].astype(out_ref.dtype)


def tokens_grad_body(d_first_ref, *refs):
    heads = lax.axis_size("heads")
    part_refs, own_refs = refs[:heads], refs[heads : heads + BLOCKS]
    other_refs, out_ref = rows_of(*refs[heads + BLOCKS : -1]), refs[-1]
    chans = part_refs[0].shape[1]
    own_refs = views(own_refs, own_refs[0].shape[0] - chans, chans)
    rows = cat([ref[0 : out_ref.shape[0]] for ref in part_refs], 1)
    count = chans // LANES
    for pair in range(BLOCKS // 2):
        both = slice(2 * pair, 2 * pair + 2)
        weights = [wide_rows(own_refs[both], 0, count)]
        weights += [wide_rows(other_refs[both], j * chans, count) for j in range(heads - 1)]
        lanes = slice(2 * pair * LANES, 2 * (pair + 1) * LANES)
        grad = d_first_ref[:, lanes].astype(wide) + dot(rows, cat(weights, 1), (1, 1))
        for i in range(2):
            block = block_at(2 * pair + i)
            to = pl.ds(pl.multiple_of(LANES * block, LANES), LANES)
            out_ref[:, to] = grad[:, i * LANES : (i + 1) * LANES]


def norm_back_body(values_ref, base_ref, gain_ref, *refs):
    part_refs, (sum_ref, low_ref) = refs[:-2], refs[-2:]
    rows = sum_ref.shape[0]
    head = lax.axis_index("heads")
    scaled, inv_std = normed(own_rows(values_ref, head, rows))
    upstream = total_of(part_refs)
    weighted = upstream * gain_ref[...]
    inner = (
        weighted
        - jnp.mean(weighted, axis=-1, keepdims=True)
        - scaled * jnp.mean(weighted * scaled, axis=-1, keepdims=True)
    )
    base = base_ref[...] if base_ref.shape[0] == rows else own_rows(base_ref, head, rows)
    total = base.astype(wide) + inv_std * inner
    sum_ref[...] = total
    sums = [
        jnp.sum(upstream * scaled, axis=0, keepdims=True),
        jnp.sum(upstream, axis=0, keepdims=True),
    ]
    coarse = [each.astype(low).astype(wide) for each in sums]
    fine = [each - near for each, near in zip(sums, coarse)]
    extra = low_ref.shape[0] - rows - 4
    blank = jnp.zeros((extra, total.shape[1]), wide)
    low_ref[...] = cat([total, *coarse, *fine, blank], 0).astype(low)


def sums_from(part_refs, sums_ref, shard):
    found = total_of(part_refs, slice(shard, shard + 8))
    sums_ref[...] = found[0:2] + found[2:4]


def attend_back_body(query_ref, *refs):
    heads = lax.axis_size("heads")
    kv_refs, part_refs = refs[:4], refs[4 : 4 + heads]
    piece_refs, _, refs = third_refs(refs[4 + heads :], 7)
    all_ref, d_query_ref, keep_ref, send_ref, sums_ref, d_mixed_ref, hold = refs
    chans = query_ref.shape[1]
    cells = TILE * TILE
    scale = HEAD_DIM ** (-0.5)
    shard = all_ref.shape[0] // heads
    all_ref[...] = whole_rows(part_refs, hold, shard)
    sums_from(part_refs, sums_ref, shard)
    weights = wide_cols(views(piece_refs, 0, heads * chans), 0, chans)
    d_mixed_ref[...] = dot(all_ref[...], weights, (1, 1)).astype(low)
    masks = head_masks(cells)
    for batch in range(query_ref.shape[0] // cells):
        at = slice(batch * cells, (batch + 1) * cells)
        for pair in range(chans // LANES):
            lanes = slice(pair * LANES, (pair + 1) * LANES)
            value_lanes = slice(chans + pair * LANES, chans + (pair + 1) * LANES)
            keys = cat([ref[at, lanes] for ref in kv_refs], 0)
            values = cat([ref[at, value_lanes] for ref in kv_refs], 0)
            query = query_ref[at, lanes]
            d_mixed = d_mixed_ref[at, lanes]
            d_queries = []
            d_keys = 0.0
            d_values = 0.0
            for mask in masks:
                own_query = jnp.where(mask, query, jnp.zeros_like(query))
                own_mixed = jnp.where(mask, d_mixed, jnp.zeros_like(d_mixed))
                probs = softmax_parts(own_query, keys)
                d_probs = dot(own_mixed, values, (1, 1))
                inner = jnp.sum(probs * d_probs, axis=-1, keepdims=True)
                d_scores = (probs * (d_probs - inner)).astype(low)
                d_queries.append(dot(d_scores, keys))
                d_keys = d_keys + dot(d_scores, own_query, (0, 0))
                d_values = d_values + dot(probs.astype(low), own_mixed, (0, 0))
            d_query = jnp.where(masks[0], d_queries[0], d_queries[1]) * scale
            d_query_ref[at, lanes] = d_query.astype(low)
            d_keys = d_keys * scale
            for i in range(4):
                target = (keep_ref, send_ref)[i // 2]
                own = slice(i * cells, (i + 1) * cells)
                target[i % 2, at, lanes] = d_keys[own].astype(target.dtype)
                target[i % 2, at, value_lanes] = d_values[own].astype(target.dtype)


def add_pair_body(keep_ref, got_ref, own_ref, send_ref):
    own_ref[...] = keep_ref[0] + got_ref[0].astype(wide)
    send_ref[...] = (keep_ref[1] + got_ref[1].astype(wide)).astype(low)


def d_qkv_body(d_query_ref, own_ref, got_ref, *refs):
    piece_refs, (d_qkv_ref, *out_refs, total_ref) = rows_of(*refs[:2]), refs[2:]
    chans = d_query_ref.shape[1]
    d_qkv_ref[:, :chans] = d_query_ref[...]
    d_qkv_ref[:, chans:] = (own_ref[...] + got_ref[...].astype(wide)).astype(low)
    d_qkv = d_qkv_ref[...]
    count = 3 * chans // LANES
    piece_refs = views(piece_refs, lax.axis_size("heads") * chans, 3 * chans)
    for pair in range(BLOCKS // 2):
        weights = wide_rows(piece_refs[2 * pair : 2 * pair + 2], 0, count)
        lanes = slice(2 * pair * LANES, 2 * (pair + 1) * LANES)
        total_ref[:, lanes] = dot(d_qkv, weights, (1, 1))
    write_chunks(total_ref, out_refs)


def gate_back_body(gate_ref, spread_ref, result_ref, *refs):
    heads = lax.axis_size("heads")
    head = lax.axis_index("heads")
    part_refs, piece_refs = refs[:heads], rows_of(*refs[heads : heads + 2])
    all_ref, d_gate_ref, tail_ref, grid_ref, sums_ref, *edge_refs, edge, hold = refs[heads + 2 :]
    shard = all_ref.shape[0] // heads
    all_ref[...] = whole_rows(part_refs, hold, shard)
    sums_from(part_refs, sums_ref, shard)
    chans = gate_ref.shape[1]
    weights = wide_cols(views(piece_refs, 0, heads * chans), 0, chans)
    d_joined = dot(all_ref[...], weights, (1, 1))
    gate = gate_ref[...]
    d_gate = d_joined * spread_ref[...] * (1.0 - gate * gate)
    d_gate_ref[...] = d_gate.astype(low)
    result = result_ref[...].astype(wide)
    folded = [result[:, m * chans : (m + 1) * chans] for m in range(result.shape[1] // chans)]
    tail_ref[...] = cat([d_gate, *folded], 0).astype(low)
    grid_ref[...] = d_joined * gate
    send_edges(grid_ref, edge, *edge_refs)


def depthwise_back_body(grid_ref, col_ref, row_ref, corner_ref, dw_ref, out_ref, d_pad, hold, flat):
    fill_padded(grid_ref, col_ref, row_ref, corner_ref, d_pad, hold)
    cells = TILE * TILE
    per_batch = (TILE + 2) * PAD
    chans = grid_ref.shape[1]
    for batch in range(grid_ref.shape[0] // cells):
        for a in range(TILE):
            running = jnp.zeros((TILE, chans), wide)
            for tap in range(9):
                row, col = divmod(tap, 3)
                at = batch * per_batch + (a + 2 - row) * PAD + 2 - col
                running = running + dw_ref[tap : tap + 1] * d_pad[at : at + TILE]
            flat[batch * cells + a * TILE : batch * cells + (a + 1) * TILE] = running
    out_ref[...] = flat[...].astype(low)


def taps_body(grid_ref, pad_ref, ln1_ref, ln2_ref, small_ref):
    cells = TILE * TILE
    per_batch = (TILE + 2) * PAD
    chans = grid_ref.shape[1]
    sums = [jnp.zeros((TILE, chans), wide) for _ in range(10)]
    for batch in range(grid_ref.shape[0] // cells):
        for a in range(TILE):
            own = grid_ref[batch * cells + a * TILE : batch * cells + (a + 1) * TILE]
            for tap in range(9):
                row, col = divmod(tap, 3)
                at = batch * per_batch + (a + row) * PAD + col
                sums[tap] = sums[tap] + own * pad_ref[at : at + TILE]
            sums[9] = sums[9] + own
    small_ref[...] = jnp.zeros(small_ref.shape, wide)
    for place in range(BLOCKS):
        lanes = slice(place * LANES, (place + 1) * LANES)
        to = pl.ds(pl.multiple_of(LANES * block_at(place), LANES), LANES)
        small_ref[0:2, to] = ln1_ref[:, lanes]
        small_ref[2:4, to] = ln2_ref[:, lanes]
    per_row = small_ref.shape[1] // chans
    for tap in range(10):
        row, lane = 4 + tap // per_row, tap % per_row * chans
        total = jnp.sum(sums[tap], axis=0, keepdims=True)
        small_ref[row : row + 1, lane : lane + chans] = total


def small_final_body(own_ref, got_ref, ln1_ref, ln2_ref, taps_ref):
    total = own_ref[...] + got_ref[...]
    ln1_ref[...] = total[0:2]
    ln2_ref[...] = total[2:4]
    chans = taps_ref.shape[1]
    per_row = total.shape[1] // chans
    for tap in range(10):
        row, lane = 4 + tap // per_row, tap % per_row * chans
        taps_ref[tap : tap + 1] = total[row : row + 1, lane : lane + chans]


def conv_back_body(pool_ref, whole_ref, *refs):
    heads = lax.axis_size("heads")
    head = lax.axis_index("heads")
    part_refs, (hires_ref,) = refs[:heads], refs[heads:]
    per_chunk = BLOCKS // heads
    d_pooled = 0.0
    for j, ref in enumerate(part_refs):
        first = per_chunk * (head ^ j)
        chunk = cat([whole_ref[first + i] for i in range(per_chunk)], 1)
        d_pooled = d_pooled + dot(ref[...], chunk, (1, 1))
    d_pooled = d_pooled.astype(low)
    batches = pool_ref.shape[0]
    rows = pool_ref.shape[1]
    for batch in range(batches):
        own = d_pooled[batch * rows : (batch + 1) * rows]
        hires_ref[batch] = dot(pool_ref[batch], own, (0, 0))


def conv_grad_body(pooled_ref, *refs):
    heads = lax.axis_size("heads")
    head = lax.axis_index("heads")
    part_refs, (keep_ref, send_ref, hold) = refs[:heads], refs[heads + 2 :]
    per_chunk = BLOCKS // heads
    for j, ref in enumerate(part_refs):
        grad = dot(pooled_ref[...], ref[...], (0, 0)).astype(low)
        for i in range(per_chunk):
            hold[per_chunk * (head ^ j) + i] = grad[:, i * LANES : (i + 1) * LANES]
    for place in range(BLOCKS):
        target = place_refs(keep_ref, send_ref, place)
        target[0 : hold.shape[1]] = hold[block_at(place)]


def place_refs(keep_ref, send_ref, place):
    return ((keep_ref, send_ref)[place // 4]).at[place % 4]


def row_grad(left_ref, right, keep_ref, send_ref, start):
    count = right.shape[1] // LANES
    for place in range(BLOCKS):
        lanes = slice(place * LANES, (place + 1) * LANES)
        grad = dot(left_ref[:, lanes], right, (0, 0)).astype(low)
        target = place_refs(keep_ref, send_ref, place)
        for m in range(count):
            target[start + m * LANES : start + (m + 1) * LANES] = grad[
                :, m * LANES : (m + 1) * LANES
            ]


def col_grad(left_ref, right_ref, keep_ref, send_ref, start):
    width = left_ref.shape[1]
    for m in range(width // LANES):
        grad = dot(left_ref[:, m * LANES : (m + 1) * LANES], right_ref[...], (0, 0)).astype(low)
        for place in range(BLOCKS):
            target = place_refs(keep_ref, send_ref, place)
            target[start + m * LANES : start + (m + 1) * LANES] = grad[
                :, place * LANES : (place + 1) * LANES
            ]


def pair_grad_body(row_left, row_right, col_left, col_right, keep_ref, send_ref):
    width = row_right.shape[1]
    start = keep_ref.shape[1] - width - col_left.shape[1]
    row_grad(row_left, row_right[...], keep_ref, send_ref, start)
    col_grad(col_left, col_right, keep_ref, send_ref, start + width)


def final_rows(refs, start, count):
    return cat(
        [total_of(refs, slice(start + m * LANES, start + (m + 1) * LANES)) for m in range(count)],
        1,
    )


def last_final_body(*refs):
    first_refs, rest_ref, results = refs[:4], refs[4], refs[5:]
    conv_ref, gate_ref, join_ref, attn_ref, out_ref = results
    rows, chans = conv_ref.shape[0], gate_ref.shape[1]
    conv_ref[...] = total_of(first_refs, slice(0, rows))
    gate_ref[...] = final_rows(first_refs, rows, chans // LANES)
    join_ref[...] = total_of(first_refs, slice(rows + chans, rows + 2 * chans))
    at = first_refs[0].shape[0]
    behind = pl.ds(at, rest_ref.shape[0])
    part_refs = [rest_ref, *[ref.at[behind] for ref in first_refs[1:]]]
    for s in range(3):
        attn_ref[s] = final_rows(part_refs, s * chans, chans // LANES)
    out_ref[...] = total_of(part_refs, slice(3 * chans, 3 * chans + out_ref.shape[0]))


def up_down_final_body(*refs):
    part_refs, (up_ref, down_ref) = refs[:-2], refs[-2:]
    width = up_ref.shape[1]
    up_ref[...] = final_rows(part_refs, 0, width // LANES)
    down_ref[...] = total_of(part_refs, slice(width, width + down_ref.shape[0]))


def final_body(*refs):
    heads = lax.axis_size("heads")
    count = 3 + heads + BLOCKS
    token_refs, grad_refs, outs = refs[:count], refs[count : count + 5], refs[count + 5 :]
    tokens_ref, block_ref, *result_refs, hold = outs
    last_final_body(*grad_refs, *result_refs)
    tokens_grad_body(*token_refs, tokens_ref)
    block_out_body(*refs[1 : 1 + heads], block_ref, hold)


def unpack_rows(packed, count):
    places = packed.shape[0]
    return (
        packed.reshape(places, count, LANES, LANES)
        .transpose(0, 2, 1, 3)
        .reshape(places * LANES, count * LANES)
    )


def unpack_cols(packed):
    return packed.transpose(1, 0, 2).reshape(packed.shape[1], -1)


def pack_rows(weights):
    count = weights.shape[1] // LANES
    return (
        weights.reshape(BLOCKS, LANES, count, LANES)
        .transpose(0, 2, 1, 3)
        .reshape(BLOCKS, count * LANES, LANES)
    )


def pack_cols(weights):
    return weights.reshape(weights.shape[0], BLOCKS, LANES).transpose(1, 0, 2)


def scatter_dim(grad, axis):
    return lax.psum_scatter(grad, "tiles", scatter_dimension=axis, tiled=True).astype(wide)


def local(
    vit_tokens,
    hires_maps,
    map_sizes,
    out_grad,
    ln_gain,
    ln_bias,
    dw_params,
    conv_w,
    gate_w,
    join_w,
    attn_in_w,
    out_w,
    up_w,
    down_w,
):
    tiles = lax.axis_size("tiles")
    heads = lax.axis_size("heads")
    fast = fast_tiles()
    batches, rows, width = vit_tokens.shape
    total = batches * rows
    shard = total // heads
    chans = dw_params.shape[1]
    hidden_width = down_w.shape[0]
    pixels, hires_chans = hires_maps.shape[1:]
    dma = pltpu.SemaphoreType.DMA
    plan = Plan(STARTS, FINISHES, TURNS)

    cross = heads * chans
    lanes_of = chans // LANES
    if fast:
        first_own, cross_own = run_kernel(
            pack_first_body,
            [shape((hires_chans + chans, LANES)), shape((3 * chans, LANES))],
            conv_w,
            gate_w,
            join_w,
            out_w,
            scratch=[((), dma((3 + 2 * lanes_of,)))],
            fetch=True,
        )
        found = [first_own, over_x(first_own), over_y(first_own), over_corner(first_own)]
        for name, piece in zip((At.first_x, At.first_y, At.first_corner), found[1:]):
            plan.mark(name, piece)
    else:

        def whole_of(weights, axis):
            return lax.all_gather(weights, "tiles", axis=axis, tiled=True)

        def halves(*packed):
            joint = jnp.concatenate(packed, axis=1)
            return joint[: BLOCKS // 2], joint[BLOCKS // 2 :]

        gate_all = [pack_rows(each) for each in gather_heads(whole_of(gate_w, 0))]
        join_all = [pack_cols(each) for each in gather_heads(whole_of(join_w, 1))]
        out_all = [pack_cols(each) for each in gather_heads(whole_of(out_w, 1))]
        attn_whole = whole_of(attn_in_w, 1)
        first_stack = jnp.concatenate([pack_cols(whole_of(conv_w, 1)), gate_all[0]], axis=1)
        first_pieces = [first_stack[p] for p in range(BLOCKS)]
        second = halves(*join_all, *[pack_rows(each) for each in attn_whole])
        third = halves(
            *out_all,
            pack_rows(whole_of(up_w, 0)),
            pack_cols(whole_of(down_w, 1)),
        )
        fourth = halves(*gate_all[1:])

    inputs = (
        vit_tokens.reshape(total, width),
        out_grad.reshape(total, width),
        ln_gain,
        ln_bias,
    )
    tokens, upstream, gains, biases = run_kernel(
        relative_body,
        [shape(each.shape, each.dtype) for each in inputs],
        *inputs,
        scratch=[(each.shape, each.dtype) for each in inputs] + [((), dma((4,)))],
        fetch=True,
    )
    upstream_wide = upstream.astype(wide)
    plan.mark(At.relative, tokens)

    pooled, pools = pl.pallas_call(
        pool_body,
        out_shape=(shape((total, hires_chans)), shape((batches, rows, pixels))),
        in_specs=[
            pl.BlockSpec(memory_space=pltpu.SMEM),
            pl.BlockSpec(memory_space=pl.ANY),
        ],
        out_specs=tuple([pl.BlockSpec(memory_space=pltpu.VMEM)] * 2),
        scratch_shapes=[pltpu.VMEM(hires_maps.shape, low), dma((1,))],
        compiler_params=pltpu.CompilerParams(vmem_limit_bytes=VMEM_LIMIT),
    )(map_sizes, pltpu.with_memory_space_constraint(hires_maps, pltpu.HBM))
    plan.mark(At.pool, pooled)
    if fast:
        first_pieces = list(found)
        events = (At.first_own_core, At.first_x_core, At.first_y_core, At.first_corner_core)
        for name, piece in zip(events, found):
            first_pieces.append(plan.mark(name, over_core(plan.start(name, piece))))
        cross_parts = plan.gather(At.cross, cross_own)

    conv_whole, *conv_parts = run_kernel(
        conv_body,
        [shape((BLOCKS, hires_chans, LANES))] + [shape((total, chans))] * heads,
        plan.enter(At.conv, after(pooled, tokens)),
        *first_pieces,
        flops=2 * total * hires_chans * width,
    )
    edge_shapes = [
        shape((batches * TILE, chans)),
        shape((batches * PAD, chans)),
        shape((PAD, chans)),
    ]
    edge_scratch = ((batches * PAD, chans), wide)
    grid_scratch = ((total, chans), wide)
    pad_dims = (batches * (TILE + 2) * PAD, chans)
    plan.mark(At.conv, conv_whole)
    own_part, *other_parts = plan.over_heads(At.conv_z, conv_parts)
    mapped, *edges = run_kernel(
        map_body,
        [shape((total, chans))] + edge_shapes,
        plan.enter(At.map, own_part),
        *other_parts,
        scratch=[grid_scratch, edge_scratch],
    )

    def swap_edges(name, col, row, corner):
        return (
            plan.mark(name + 1, over_core(col)),
            plan.mark(name + 2, over_x(row)),
            plan.mark(name + 3, swap_with(corner, "tiles", 3)),
        )

    plan.mark(At.map, mapped)
    edges = swap_edges(At.edge, *edges)

    (gate,) = run_kernel(
        gate_body,
        [shape((total, chans), wide)],
        tokens,
        *first_pieces,
        flops=2 * total * chans * width,
    )
    chunk_shapes = [shape((shard, width))] * heads
    padded, spread, joined = run_kernel(
        depthwise_body,
        [shape(pad_dims, wide), shape((total, chans), wide), shape((total, chans))],
        plan.enter(At.depthwise, mapped),
        *edges,
        dw_params,
        gate,
        scratch=[grid_scratch, edge_scratch],
    )

    plan.mark(At.depthwise, joined)
    joined_parts = plan.gather(At.joined, joined)
    if fast:
        second_own, third_own, fourth_own = run_kernel(
            pack_rest_body,
            [
                shape((cross + 3 * chans, LANES)),
                shape((cross + 2 * hidden_width, LANES)),
                shape((cross - chans, LANES)),
            ],
            attn_in_w,
            up_w,
            down_w,
            plan.start(At.pack_rest, cross_parts[0]),
            *cross_parts[1:],
            scratch=[((), dma((3 * heads + 3 * lanes_of + hidden_width // LANES,)))],
            fetch=3,
        )
        second_x = plan.finish(At.second_x, over_x(plan.start(At.second_x, second_own)))
        second_y = plan.finish(At.second_y, over_y(plan.start(At.second_y, second_own)))
        corner = over_y(plan.start(At.second_corner, second_x))
        plan.finish(At.second_corner, corner)
        second_stack = stacked(
            plan.start(At.second_stack, second_own), second_x, second_y, corner
        )
        second_core = over_core(plan.start(At.second_core, second_stack))
        second = (second_stack, plan.finish(At.second_core, second_core))
    wide_rows_shape = shape((total, width), wide)
    first, normed1, query, kv_own = run_kernel(
        join_body,
        [
            wide_rows_shape,
            shape((total, width)),
            shape((total, chans)),
            shape((total, 2 * chans)),
        ],
        tokens,
        gains,
        biases,
        plan.enter(At.join, joined_parts[0]),
        *joined_parts[1:],
        *second,
        flops=2 * total * width * (width + 3 * chans),
    )
    plan.mark(At.join, kv_own)
    kv_x = plan.mark(At.kv_x, over_x(kv_own))
    kv_all = [
        kv_own,
        kv_x,
        plan.mark(At.kv_core, over_core(kv_own)),
        plan.mark(At.kv_x_core, over_core(kv_x)),
    ]
    (mixed,) = run_kernel(
        attend_body,
        [shape((total, chans))],
        plan.enter(At.attend, query),
        *kv_all,
        flops=8 * total * 4 * rows * chans,
    )
    plan.mark(At.attend, mixed)
    if fast:
        third_x = plan.finish(At.third_x, over_x(plan.start(At.third_x, third_own)))
        third_y = plan.finish(At.third_y, over_y(plan.start(At.third_y, third_own)))
        third_stack = stacked(third_own, third_x, third_y)
        upper = over_y(plan.start(At.upper, third_x[:cross]))
        lower = over_x(plan.start(At.lower, third_y[cross:]))
        plan.finish(At.upper, upper)
        plan.finish(At.lower, lower)
        third_core = over_core(plan.start(At.third_core, third_stack))
        plan.finish(At.third_core, third_core)
    mixed_parts = plan.gather(At.mixed, mixed)
    if fast:
        third = (
            third_stack,
            upper,
            lower,
            third_core,
            over_core(plan.start(At.upper_core, upper)),
            over_core(plan.start(At.lower_core, lower)),
        )

    wide_shape = shape((total, hidden_width))
    total_scratch = ((total, width), wide)
    second_rows, normed2, hidden, d_hidden, *ffn_parts = run_kernel(
        ffn_body,
        [wide_rows_shape, shape((total, width)), wide_shape, wide_shape] + chunk_shapes,
        upstream,
        first,
        gains,
        biases,
        plan.enter(At.ffn, mixed_parts[0]),
        *mixed_parts[1:],
        *third,
        scratch=[total_scratch],
        flops=2 * total * width * (width + 3 * hidden_width),
    )
    plan.mark(At.ffn, normed2)
    ffn_parts = plan.over_heads(At.ffn_z, ffn_parts)
    if fast:
        fourth_x = plan.finish(At.fourth_x, over_x(plan.start(At.fourth_x, fourth_own)))
        fourth_y = plan.finish(At.fourth_y, over_y(plan.start(At.fourth_y, fourth_own)))
    back_shapes = [shape((shard, width), wide), shape((shard + 8, width))]
    d_second, d_attn_own = run_kernel(
        norm_back_body,
        back_shapes,
        plan.enter(At.norm2, second_rows),
        upstream_wide,
        gains[1:2],
        *ffn_parts,
    )
    plan.mark(At.norm2, d_attn_own)
    d_attn_parts = plan.gather(At.d_attn, d_attn_own)
    if fast:
        fourth_corner = over_y(plan.start(At.fourth_corner, fourth_x))
        plan.finish(At.fourth_corner, fourth_corner)
    ud_keep, ud_send = run_kernel(
        pair_grad_body,
        [shape((4, 2 * hidden_width, LANES))] * 2,
        plan.start(At.ud_kernel, normed2),
        d_hidden,
        hidden,
        upstream,
        flops=4 * total * hidden_width * width,
    )
    plan.finish(At.ud_kernel, ud_keep)

    down_parts = run_kernel(
        down_body,
        chunk_shapes,
        plan.start(At.down_kernel, hidden),
        *third,
        scratch=[total_scratch],
        flops=2 * total * hidden_width * width,
    )
    plan.finish(At.down_kernel, down_parts[0])

    d_attn, d_query, kv_keep, kv_send, ln2_sums = run_kernel(
        attend_back_body,
        [
            shape((total, width)),
            shape((total, chans)),
            shape((2, total, 2 * chans), wide),
            shape((2, total, 2 * chans)),
            shape((2, width), wide),
        ],
        plan.enter(At.attend_back, query),
        *kv_all,
        *d_attn_parts,
        *third,
        scratch=[((total, chans), low), total_scratch],
        flops=2 * total * chans * width + 20 * total * 4 * rows * chans,
    )
    plan.mark(At.attend_back, kv_keep)
    kv_got = plan.mark(At.kv_got, over_core(kv_send))
    kv_mine, kv_over = run_kernel(
        add_pair_body,
        [shape((total, 2 * chans), wide), shape((total, 2 * chans))],
        plan.enter(At.add_pair, kv_keep),
        kv_got,
    )
    plan.mark(At.add_pair, kv_over)
    kv_back = plan.mark(At.kv_back, over_x(kv_over))
    down_parts = plan.over_heads(At.down, down_parts)
    (result_own,) = run_kernel(whole_cols_body, [shape((shard, width))], second_rows, *down_parts)
    if fast:
        fourth_stack = stacked(
            plan.start(At.fourth_stack, fourth_own), fourth_x, fourth_y, fourth_corner
        )
        fourth_core = over_core(plan.start(At.fourth_core, fourth_stack))
        fourth = (fourth_stack, plan.finish(At.fourth_core, fourth_core))
    d_qkv, *qkv_parts = run_kernel(
        d_qkv_body,
        [shape((total, 3 * chans))] + chunk_shapes,
        plan.enter(At.d_qkv, d_query),
        kv_mine,
        kv_back,
        *second,
        scratch=[total_scratch],
        flops=6 * total * chans * width,
    )
    plan.mark(At.d_qkv, d_qkv)
    qkv_parts = plan.over_heads(At.qkv_z, qkv_parts)
    if fast:
        ud_got = plan.finish(At.ud_core, over_core(plan.start(At.ud_core, ud_send)))
        ud_parts = add_cores(ud_keep, ud_got)
        ud_x = plan.finish(At.ud_x, over_x(plan.start(At.ud_x, ud_parts[1])))
        ud_y = plan.finish(At.ud_y, over_y(plan.start(At.ud_y, ud_parts[2])))
    else:
        ud_sums = jnp.concatenate([ud_keep, ud_send], axis=0)
    d_first, d_join_own = run_kernel(
        norm_back_body, back_shapes, first, plan.enter(At.norm3, d_second), gains[0:1], *qkv_parts
    )
    plan.mark(At.norm3, d_join_own)
    d_join_parts = plan.gather(At.d_join, d_join_own)
    ap_keep, ap_send = run_kernel(
        pair_grad_body,
        [shape((4, 4 * chans, LANES))] * 2,
        plan.start(At.ap_kernel, normed1),
        d_qkv,
        mixed,
        d_attn,
        flops=8 * total * chans * width,
    )
    plan.finish(At.ap_kernel, ap_keep)

    d_join, d_gate_in, tail, d_grid, ln1_sums, *edges = run_kernel(
        gate_back_body,
        [
            shape((total, width)),
            shape((total, chans)),
            shape((total + shard * (width // chans), chans)),
            shape((total, chans), wide),
            shape((2, width), wide),
        ]
        + edge_shapes,
        gate,
        spread,
        result_own,
        plan.enter(At.gate_back, d_join_parts[0]),
        *d_join_parts[1:],
        *second,
        scratch=[edge_scratch, total_scratch],
        flops=2 * total * chans * width,
    )
    plan.mark(At.gate_back, d_grid)
    edges = swap_edges(At.back, *edges)
    (d_mapped,) = run_kernel(
        depthwise_back_body,
        [shape((total, chans))],
        plan.enter(At.dw_back, d_grid),
        *edges,
        dw_params,
        scratch=[(pad_dims, wide), edge_scratch, grid_scratch],
    )
    plan.mark(At.dw_back, d_mapped)
    d_mapped_parts = plan.gather(At.d_mapped, d_mapped)
    if fast:
        ud_corner = over_corner(plan.start(At.ud_corner, ud_parts[3]))
        ud_sums = [ud_parts[0], ud_x, ud_y, plan.finish(At.ud_corner, ud_corner)]
        ap_got = plan.finish(At.ap_core, over_core(plan.start(At.ap_core, ap_send)))
        ap_parts = add_cores(ap_keep, ap_got)
    else:
        ap_sums = jnp.concatenate([ap_keep, ap_send], axis=0)
    (small,) = run_kernel(
        taps_body,
        [shape((8, width), wide)],
        plan.start(At.taps, d_grid),
        padded,
        ln1_sums,
        ln2_sums,
    )
    bit = 1
    while bit < tiles // 2:
        name = {1: At.small1, 2: At.small2}.get(bit)
        got = swap_with(plan.start(name, small), "tiles", bit)
        small = small + plan.finish(name, got)
        bit *= 2
    small_got = swap_with(plan.start(At.small_last, small), "tiles", bit)
    plan.finish(At.small_last, small_got)
    if fast:
        up_grad, down_grad = run_kernel(
            up_down_final_body,
            [shape(up_w.shape, wide), shape(down_w.shape, wide)],
            *ud_sums,
            leave=True,
        )
        plan.finish(At.up_down, up_grad)
    first_shape = shape((4, hires_chans + 2 * chans, LANES))
    first_keep, first_send = run_kernel(
        pair_grad_body,
        [first_shape] * 2,
        plan.start(At.first_kernel, tokens),
        d_gate_in,
        joined,
        d_join,
        flops=4 * total * chans * width,
    )
    first_keep, first_send = run_kernel(
        conv_grad_body,
        [first_shape] * 2,
        plan.enter(At.conv_grad, pooled),
        *d_mapped_parts,
        first_keep,
        first_send,
        scratch=[((BLOCKS, hires_chans, LANES), low)],
        flops=2 * total * hires_chans * width,
        alias={heads + 1: 0, heads + 2: 1},
    )
    plan.mark(At.conv_grad, first_send)
    tail_parts = plan.gather(At.tail, tail)
    (hires_grad,) = run_kernel(
        conv_back_body,
        [shape((batches, pixels, hires_chans), wide)],
        plan.start(At.hires, pools),
        conv_whole,
        *d_mapped_parts,
        flops=2 * total * hires_chans * width + 2 * total * pixels * hires_chans,
        leave=True,
    )
    plan.finish(At.hires, hires_grad)
    if fast:
        first_got = plan.mark(At.first_got, over_core(first_send))
        first_rows = first_keep.shape[1]
        first_parts = run_kernel(
            add_first_body,
            [shape((first_rows, LANES))] + [shape((first_rows + 4 * chans, LANES))] * 3,
            plan.enter(At.add_first, first_keep),
            first_got,
            *ap_parts[1:],
        )
        plan.mark(At.add_first, first_parts[0])
        first_sums = [
            first_parts[0],
            over_x(plan.start(At.last_x, plan.enter(At.last_x, first_parts[1]))),
            over_y(plan.start(At.last_y, plan.enter(At.last_y, first_parts[2]))),
            over_corner(plan.start(At.last_corner, plan.enter(At.last_corner, first_parts[3]))),
        ]
    else:
        first_sums = jnp.concatenate([first_keep, first_send], axis=0)
    ln1_grad, ln2_grad, taps_grad = run_kernel(
        small_final_body,
        [shape((2, width), wide), shape((2, width), wide), shape(dw_params.shape, wide)],
        small,
        small_got,
        leave=True,
    )

    if fast:
        results = (conv_w, gate_w, join_w, attn_in_w, out_w)
        tokens_grad, block_out, *grads = run_kernel(
            final_body,
            [shape((total, width), wide), shape((total, width))]
            + [shape(each.shape, wide) for each in results],
            plan.enter(At.tokens, d_join),
            *tail_parts,
            *first_pieces,
            *fourth,
            plan.enter(At.last, first_sums[0]),
            *first_sums[1:],
            ap_parts[0],
            scratch=[total_scratch],
            leave=True,
        )
        conv_grad, gate_grad, join_grad, attn_grad, out_w_grad = grads
    else:
        (tokens_grad,) = run_kernel(
            tokens_grad_body,
            [shape((total, width), wide)],
            plan.enter(At.tokens, d_join),
            *tail_parts,
            *first_pieces,
            *fourth,
            flops=2 * total * width * width,
            leave=True,
        )
        (block_out,) = run_kernel(
            block_out_body,
            [shape((total, width))],
            *tail_parts,
            scratch=[total_scratch],
            leave=True,
        )

        plan.finish(At.tokens, tokens_grad)
        plan.finish(At.block, block_out)
        count = chans // LANES
        at = hires_chans
        conv_grad = scatter_dim(unpack_cols(first_sums[:, :at]), 1)
        gate_grad = scatter_dim(unpack_rows(first_sums[:, at : at + chans], count), 0)
        join_grad = scatter_dim(unpack_cols(first_sums[:, at + chans :]), 1)
        attn_grad = jnp.stack(
            [
                scatter_dim(unpack_rows(ap_sums[:, s * chans : (s + 1) * chans], count), 0)
                for s in range(3)
            ]
        )
        out_w_grad = scatter_dim(unpack_cols(ap_sums[:, 3 * chans :]), 1)
        up_grad = scatter_dim(unpack_rows(ud_sums[:, :hidden_width], hidden_width // LANES), 0)
        down_grad = scatter_dim(unpack_cols(ud_sums[:, hidden_width:]), 1)

    return (
        block_out.reshape(batches, rows, width),
        tokens_grad.reshape(batches, rows, width),
        hires_grad,
        ln1_grad,
        ln2_grad,
        taps_grad,
        conv_grad,
        gate_grad,
        join_grad,
        attn_grad,
        out_w_grad,
        up_grad,
        down_grad,
    )


def solution(mesh):
    placed = (
        P(None, "tiles", None),
        P(None, "tiles", "heads"),
        P(),
        P(None, "tiles", None),
        P(),
        P(),
        P(None, "heads"),
        P("heads", "tiles"),
        P("tiles", "heads"),
        P("heads", "tiles"),
        P(None, "tiles", "heads"),
        P("heads", "tiles"),
        P("tiles", "heads"),
        P("heads", "tiles"),
    )
    return jax.shard_map(
        local,
        mesh=mesh,
        in_specs=placed,
        out_specs=(
            P(None, "tiles", None),
            P(None, "tiles", None),
            P(None, "tiles", "heads"),
            P(),
            P(),
            P(None, "heads"),
            P("heads", "tiles"),
            P("tiles", "heads"),
            P("heads", "tiles"),
            P(None, "tiles", "heads"),
            P("heads", "tiles"),
            P("tiles", "heads"),
            P("heads", "tiles"),
        ),
        check_vma=False,
    )
```
